32 devices in a mesh: obs: 8 (over z, y), coef: 4 (over x, core).
Axes of the slice: x: 2, y: 2, z: 4, core: 2. Of those that a mesh axis runs over, the one named last changes fastest.
Arguments:
- design: bfloat16 [8192, 36864], P('obs', 'coef'), may hold values from -0.03125 to 0.03125
- observations: bfloat16 [8, 8192], P(None, 'obs'), may hold values from -6 to 6
- shift_table: float32 [16], replicated, may hold values from 0.1 to 3
- shift_index: int32 [8], replicated, may hold values from 0 to 15
- coef_perm: int32 [36864], P('coef'), may hold values from 0 to 36863, as said below
- order_map: int32 [8], replicated, may hold values from 0 to 7, each once
Outputs:
- band_fourier: float32 [192, 2, 8, 32], P('coef', None, None, 'obs')
- field: float32 [8, 32, 1024], P(None, ('obs', 'coef'))
The draws below stay inside these ranges and needn't reach their ends.
Inputs may be any that keep to these rules, and one draw needn't show every extreme that they name: coef_perm is a permutation; the design columns of each block of 9216 consecutive columns hold exactly 1152 values of each range of 4608 consecutive values. `order_map`: each block number appears once.
All inputs are finite; a program needn't handle non-finite values.
Results may differ from the reference program's by a relative error of at most 0.007.
Values may be sent and summed in bfloat16 or wider, within the bound.
A program may use at most 64 MiB of HBM per device.

```python
import math
import jax
import jax.numpy as jnp
from jax import lax

NL = 192
COLS = 8
ITERS = 2
NSHIFT = 16
NLON = 1024
K = 36864
M = 8192
KDEV = 9216
NBLK = 8
OB = 24
KB = 1152
NLAT = 32
N_COEF = 4


def shuffle_block(block_key):
    return jax.random.permutation(block_key, OB * NL).astype(jnp.int32)


def shuffle_columns(column_key):
    return jax.random.permutation(column_key, KDEV).astype(jnp.int32)


def draw_coef_perm(key, part):
    block_size = OB * NL
    block_keys = jax.random.split(jax.random.fold_in(key, 11), NBLK)
    inside = jax.vmap(shuffle_block)(block_keys)
    values = inside + (jnp.arange(NBLK, dtype=jnp.int32) * block_size)[:, None]
    values = values.reshape(NBLK, N_COEF, KB).transpose(1, 0, 2).reshape(N_COEF, KDEV)
    column_keys = jax.random.split(jax.random.fold_in(key, 23), N_COEF)
    orders = jax.vmap(shuffle_columns)(column_keys)
    shuffled = jnp.take_along_axis(values, orders, axis=1)
    return shuffled.reshape(K).astype(jnp.int32)


def touch_ends(values, own_key, least, largest):
    longest = values.shape.index(max(values.shape))
    spots = []
    for shift in (0, 1):
        where = [jax.random.randint(jax.random.fold_in(own_key, axis), (), 0, length) for axis, length in enumerate(values.shape)]
        where[longest] = (where[longest] + shift) % values.shape[longest]
        spots.append(tuple(where))
    return values.at[spots[0]].set(least).at[spots[1]].set(largest)


def steps_of(key, shape, cuts, smallest, high):
    def one(axis_at, blocks):
        heights = jax.random.uniform(jax.random.fold_in(jax.random.fold_in(key, 6), axis_at), (blocks,), jnp.float32, smallest / len(cuts), high / len(cuts))
        return jnp.repeat(jnp.exp(heights), shape[axis_at] // blocks).reshape((-1,) + (1,) * (len(shape) - axis_at - 1))

    gain = one(*cuts[0])
    for cut in cuts[1:]:
        gain = gain * one(*cut)
    return gain


def normal_values(key, shape, spread, bound, cuts=(), kind=jnp.bfloat16):
    entries = spread * jax.random.normal(key, shape, jnp.float32)
    if cuts:
        entries = entries * steps_of(key, shape, cuts, -0.22, 0.18)
    return jnp.clip(entries, -bound, bound).astype(kind)


def setup_inputs(seed: int = 0) -> dict:
    key_list = jax.random.split(jax.random.key(seed), 7)
    design = normal_values(key_list[0], (M, K), K ** -0.5, 0.03125, ((0, 8), (1, 4)))
    observations = normal_values(key_list[1], (COLS, M), 1.0, 6.0, ((1, 8),))
    shift_table = jnp.clip(jnp.exp(jax.random.uniform(key_list[2], (NSHIFT,), jnp.float32, math.log(0.1), math.log(3.0))), 0.1, 3.0)
    shift_index = touch_ends(jax.random.randint(key_list[3], (COLS,), 0, NSHIFT), jax.random.fold_in(key_list[3], 1), 0, NSHIFT - 1).astype(jnp.int32)
    coef_perm = draw_coef_perm(jax.random.fold_in(key_list[6], 71), 0)
    order_map = jax.random.permutation(key_list[5], NBLK).astype(jnp.int32)
    return {"design": design, "observations": observations, "shift_table": shift_table, "shift_index": shift_index, "coef_perm": coef_perm, "order_map": order_map}


CENTRE_OFFSET = 1.25
HALF_WIDTH = 0.95

def legendre_table(orders, colatitude, degrees):
    cosine = jnp.cos(colatitude)
    sine = jnp.sin(colatitude)
    order_value = orders.astype(sine.dtype)[:, None]

    def advance(carry, degree):
        diagonal, previous, earlier = carry
        level = degree.astype(sine.dtype)
        safe_level = jnp.maximum(level, 1.0)
        grown = diagonal * sine * jnp.sqrt((2.0 * safe_level + 1.0) / (2.0 * safe_level))
        diagonal_next = jnp.where(degree == 0, jnp.ones_like(sine), jnp.where(degree == 1, jnp.sqrt(3.0) * sine, grown))
        above = level > order_value
        product = (level - order_value) * (level + order_value)
        denom = jnp.where(above, product, 1.0)
        first = jnp.sqrt(jnp.maximum((2.0 * level - 1.0) * (2.0 * level + 1.0), 0.0) / denom)
        second = jnp.sqrt(jnp.maximum((2.0 * level + 1.0) * (level + order_value - 1.0) * (level - order_value - 1.0), 0.0) / (denom * jnp.maximum(2.0 * level - 3.0, 1.0)))
        recur = first * cosine[None, :] * previous - second * earlier
        value = jnp.where(above, recur, jnp.where(level == order_value, diagonal_next[None, :], 0.0))
        return ((diagonal_next, value, previous), value)
    start = jnp.zeros((orders.shape[0], colatitude.shape[0]), sine.dtype)
    final_state, table = lax.scan(advance, (jnp.zeros_like(sine), start, start), jnp.arange(degrees, dtype=jnp.int32))
    return table

def wave_tables(rows, longitudes):
    steps_k = jnp.arange(longitudes, dtype=jnp.int32)
    scale = 2.0 * math.pi / longitudes
    cos_angle = (rows[:, None] * steps_k[None, :] % longitudes).astype(jnp.float32) * scale
    sin_angle = ((NL - rows)[:, None] * steps_k[None, :] % longitudes).astype(jnp.float32) * scale
    return (jnp.cos(cos_angle), jnp.sin(sin_angle))

def reference(design, observations, shift_table, shift_index, coef_perm, order_map):
    table_index = jnp.arange(NSHIFT, dtype=jnp.int32)
    shifts = lax.optimization_barrier(jnp.sum(jnp.where(shift_index[:, None] == table_index[None, :], shift_table[None, :], 0.0), axis=1))
    centre = shifts + CENTRE_OFFSET
    ratio_start = centre / HALF_WIDTH
    residual = jnp.dot(observations, design, preferred_element_type=jnp.float32)
    solution = jnp.zeros_like(residual)
    factor = 1.0 / ratio_start
    direction = residual / centre[:, None]
    for iteration in range(ITERS):
        solution = solution + direction
        image = lax.dot_general(direction.astype(jnp.bfloat16), design, (((1,), (1,)), ((), ())), preferred_element_type=jnp.float32)
        normal = jnp.dot(image.astype(jnp.bfloat16), design, preferred_element_type=jnp.float32)
        residual = residual - (normal + shifts[:, None] * direction)
        factor_next = 1.0 / (2.0 * ratio_start - factor)
        direction = (factor_next * factor)[:, None] * direction + (2.0 * factor_next / HALF_WIDTH)[:, None] * residual
        factor = factor_next
    solution = solution + direction
    paired = jnp.zeros((COLS, K), jnp.float32).at[:, coef_perm].set(solution).reshape(COLS, NL, NL)
    rows_all = jnp.arange(NL, dtype=jnp.int32)
    colatitude = math.pi * (jnp.arange(NLAT, dtype=jnp.int32).astype(jnp.float32) + 0.5) / NLAT
    cos_leg = legendre_table(rows_all, colatitude, NL)
    sin_leg = legendre_table(NL - rows_all, colatitude, NL)
    roll_index = (rows_all[None, :] - rows_all[:, None]) % NL
    shifted = jnp.take_along_axis(paired, roll_index[None, :, :], axis=2)
    cos_part = jnp.einsum('dqt,cqd->qct', cos_leg, shifted, precision=lax.Precision.HIGHEST)
    sin_part = jnp.einsum('dqt,cqd->qct', sin_leg, paired, precision=lax.Precision.HIGHEST)
    fourier = jnp.stack([cos_part, sin_part], axis=1) / math.sqrt(NL)
    owner_rows = (order_map[:, None] * OB + jnp.arange(OB, dtype=jnp.int32)[None, :]).reshape(NL)
    band_fourier = fourier[owner_rows]
    wave_cos, wave_sin = wave_tables(rows_all, NLON)
    dims = (((0,), (0,)), ((), ()))
    field = (lax.dot_general(fourier[:, 0].reshape(NL, COLS * NLAT), wave_cos, dims, precision=lax.Precision.HIGHEST) + lax.dot_general(fourier[:, 1].reshape(NL, COLS * NLAT), wave_sin, dims, precision=lax.Precision.HIGHEST)) / math.sqrt(NL)
    return (band_fourier, field.reshape(COLS, NLAT, NLON))
```

```python
import functools
import math

import jax
import jax.numpy as jnp
from jax import lax
from jax.experimental import pallas as pl
from jax.experimental.pallas import tpu as pltpu
from jax.sharding import PartitionSpec as P

NL = 192
COLS = 8
ITERS = 2
NSHIFT = 16
BPO = 2
NLON = 1024
LAT_DEV = 1

CENTRE_OFFSET = 1.25
HALF_WIDTH = 0.95
VMEM_SPEC = pl.BlockSpec(memory_space=pltpu.VMEM)
MESH = pl.DeviceIdType.MESH


def greet(axis, n, me):
    barrier = pltpu.get_barrier_semaphore()
    for step in range(1, n):
        pl.semaphore_signal(
            barrier, inc=1, device_id={axis: lax.rem(me + step, n)}, device_id_type=MESH
        )
    pl.semaphore_wait(barrier, n - 1)


def push(axis, n, me, step, src, dst, send_sem, recv_sem):
    return pltpu.make_async_remote_copy(
        src_ref=src,
        dst_ref=dst,
        send_sem=send_sem.at[step],
        recv_sem=recv_sem.at[step],
        device_id={axis: lax.rem(me + step, n)},
        device_id_type=MESH,
    )


def flip(index, mask):
    other = index
    bit = 1
    while bit <= mask:
        if mask & bit:
            other = other + bit - 2 * bit * (index // bit % 2)
        bit *= 2
    return other


def swap(axis, rank, mask, src, dst, send_sem, recv_sem):
    return pltpu.make_async_remote_copy(
        src_ref=src,
        dst_ref=dst,
        send_sem=send_sem.at[mask],
        recv_sem=recv_sem.at[mask],
        device_id={axis: flip(rank, mask)},
        device_id_type=MESH,
    )


def solver_kernel(
    n, nc, obs_ref, design_ref, shift_ref, keep_ref, gain_ref, full_out,
    held, part, landed, gathered, image_sent, image_landed, left_ref, acc,
    load_sem, send_a, recv_a, send_b, recv_b, send_c, recv_c,
):
    me = lax.axis_index("obs")
    mine = lax.axis_index("coef")
    chunk = held.shape[2]
    far_first = list(range(n - 1, 0, -1))

    def load(mask):
        return pltpu.make_async_copy(
            design_ref.at[:, pl.ds(pl.multiple_of(flip(me, mask) * chunk, 128), chunk)],
            held.at[mask],
            load_sem.at[mask],
        )

    for mask in far_first + [0]:
        load(mask).start()
    barrier = pltpu.get_barrier_semaphore()
    for axis, count, rank in (("obs", n, me), ("coef", nc, mine)):
        for mask in range(1, count):
            pl.semaphore_signal(
                barrier, inc=1, device_id={axis: flip(rank, mask)}, device_id_type=MESH
            )
    pl.semaphore_wait(barrier, n + nc - 2)

    def scatter_copy(rnd, mask):
        return swap(
            "obs", me, mask, part.at[rnd, mask], landed.at[rnd, mask], send_a.at[rnd], recv_a.at[rnd]
        )

    def gather_copy(rnd, mask):
        return swap(
            "obs", me, mask, gathered.at[rnd, 0], gathered.at[rnd, mask],
            send_b.at[rnd], recv_b.at[rnd],
        )

    def image_copy(rnd, mask):
        return swap(
            "coef", mine, mask, image_sent.at[rnd], image_landed.at[rnd, mask],
            send_c.at[rnd], recv_c.at[rnd],
        )

    def transposed_pass(rnd):
        def product(mask):
            both = jnp.dot(left_ref[...], held[mask], preferred_element_type=jnp.float32)
            return both[:COLS] + both[COLS:]

        for mask in far_first:
            if rnd == 0:
                load(mask).wait()
            part[rnd, mask] = product(mask).astype(jnp.bfloat16)
            scatter_copy(rnd, mask).start()
        if rnd == 0:
            load(0).wait()
        total = product(0)
        for mask in far_first:
            scatter_copy(rnd, mask).wait_recv()
            total = total + landed[rnd, mask].astype(jnp.float32)
        gathered[rnd, 0] = total.astype(jnp.bfloat16)
        for mask in far_first:
            gather_copy(rnd, mask).start()

    def image_of(rnd):
        for mask in range(n):
            if mask:
                gather_copy(rnd, mask).wait_recv()
            term = lax.dot_general(
                gathered[rnd, mask],
                held[mask],
                (((1,), (1,)), ((), ())),
                preferred_element_type=jnp.float32,
            )
            acc[...] = term if mask == 0 else acc[...] + term
        image = acc[...]
        image_sent[rnd] = image.astype(jnp.bfloat16)
        for mask in range(nc - 1, 0, -1):
            image_copy(rnd, mask).start()
        for mask in range(1, nc):
            image_copy(rnd, mask).wait_recv()
            image = image + image_landed[rnd, mask].astype(jnp.float32)
        return image

    def split(value):
        high = value.astype(jnp.bfloat16).astype(jnp.float32)
        left_ref[...] = jnp.concatenate([high, value - high], axis=0).astype(jnp.bfloat16)

    residual = obs_ref[...].astype(jnp.float32)
    split(residual)
    transposed_pass(0)
    direction = residual / keep_ref[0]
    answer = direction
    for rnd in range(1, ITERS + 1):
        image = image_of(rnd - 1)
        if rnd == 1:
            image = image / keep_ref[0]
        residual = residual - (image + shift_ref[...] * direction)
        direction = keep_ref[rnd] * direction + gain_ref[rnd] * residual
        answer = answer + direction
        split(answer if rnd == ITERS else direction)
        transposed_pass(rnd)
    for mask in range(n):
        if mask:
            gather_copy(ITERS, mask).wait_recv()
        at = pl.ds(pl.multiple_of(flip(me, mask) * chunk, 128), chunk)
        full_out[:, at] = gathered[ITERS, mask]
    for rnd in range(ITERS + 1):
        for mask in far_first:
            scatter_copy(rnd, mask).wait_send()
            gather_copy(rnd, mask).wait_send()
        if rnd < ITERS:
            for mask in range(1, nc):
                image_copy(rnd, mask).wait_send()


def solve(n, nc, observations, design, shift, keep, gain):
    rows, kdev = design.shape
    chunk = kdev // n
    rounds = ITERS + 1
    blocks = pltpu.VMEM((rounds, n, COLS, chunk), jnp.bfloat16)
    return pl.pallas_call(
        functools.partial(solver_kernel, n, nc),
        out_shape=jax.ShapeDtypeStruct((COLS, kdev), jnp.bfloat16),
        in_specs=[VMEM_SPEC, pl.BlockSpec(memory_space=pl.ANY)] + [VMEM_SPEC] * 3,
        out_specs=VMEM_SPEC,
        scratch_shapes=[pltpu.VMEM((n, rows, chunk), jnp.bfloat16)]
        + [blocks] * 3
        + [
            pltpu.VMEM((ITERS, COLS, rows), jnp.bfloat16),
            pltpu.VMEM((ITERS, nc, COLS, rows), jnp.bfloat16),
            pltpu.VMEM((2 * COLS, rows), jnp.bfloat16),
            pltpu.VMEM((COLS, rows), jnp.float32),
            pltpu.SemaphoreType.DMA((n,)),
        ]
        + [pltpu.SemaphoreType.DMA((rounds, n))] * 4
        + [pltpu.SemaphoreType.DMA((ITERS, nc))] * 2,
        compiler_params=pltpu.CompilerParams(
            collective_id=0, has_side_effects=True, vmem_limit_bytes=48 << 20
        ),
        name="solve",
    )(observations, design, shift, keep, gain)


def sum_kernel(n, x_ref, o_ref, landed, send_sem, recv_sem):
    me = lax.axis_index("coef")
    greet("coef", n, me)
    copies = []
    for step in range(1, n):
        copy = push("coef", n, me, step, x_ref, landed.at[step], send_sem, recv_sem)
        copy.start()
        copies.append(copy)
    total = x_ref[...]
    for step in range(1, n):
        copies[step - 1].wait()
        total = total + landed[step]
    o_ref[...] = total.astype(o_ref.dtype)


def coef_sum(partial, n, cid):
    return pl.pallas_call(
        functools.partial(sum_kernel, n),
        out_shape=jax.ShapeDtypeStruct(partial.shape, jnp.bfloat16),
        in_specs=[VMEM_SPEC],
        out_specs=VMEM_SPEC,
        scratch_shapes=[pltpu.VMEM((n,) + partial.shape, jnp.float32)]
        + [pltpu.SemaphoreType.DMA((n,))] * 2,
        compiler_params=pltpu.CompilerParams(collective_id=cid, has_side_effects=True),
        name="coef_sum",
    )(partial)


def solve_plain(nc, observations, design, shift, keep, gain):
    def transposed_pass(left):
        return lax.psum(jnp.dot(left, design, preferred_element_type=jnp.float32), "obs")

    residual = transposed_pass(observations)
    direction = residual / keep[0]
    solution = direction
    for rnd in range(1, ITERS + 1):
        partial_image = lax.dot_general(
            direction.astype(jnp.bfloat16),
            design,
            (((1,), (1,)), ((), ())),
            preferred_element_type=jnp.float32,
        )
        total = transposed_pass(coef_sum(partial_image, nc, 2 + rnd))
        residual = residual - (total + shift * direction)
        direction = keep[rnd] * direction + gain[rnd] * residual
        solution = solution + direction
    return solution.astype(jnp.bfloat16)


def scatter_kernel(n, x_ref, o_ref, landed, send_sem, recv_sem):
    me = lax.axis_index("coef")
    greet("coef", n, me)
    copies = []
    for step in range(1, n):
        target = lax.rem(me + step, n)
        copy = push("coef", n, me, step, x_ref.at[target], landed.at[step], send_sem, recv_sem)
        copy.start()
        copies.append(copy)
    total = x_ref[me].astype(jnp.float32)
    for step in range(1, n):
        copies[step - 1].wait()
        total = total + landed[step].astype(jnp.float32)
    o_ref[...] = total


def coef_scatter(parts, n, cid):
    return pl.pallas_call(
        functools.partial(scatter_kernel, n),
        out_shape=jax.ShapeDtypeStruct(parts.shape[1:], jnp.float32),
        in_specs=[VMEM_SPEC],
        out_specs=VMEM_SPEC,
        scratch_shapes=[pltpu.VMEM(parts.shape, parts.dtype)]
        + [pltpu.SemaphoreType.DMA((n,))] * 2,
        compiler_params=pltpu.CompilerParams(collective_id=cid, has_side_effects=True),
        name="coef_scatter",
    )(parts)


def place_kernel(width, row_ref, col_ref, sol_ref, out_ref, spread):
    out_ref[...] = jnp.zeros_like(out_ref)
    wide = jnp.zeros((COLS, width), jnp.int32)

    def step(index, carry):
        at = pl.ds(pl.multiple_of(index * width, 128), width)
        values = sol_ref[:, at].astype(jnp.float32)
        rows = row_ref[:, at] + wide
        for pair in range(NL // 2):
            first = jnp.where(rows == 2 * pair, values, 0.0)
            second = jnp.where(rows == 2 * pair + 1, values, 0.0)
            both = jnp.concatenate([first, second], axis=0)
            spread[pair * 2 * COLS : (pair + 1) * 2 * COLS, :] = both.astype(jnp.bfloat16)
        degree = lax.broadcasted_iota(jnp.int32, (NL, width), 0)
        hot = jnp.where(degree == col_ref[:, at], 1.0, 0.0).astype(jnp.bfloat16)
        out_ref[...] += lax.dot_general(
            spread[...], hot, (((1,), (1,)), ((), ())), preferred_element_type=jnp.float32
        )
        return carry

    lax.fori_loop(0, sol_ref.shape[1] // width, step, 0)


def place(rows, cols, sol):
    kdev = sol.shape[1]
    width = next(w for w in (512, 384, 256, 128) if kdev % w == 0)
    return pl.pallas_call(
        functools.partial(place_kernel, width),
        out_shape=jax.ShapeDtypeStruct((NL * COLS, NL), jnp.float32),
        in_specs=[VMEM_SPEC] * 3,
        out_specs=VMEM_SPEC,
        scratch_shapes=[pltpu.VMEM((NL * COLS, width), jnp.bfloat16)],
        compiler_params=pltpu.CompilerParams(vmem_limit_bytes=32 << 20),
        name="place",
    )(rows, cols, sol)


def share_kernel(
    n, nc, width, row_ref, col_ref, sol_ref, out_ref,
    spread, acc, sent, landed, gathered, send_a, recv_a, send_b, recv_b,
):
    me = lax.axis_index("obs")
    mine = lax.axis_index("coef")
    owned = NL // nc
    sub = owned // n
    span = sub * COLS
    barrier = pltpu.get_barrier_semaphore()
    for axis, count, rank in (("obs", n, me), ("coef", nc, mine)):
        for step in range(1, count):
            pl.semaphore_signal(
                barrier,
                inc=1,
                device_id={axis: lax.rem(rank + step, count)},
                device_id_type=MESH,
            )
    acc[...] = jnp.zeros_like(acc)
    wide = jnp.zeros((COLS, width), jnp.int32)

    def step_of(index, carry):
        at = pl.ds(pl.multiple_of(index * width, 128), width)
        values = sol_ref[:, at].astype(jnp.float32)
        rows = row_ref[:, at] + wide - me * sub
        for pair in range(nc * sub // 2):
            halves = []
            for entry in (2 * pair, 2 * pair + 1):
                row = entry // sub * owned + entry % sub
                halves.append(jnp.where(rows == row, values, 0.0))
            both = jnp.concatenate(halves, axis=0)
            spread[pair * 2 * COLS : (pair + 1) * 2 * COLS, :] = both.astype(jnp.bfloat16)
        degree = lax.broadcasted_iota(jnp.int32, (NL, width), 0)
        hot = jnp.where(degree == col_ref[:, at], 1.0, 0.0).astype(jnp.bfloat16)
        acc[...] += lax.dot_general(
            spread[...], hot, (((1,), (1,)), ((), ())), preferred_element_type=jnp.float32
        )
        return carry

    lax.fori_loop(0, sol_ref.shape[1] // width, step_of, 0)
    for owner in range(nc):
        sent[owner] = acc[owner * span : (owner + 1) * span, :].astype(jnp.bfloat16)
    pl.semaphore_wait(barrier, n + nc - 2)
    copies = []
    for step in range(1, nc):
        target = lax.rem(mine + step, nc)
        copy = push("coef", nc, mine, step, sent.at[target], landed.at[step], send_a, recv_a)
        copy.start()
        copies.append(copy)
    total = sent[mine].astype(jnp.float32)
    for step in range(1, nc):
        copies[step - 1].wait()
        total = total + landed[step].astype(jnp.float32)
    gathered[0] = total.astype(jnp.bfloat16)
    copies = []
    for step in range(1, n):
        copy = push("obs", n, me, step, gathered.at[0], gathered.at[step], send_b, recv_b)
        copy.start()
        copies.append(copy)
    for step in range(n):
        if step:
            copies[step - 1].wait()
        origin = lax.rem(me + n - step, n)
        at = pl.ds(pl.multiple_of(origin * span, COLS), span)
        out_ref[at, :] = gathered[step].astype(jnp.float32)


def share(n, nc, rows, cols, sol):
    kdev = sol.shape[1]
    width = next(w for w in (1152, 512, 384, 256, 128) if kdev % w == 0)
    part = NL // n * COLS
    span = part // nc
    return pl.pallas_call(
        functools.partial(share_kernel, n, nc, width),
        out_shape=jax.ShapeDtypeStruct((n * span, NL), jnp.float32),
        in_specs=[VMEM_SPEC] * 3,
        out_specs=VMEM_SPEC,
        scratch_shapes=[
            pltpu.VMEM((part, width), jnp.bfloat16),
            pltpu.VMEM((part, NL), jnp.float32),
            pltpu.VMEM((nc, span, NL), jnp.bfloat16),
            pltpu.VMEM((nc, span, NL), jnp.bfloat16),
            pltpu.VMEM((n, span, NL), jnp.bfloat16),
        ]
        + [pltpu.SemaphoreType.DMA((nc,))] * 2
        + [pltpu.SemaphoreType.DMA((n,))] * 2,
        compiler_params=pltpu.CompilerParams(
            collective_id=1, has_side_effects=True, vmem_limit_bytes=32 << 20
        ),
        name="share",
    )(rows, cols, sol)


def table_of(level, order, valid):
    product = (level - order) * (level + order)
    denom = jnp.where(valid, product, 1.0)
    first = jnp.sqrt(jnp.maximum((2.0 * level - 1.0) * (2.0 * level + 1.0), 0.0) / denom)
    second = jnp.sqrt(
        jnp.maximum((2.0 * level + 1.0) * (level + order - 1.0) * (level - order - 1.0), 0.0)
        / (denom * jnp.maximum(2.0 * level - 3.0, 1.0))
    )
    return jnp.where(valid, first, 0.0), jnp.where(valid, second, 0.0)


def legendre_kernel(
    angle_ref, local_ref, out_ref, a_c, b_c, a_s, b_s, grow, w_ref
):
    lats, lanes = angle_ref.shape[1:]
    w_ref[...] = local_ref[...].T
    order = angle_ref[0, 0:1, :]
    other = float(NL) - order
    count = lax.broadcasted_iota(jnp.int32, (NL, lanes), 0).astype(jnp.float32)
    wide = jnp.zeros((NL, lanes), jnp.float32)
    low = order + wide
    high = other + wide
    level = count + low
    a, b = table_of(level, low, jnp.logical_and(count > 0.0, level < float(NL)))
    a_c[...] = a
    b_c[...] = b
    a, b = table_of(count, high, count > high)
    a_s[...] = a
    b_s[...] = b
    safe = jnp.maximum(count, 1.0)
    grow[...] = jnp.where(
        count == 1.0, math.sqrt(3.0), jnp.sqrt((2.0 * safe + 1.0) / (2.0 * safe))
    )
    cosine = angle_ref[1]
    sine = angle_ref[2]
    zero = cosine * 0.0
    low = angle_ref[0]
    high = float(NL) - low

    def climb(degree, carry):
        diag, dc, ds = carry
        diag = diag * sine * grow[pl.ds(degree, 1), :]
        here = degree.astype(jnp.float32)
        return diag, jnp.where(low == here, diag, dc), jnp.where(high == here, diag, ds)

    start = zero + 1.0
    _, dc, ds = lax.fori_loop(
        1, NL, climb, (start, jnp.where(low == 0.0, start, zero), zero), unroll=4
    )
    acc_c = dc * w_ref[pl.ds(0, 1), :]

    def advance(column, carry):
        pc, ec, ps, es, acc_c, acc_s = carry
        at = pl.ds(column, 1)
        w = w_ref[at, :]
        vc = a_c[at, :] * cosine * pc - b_c[at, :] * ec
        begin = jnp.where(high == column.astype(jnp.float32), ds, 0.0)
        vs = a_s[at, :] * cosine * ps - b_s[at, :] * es + begin
        return vc, pc, vs, ps, acc_c + vc * w, acc_s + vs * w

    _, _, _, _, acc_c, acc_s = lax.fori_loop(
        1, NL, advance, (dc, zero, zero, zero, acc_c, zero), unroll=4
    )
    out_ref[0] = acc_c / math.sqrt(NL)
    out_ref[1] = acc_s / math.sqrt(NL)


def legendre(orders, colatitude, w):
    lanes = w.shape[0]
    lats = colatitude.shape[0]
    which = lax.broadcasted_iota(jnp.int32, (3, lats, lanes), 0)
    angles = jnp.where(
        which == 0,
        orders[None, None, :],
        jnp.where(which == 1, jnp.cos(colatitude)[:, None], jnp.sin(colatitude)[:, None]),
    )
    table = pltpu.VMEM((NL, lanes), jnp.float32)
    return pl.pallas_call(
        legendre_kernel,
        out_shape=jax.ShapeDtypeStruct((2, lats, lanes), jnp.float32),
        in_specs=[VMEM_SPEC] * 2,
        out_specs=VMEM_SPEC,
        scratch_shapes=[table] * 6,
        name="legendre",
    )(
        angles,
        w,
    )


def wave_tables(rows, longitudes):
    steps_k = jnp.arange(longitudes, dtype=jnp.int32)
    scale = 2.0 * math.pi / longitudes
    cos_angle = (rows[:, None] * steps_k[None, :] % longitudes).astype(jnp.float32) * scale
    sin_angle = ((NL - rows)[:, None] * steps_k[None, :] % longitudes).astype(jnp.float32) * scale
    return (jnp.cos(cos_angle), jnp.sin(sin_angle))


def body(design, observations, shift_table, shift_index, coef_perm, order_map):
    obs_count = lax.axis_size("obs")
    coef_count = lax.axis_size("coef")
    coef_rank = lax.axis_index("coef")
    obs_rank = lax.axis_index("obs")
    kdev = design.shape[1]
    chunk = kdev // obs_count
    paired_up = all(c & (c - 1) == 0 for c in (obs_count, coef_count))
    direct = chunk % 128 == 0 and paired_up
    table_index = jnp.arange(NSHIFT, dtype=jnp.int32)
    shifts = jnp.sum(
        jnp.where(shift_index[:, None] == table_index[None, :], shift_table[None, :], 0.0), axis=1
    )
    centre = shifts + CENTRE_OFFSET
    ratio_start = centre / HALF_WIDTH

    keep = [centre]
    gain = [centre]
    factor = 1.0 / ratio_start
    for iteration in range(ITERS):
        factor_next = 1.0 / (2.0 * ratio_start - factor)
        keep.append(factor_next * factor)
        gain.append(2.0 * factor_next / HALF_WIDTH)
        factor = factor_next
    keep = jnp.stack(keep)[:, :, None]
    gain = jnp.stack(gain)[:, :, None]
    if direct:
        full = solve(
            obs_count, coef_count, observations, design, shifts[:, None], keep, gain
        )
    else:
        full = solve_plain(coef_count, observations, design, shifts[:, None], keep, gain)
    block_count = coef_count * BPO
    block_rows = NL // block_count
    owned_rows = kdev // NL
    block_ids = jnp.arange(block_count, dtype=jnp.int32)
    position = jnp.sum(
        jnp.where(order_map[:, None] == block_ids[None, :], block_ids[:, None], 0), axis=0
    )
    paired_row = coef_perm // NL
    column = coef_perm % NL
    place_of = jnp.sum(
        jnp.where(
            (paired_row // block_rows)[None, :] == block_ids[:, None], position[:, None], 0
        ),
        axis=0,
    )
    owner_row = place_of * block_rows + paired_row % block_rows
    lanes = owned_rows * COLS
    if direct and owned_rows % (2 * obs_count) == 0:
        local = share(obs_count, coef_count, owner_row[None, :], column[None, :], full)
    else:
        placed = place(owner_row[None, :], column[None, :], full)
        outgoing = placed.astype(jnp.bfloat16).reshape(coef_count, lanes, NL)
        local = coef_scatter(outgoing, coef_count, 5)
    my_blocks = lax.dynamic_slice_in_dim(order_map, coef_rank * BPO, BPO)
    row_offsets = jnp.arange(block_rows, dtype=jnp.int32)
    owned_canon = (my_blocks[:, None] * block_rows + row_offsets[None, :]).reshape(owned_rows)
    lat_block = LAT_DEV * coef_count
    lat_total = lat_block * obs_count
    lat_ids = obs_rank * lat_block + jnp.arange(lat_block, dtype=jnp.int32)
    colatitude = math.pi * (lat_ids.astype(jnp.float32) + 0.5) / lat_total
    orders = jnp.repeat(owned_canon, COLS).astype(jnp.float32)
    parts = legendre(orders, colatitude, local).reshape(2, lat_block, owned_rows, COLS)
    band = parts.transpose(2, 0, 3, 1)
    own_cos, own_sin = wave_tables(owned_canon, NLON)
    first_sum = jnp.einsum("lqc,qk->lck", parts[0], own_cos, precision=lax.Precision.HIGHEST)
    second_sum = jnp.einsum("lqc,qk->lck", parts[1], own_sin, precision=lax.Precision.HIGHEST)
    shares = ((first_sum + second_sum) / math.sqrt(NL)).reshape(
        coef_count, LAT_DEV * COLS, NLON
    )
    field = coef_scatter(shares, coef_count, 6).reshape(LAT_DEV, COLS, NLON).transpose(1, 0, 2)
    return (band, field)


def solution(mesh):
    placed = (P("obs", "coef"), P(None, "obs"), P(), P(), P("coef"), P())
    return jax.shard_map(
        body,
        mesh=mesh,
        in_specs=placed,
        out_specs=(P("coef", None, None, "obs"), P(None, ("obs", "coef"), None)),
        check_vma=False,
    )
```

```python
import functools
import math

import jax
import jax.numpy as jnp
from jax import lax
from jax.experimental import pallas as pl
from jax.experimental.pallas import tpu as pltpu
from jax.sharding import PartitionSpec as P

NL = 192
COLS = 8
ITERS = 2
NSHIFT = 16
BPO = 2
NLON = 1024
LAT_DEV = 1

CENTRE_OFFSET = 1.25
HALF_WIDTH = 0.95
VMEM_SPEC = pl.BlockSpec(memory_space=pltpu.VMEM)
MESH = pl.DeviceIdType.MESH


def greet(axis, n, me):
    barrier = pltpu.get_barrier_semaphore()
    for step in range(1, n):
        pl.semaphore_signal(
            barrier, inc=1, device_id={axis: lax.rem(me + step, n)}, device_id_type=MESH
        )
    pl.semaphore_wait(barrier, n - 1)


def push(axis, n, me, step, src, dst, send_sem, recv_sem):
    return pltpu.make_async_remote_copy(
        src_ref=src,
        dst_ref=dst,
        send_sem=send_sem.at[step],
        recv_sem=recv_sem.at[step],
        device_id={axis: lax.rem(me + step, n)},
        device_id_type=MESH,
    )


def flip(index, mask):
    other = index
    bit = 1
    while bit <= mask:
        if mask & bit:
            other = other + bit - 2 * bit * (index // bit % 2)
        bit *= 2
    return other


def swap(axis, rank, mask, src, dst, send_sem, recv_sem):
    return pltpu.make_async_remote_copy(
        src_ref=src,
        dst_ref=dst,
        send_sem=send_sem.at[mask],
        recv_sem=recv_sem.at[mask],
        device_id={axis: flip(rank, mask)},
        device_id_type=MESH,
    )


def solver_kernel(
    n, nc, obs_ref, design_ref, shift_ref, keep_ref, gain_ref, map_ref, place_ref,
    band_out, field_out,
    held, part, landed, gathered, image_sent, image_landed, left_ref, acc,
    hot, raw, table, a_tab, b_tab, grow, picked, wave_ref, spectrum, spectrum_t, sent, arrived,
    load_sem, send_a, recv_a, send_b, recv_b, send_c, recv_c, send_d, recv_d,
):
    me = lax.axis_index("obs")
    mine = lax.axis_index("coef")
    chunk = held.shape[2]
    lanes = hot.shape[0]
    lats = LAT_DEV * nc
    owned = NL // nc
    far_first = list(range(n - 1, 0, -1))

    def load(mask):
        return pltpu.make_async_copy(
            design_ref.at[:, pl.ds(pl.multiple_of(flip(me, mask) * chunk, 128), chunk)],
            held.at[mask],
            load_sem.at[mask],
        )

    for mask in far_first + [0]:
        load(mask).start()
    barrier = pltpu.get_barrier_semaphore()
    for axis, count, rank in (("obs", n, me), ("coef", nc, mine)):
        for mask in range(1, count):
            pl.semaphore_signal(
                barrier, inc=1, device_id={axis: flip(rank, mask)}, device_id_type=MESH
            )

    def scatter_copy(rnd, mask):
        return swap(
            "obs", me, mask, part.at[rnd, mask], landed.at[rnd, mask], send_a.at[rnd], recv_a.at[rnd]
        )

    def gather_copy(rnd, mask):
        return swap(
            "obs", me, mask, gathered.at[rnd, 0], gathered.at[rnd, mask],
            send_b.at[rnd], recv_b.at[rnd],
        )

    def image_copy(rnd, mask):
        return swap(
            "coef", mine, mask, image_sent.at[rnd], image_landed.at[rnd, mask],
            send_c.at[rnd], recv_c.at[rnd],
        )

    def final_copy(mask):
        return swap("coef", mine, mask, sent, arrived.at[mask], send_d, recv_d)

    def canon(shape, axis):
        lane = lax.broadcasted_iota(jnp.int32, shape, axis)
        blocks = nc * BPO
        size = NL // blocks
        total = jnp.zeros(shape, jnp.int32)
        for block in range(blocks):
            inside = jnp.logical_and(lane >= block * size, lane < (block + 1) * size)
            total = jnp.where(inside, lane + (map_ref[block] - block) * size, total)
        return total

    def legendre_table():
        order = canon((8, lanes), 1).astype(jnp.float32)
        other = float(NL) - order
        count = lax.broadcasted_iota(jnp.int32, (NL, lanes), 0).astype(jnp.float32)
        low = order[0:1, :] + jnp.zeros((NL, lanes), jnp.float32)
        high = float(NL) - low
        cosine_part = count < high
        level = jnp.where(cosine_part, count + low, count)
        degree_order = jnp.where(cosine_part, low, high)
        valid = jnp.logical_and(count != high, count > 0.0)
        a, b = table_of(level, degree_order, valid)
        a_tab[...] = a
        b_tab[...] = b
        safe = jnp.maximum(count, 1.0)
        grow[...] = jnp.where(
            count == 1.0, math.sqrt(3.0), jnp.sqrt((2.0 * safe + 1.0) / (2.0 * safe))
        )
        lat = lax.broadcasted_iota(jnp.int32, (8, lanes), 0) + me * lats
        colatitude = math.pi * (lat.astype(jnp.float32) + 0.5) / (lats * n)
        cosine = jnp.cos(colatitude)
        sine = jnp.sin(colatitude)

        def climb(degree, carry):
            diag, dc, ds = carry
            diag = diag * (sine * grow[pl.ds(degree, 1), :])
            here = degree.astype(jnp.float32)
            return diag, jnp.where(order == here, diag, dc), jnp.where(other == here, diag, ds)

        start = jnp.ones((8, lanes), jnp.float32)
        zero = jnp.zeros((8, lanes), jnp.float32)
        _, dc, ds = lax.fori_loop(
            1, NL, climb, (start, jnp.where(order == 0.0, start, zero), zero), unroll=8
        )
        def keep_row(column, value):
            for half in range(lanes // 128):
                raw[half, pl.ds(pl.multiple_of(column * 8, 8), 8), :] = value[
                    :, half * 128 : (half + 1) * 128
                ]

        keep_row(0, dc)

        def advance(column, carry):
            now, before = carry
            at = pl.ds(column, 1)
            begin = jnp.where(other == column.astype(jnp.float32), ds, 0.0)
            value = (a_tab[at, :] * cosine) * now - (b_tab[at, :] * before - begin)
            keep_row(column, value)
            return value, now

        lax.fori_loop(1, NL, advance, (dc, zero), unroll=8)
        for t in range(lats):
            for half in range(lanes // 128):
                table[t, :, half * 128 : (half + 1) * 128] = raw[
                    half, pl.ds(t, NL, stride=8), :
                ].astype(jnp.bfloat16)

    tile = 256
    tiles = hot.shape[1] // tile

    def build_hot():
        def one(index, carry):
            at = pl.ds(pl.multiple_of(index * tile, 128), tile)
            row = lax.broadcasted_iota(jnp.int32, (lanes, tile), 0)
            hot[:, at] = jnp.where(row == place_ref[0:1, at], 1.0, 0.0).astype(jnp.bfloat16)
            return carry

        lax.fori_loop(0, tiles, one, 0)

    def pick(first, last):
        def one(index, carry):
            at = pl.ds(pl.multiple_of(index * tile, 128), tile)
            column = place_ref[1:2, at] + jnp.zeros((8, tile), jnp.int32)
            group = column // 8
            inner = column - group * 8 == lax.broadcasted_iota(jnp.int32, (8, tile), 0)
            for t in range(lats):
                product = jnp.dot(table[t], hot[:, at], preferred_element_type=jnp.float32)
                kept = jnp.zeros((8, tile), jnp.float32)
                for q in range(NL // 8):
                    kept = jnp.where(group == q, product[q * 8 : q * 8 + 8], kept)
                picked[t : t + 1, at] = jnp.sum(
                    jnp.where(inner, kept, 0.0), axis=0, keepdims=True
                )
            return carry

        lax.fori_loop(first, last, one, 0)

    def waves():
        order = canon((lanes, 128), 0)
        step = lax.broadcasted_iota(jnp.int32, (lanes, 128), 1)
        scale = 2.0 * math.pi / NLON
        for which in range(2):
            speed = order if which == 0 else NL - order
            fine = lax.rem(speed * step, NLON).astype(jnp.float32) * scale
            coarse = lax.rem(speed * step * 128, NLON).astype(jnp.float32) * scale
            fine_cos, fine_sin = jnp.cos(fine), jnp.sin(fine)
            coarse_cos, coarse_sin = jnp.cos(coarse), jnp.sin(coarse)
            for block in range(NLON // 128):
                cos_b = coarse_cos[:, block : block + 1]
                sin_b = coarse_sin[:, block : block + 1]
                if which == 0:
                    value = cos_b * fine_cos - sin_b * fine_sin
                else:
                    value = sin_b * fine_cos + cos_b * fine_sin
                high = value.astype(jnp.bfloat16)
                at = slice(block * 128, block * 128 + 128)
                wave_ref[which, 0, :, at] = high
                wave_ref[which, 1, :, at] = (value - high.astype(jnp.float32)).astype(jnp.bfloat16)

    def transposed_pass(rnd, filler):
        def product(mask):
            both = jnp.dot(left_ref[...], held[mask], preferred_element_type=jnp.float32)
            return both[:COLS] + both[COLS:]

        for mask in far_first:
            if rnd == 0:
                load(mask).wait()
            part[rnd, mask] = product(mask).astype(jnp.bfloat16)
            scatter_copy(rnd, mask).start()
        if rnd == 0:
            load(0).wait()
        total = product(0)
        filler()
        for mask in far_first:
            scatter_copy(rnd, mask).wait_recv()
            total = total + landed[rnd, mask].astype(jnp.float32)
        gathered[rnd, 0] = total.astype(jnp.bfloat16)
        for mask in far_first:
            gather_copy(rnd, mask).start()

    def image_of(rnd, first, second):
        for mask in range(n):
            if mask:
                gather_copy(rnd, mask).wait_recv()
            term = lax.dot_general(
                gathered[rnd, mask],
                held[mask],
                (((1,), (1,)), ((), ())),
                preferred_element_type=jnp.float32,
            )
            acc[...] = term if mask == 0 else acc[...] + term
            if mask == 0:
                first()
        image = acc[...]
        image_sent[rnd] = image.astype(jnp.bfloat16)
        for mask in range(nc - 1, 0, -1):
            image_copy(rnd, mask).start()
        second()
        for mask in range(1, nc):
            image_copy(rnd, mask).wait_recv()
            image = image + image_landed[rnd, mask].astype(jnp.float32)
        return image

    def split(value):
        high = value.astype(jnp.bfloat16).astype(jnp.float32)
        left_ref[...] = jnp.concatenate([high, value - high], axis=0).astype(jnp.bfloat16)

    idle = lambda: None
    pick_step = -(-tiles // 3)
    scatter_fill = [build_hot, waves, idle]
    first_fill = [functools.partial(pick, 0, pick_step), idle]
    second_fill = [
        functools.partial(pick, pick_step, 2 * pick_step),
        functools.partial(pick, 2 * pick_step, tiles),
    ]
    legendre_table()
    pl.semaphore_wait(barrier, n + nc - 2)
    residual = obs_ref[...].astype(jnp.float32)
    split(residual)
    transposed_pass(0, scatter_fill[0])
    direction = residual / keep_ref[0]
    answer = direction
    for rnd in range(1, ITERS + 1):
        image = image_of(rnd - 1, first_fill[rnd - 1], second_fill[rnd - 1])
        if rnd == 1:
            image = image / keep_ref[0]
        residual = residual - (image + shift_ref[...] * direction)
        direction = keep_ref[rnd] * direction + gain_ref[rnd] * residual
        answer = answer + direction
        split(answer if rnd == ITERS else direction)
        transposed_pass(rnd, scatter_fill[rnd])
    for mask in range(n):
        if mask:
            gather_copy(ITERS, mask).wait_recv()
        at = pl.ds(pl.multiple_of(flip(me, mask) * chunk, 128), chunk)
        values = gathered[ITERS, mask].astype(jnp.float32)
        cosine_part = place_ref[2:3, at] == 0
        lows, highs = [], []
        for t in range(lats):
            scaled = values * picked[t : t + 1, at]
            low = jnp.where(cosine_part, scaled, 0.0)
            lows.append(low)
            highs.append(scaled - low)
        left = jnp.concatenate(lows + highs, axis=0)
        high = left.astype(jnp.bfloat16).astype(jnp.float32)
        left = jnp.concatenate([high, left - high], axis=0).astype(jnp.bfloat16)
        both = lax.dot_general(
            left, hot[:, at], (((1,), (1,)), ((), ())), preferred_element_type=jnp.float32
        )
        term = both[: 2 * lats * COLS] + both[2 * lats * COLS :]
        sent[...] = term if mask == 0 else sent[...] + term
    for mask in range(nc - 1, 0, -1):
        final_copy(mask).start()
    total = sent[...]
    for mask in range(1, nc):
        final_copy(mask).wait_recv()
        total = total + arrived[mask]
    spectrum[...] = total / math.sqrt(NL)
    side = lats * COLS
    field = jnp.zeros((COLS, NLON), jnp.float32)
    for which in range(2):
        rows = spectrum[pl.ds(pl.multiple_of(which * side + mine * COLS, COLS), COLS), :]
        high = rows.astype(jnp.bfloat16).astype(jnp.float32)
        left = jnp.concatenate([high, rows - high], axis=0).astype(jnp.bfloat16)
        for level in range(2):
            both = jnp.dot(left, wave_ref[which, level], preferred_element_type=jnp.float32)
            field = field + both[:COLS] + both[COLS:]
    field_out[...] = field / math.sqrt(NL)
    spectrum_t[...] = spectrum[...].T
    own = spectrum_t[pl.ds(pl.multiple_of(mine * owned, 8), owned), :]
    band_out[...] = own
    for rnd in range(ITERS + 1):
        for mask in far_first:
            scatter_copy(rnd, mask).wait_send()
            gather_copy(rnd, mask).wait_send()
        if rnd < ITERS:
            for mask in range(1, nc):
                image_copy(rnd, mask).wait_send()
    for mask in range(1, nc):
        final_copy(mask).wait_send()


def solve(n, nc, observations, design, shift, keep, gain, order_map, place):
    rows, kdev = design.shape
    chunk = kdev // n
    rounds = ITERS + 1
    lanes = -(-NL // 128) * 128
    lats = LAT_DEV * nc
    side = 2 * lats * COLS
    blocks = pltpu.VMEM((rounds, n, COLS, chunk), jnp.bfloat16)
    tables = pltpu.VMEM((NL, lanes), jnp.float32)
    return pl.pallas_call(
        functools.partial(solver_kernel, n, nc),
        out_shape=(
            jax.ShapeDtypeStruct((NL // nc, side), jnp.float32),
            jax.ShapeDtypeStruct((COLS, NLON), jnp.float32),
        ),
        in_specs=[VMEM_SPEC, pl.BlockSpec(memory_space=pl.ANY)]
        + [VMEM_SPEC] * 3
        + [pl.BlockSpec(memory_space=pltpu.SMEM), VMEM_SPEC],
        out_specs=(VMEM_SPEC, VMEM_SPEC),
        scratch_shapes=[pltpu.VMEM((n, rows, chunk), jnp.bfloat16)]
        + [blocks] * 3
        + [
            pltpu.VMEM((ITERS, COLS, rows), jnp.bfloat16),
            pltpu.VMEM((ITERS, nc, COLS, rows), jnp.bfloat16),
            pltpu.VMEM((2 * COLS, rows), jnp.bfloat16),
            pltpu.VMEM((COLS, rows), jnp.float32),
            pltpu.VMEM((lanes, kdev), jnp.bfloat16),
            pltpu.VMEM((lanes // 128, NL * 8, 128), jnp.float32),
            pltpu.VMEM((lats, NL, lanes), jnp.bfloat16),
            tables,
            tables,
            tables,
            pltpu.VMEM((8, kdev), jnp.float32),
            pltpu.VMEM((2, 2, lanes, NLON), jnp.bfloat16),
            pltpu.VMEM((side, lanes), jnp.float32),
            pltpu.VMEM((lanes, side), jnp.float32),
            pltpu.VMEM((side, lanes), jnp.float32),
            pltpu.VMEM((nc, side, lanes), jnp.float32),
            pltpu.SemaphoreType.DMA((n,)),
        ]
        + [pltpu.SemaphoreType.DMA((rounds, n))] * 4
        + [pltpu.SemaphoreType.DMA((ITERS, nc))] * 2
        + [pltpu.SemaphoreType.DMA((nc,))] * 2,
        compiler_params=pltpu.CompilerParams(
            collective_id=0, has_side_effects=True, vmem_limit_bytes=56 << 20
        ),
        name="solve",
    )(observations, design, shift, keep, gain, order_map, place)


def sum_kernel(n, x_ref, o_ref, landed, send_sem, recv_sem):
    me = lax.axis_index("coef")
    greet("coef", n, me)
    copies = []
    for step in range(1, n):
        copy = push("coef", n, me, step, x_ref, landed.at[step], send_sem, recv_sem)
        copy.start()
        copies.append(copy)
    total = x_ref[...]
    for step in range(1, n):
        copies[step - 1].wait()
        total = total + landed[step]
    o_ref[...] = total.astype(o_ref.dtype)


def coef_sum(partial, n, cid):
    return pl.pallas_call(
        functools.partial(sum_kernel, n),
        out_shape=jax.ShapeDtypeStruct(partial.shape, jnp.bfloat16),
        in_specs=[VMEM_SPEC],
        out_specs=VMEM_SPEC,
        scratch_shapes=[pltpu.VMEM((n,) + partial.shape, jnp.float32)]
        + [pltpu.SemaphoreType.DMA((n,))] * 2,
        compiler_params=pltpu.CompilerParams(collective_id=cid, has_side_effects=True),
        name="coef_sum",
    )(partial)


def solve_plain(nc, observations, design, shift, keep, gain):
    def transposed_pass(left):
        return lax.psum(jnp.dot(left, design, preferred_element_type=jnp.float32), "obs")

    residual = transposed_pass(observations)
    direction = residual / keep[0]
    solution = direction
    for rnd in range(1, ITERS + 1):
        partial_image = lax.dot_general(
            direction.astype(jnp.bfloat16),
            design,
            (((1,), (1,)), ((), ())),
            preferred_element_type=jnp.float32,
        )
        total = transposed_pass(coef_sum(partial_image, nc, 2 + rnd))
        residual = residual - (total + shift * direction)
        direction = keep[rnd] * direction + gain[rnd] * residual
        solution = solution + direction
    return solution.astype(jnp.bfloat16)


def scatter_kernel(n, x_ref, o_ref, landed, send_sem, recv_sem):
    me = lax.axis_index("coef")
    greet("coef", n, me)
    copies = []
    for step in range(1, n):
        target = lax.rem(me + step, n)
        copy = push("coef", n, me, step, x_ref.at[target], landed.at[step], send_sem, recv_sem)
        copy.start()
        copies.append(copy)
    total = x_ref[me].astype(jnp.float32)
    for step in range(1, n):
        copies[step - 1].wait()
        total = total + landed[step].astype(jnp.float32)
    o_ref[...] = total


def coef_scatter(parts, n, cid):
    return pl.pallas_call(
        functools.partial(scatter_kernel, n),
        out_shape=jax.ShapeDtypeStruct(parts.shape[1:], jnp.float32),
        in_specs=[VMEM_SPEC],
        out_specs=VMEM_SPEC,
        scratch_shapes=[pltpu.VMEM(parts.shape, parts.dtype)]
        + [pltpu.SemaphoreType.DMA((n,))] * 2,
        compiler_params=pltpu.CompilerParams(collective_id=cid, has_side_effects=True),
        name="coef_scatter",
    )(parts)


def place_kernel(width, row_ref, col_ref, sol_ref, out_ref, spread):
    out_ref[...] = jnp.zeros_like(out_ref)
    wide = jnp.zeros((COLS, width), jnp.int32)

    def step(index, carry):
        at = pl.ds(pl.multiple_of(index * width, 128), width)
        values = sol_ref[:, at].astype(jnp.float32)
        rows = row_ref[:, at] + wide
        for pair in range(NL // 2):
            first = jnp.where(rows == 2 * pair, values, 0.0)
            second = jnp.where(rows == 2 * pair + 1, values, 0.0)
            both = jnp.concatenate([first, second], axis=0)
            spread[pair * 2 * COLS : (pair + 1) * 2 * COLS, :] = both.astype(jnp.bfloat16)
        degree = lax.broadcasted_iota(jnp.int32, (NL, width), 0)
        hot = jnp.where(degree == col_ref[:, at], 1.0, 0.0).astype(jnp.bfloat16)
        out_ref[...] += lax.dot_general(
            spread[...], hot, (((1,), (1,)), ((), ())), preferred_element_type=jnp.float32
        )
        return carry

    lax.fori_loop(0, sol_ref.shape[1] // width, step, 0)


def place(rows, cols, sol):
    kdev = sol.shape[1]
    width = next(w for w in (512, 384, 256, 128) if kdev % w == 0)
    return pl.pallas_call(
        functools.partial(place_kernel, width),
        out_shape=jax.ShapeDtypeStruct((NL * COLS, NL), jnp.float32),
        in_specs=[VMEM_SPEC] * 3,
        out_specs=VMEM_SPEC,
        scratch_shapes=[pltpu.VMEM((NL * COLS, width), jnp.bfloat16)],
        compiler_params=pltpu.CompilerParams(vmem_limit_bytes=32 << 20),
        name="place",
    )(rows, cols, sol)


def table_of(level, order, valid):
    product = (level - order) * (level + order)
    denom = jnp.where(valid, product, 1.0)
    first = jnp.sqrt(jnp.maximum((2.0 * level - 1.0) * (2.0 * level + 1.0), 0.0) / denom)
    second = jnp.sqrt(
        jnp.maximum((2.0 * level + 1.0) * (level + order - 1.0) * (level - order - 1.0), 0.0)
        / (denom * jnp.maximum(2.0 * level - 3.0, 1.0))
    )
    return jnp.where(valid, first, 0.0), jnp.where(valid, second, 0.0)


def legendre_kernel(
    angle_ref, local_ref, out_ref, a_c, b_c, a_s, b_s, grow, w_ref
):
    lats, lanes = angle_ref.shape[1:]
    w_ref[...] = local_ref[...].T
    order = angle_ref[0, 0:1, :]
    other = float(NL) - order
    count = lax.broadcasted_iota(jnp.int32, (NL, lanes), 0).astype(jnp.float32)
    wide = jnp.zeros((NL, lanes), jnp.float32)
    low = order + wide
    high = other + wide
    level = count + low
    a, b = table_of(level, low, jnp.logical_and(count > 0.0, level < float(NL)))
    a_c[...] = a
    b_c[...] = b
    a, b = table_of(count, high, count > high)
    a_s[...] = a
    b_s[...] = b
    safe = jnp.maximum(count, 1.0)
    grow[...] = jnp.where(
        count == 1.0, math.sqrt(3.0), jnp.sqrt((2.0 * safe + 1.0) / (2.0 * safe))
    )
    cosine = angle_ref[1]
    sine = angle_ref[2]
    zero = cosine * 0.0
    low = angle_ref[0]
    high = float(NL) - low

    def climb(degree, carry):
        diag, dc, ds = carry
        diag = diag * sine * grow[pl.ds(degree, 1), :]
        here = degree.astype(jnp.float32)
        return diag, jnp.where(low == here, diag, dc), jnp.where(high == here, diag, ds)

    start = zero + 1.0
    _, dc, ds = lax.fori_loop(
        1, NL, climb, (start, jnp.where(low == 0.0, start, zero), zero), unroll=4
    )
    acc_c = dc * w_ref[pl.ds(0, 1), :]

    def advance(column, carry):
        pc, ec, ps, es, acc_c, acc_s = carry
        at = pl.ds(column, 1)
        w = w_ref[at, :]
        vc = a_c[at, :] * cosine * pc - b_c[at, :] * ec
        begin = jnp.where(high == column.astype(jnp.float32), ds, 0.0)
        vs = a_s[at, :] * cosine * ps - b_s[at, :] * es + begin
        return vc, pc, vs, ps, acc_c + vc * w, acc_s + vs * w

    _, _, _, _, acc_c, acc_s = lax.fori_loop(
        1, NL, advance, (dc, zero, zero, zero, acc_c, zero), unroll=4
    )
    out_ref[0] = acc_c / math.sqrt(NL)
    out_ref[1] = acc_s / math.sqrt(NL)


def legendre(orders, colatitude, w):
    lanes = w.shape[0]
    lats = colatitude.shape[0]
    which = lax.broadcasted_iota(jnp.int32, (3, lats, lanes), 0)
    angles = jnp.where(
        which == 0,
        orders[None, None, :],
        jnp.where(which == 1, jnp.cos(colatitude)[:, None], jnp.sin(colatitude)[:, None]),
    )
    table = pltpu.VMEM((NL, lanes), jnp.float32)
    return pl.pallas_call(
        legendre_kernel,
        out_shape=jax.ShapeDtypeStruct((2, lats, lanes), jnp.float32),
        in_specs=[VMEM_SPEC] * 2,
        out_specs=VMEM_SPEC,
        scratch_shapes=[table] * 6,
        name="legendre",
    )(
        angles,
        w,
    )


def wave_tables(rows, longitudes):
    steps_k = jnp.arange(longitudes, dtype=jnp.int32)
    scale = 2.0 * math.pi / longitudes
    cos_angle = (rows[:, None] * steps_k[None, :] % longitudes).astype(jnp.float32) * scale
    sin_angle = ((NL - rows)[:, None] * steps_k[None, :] % longitudes).astype(jnp.float32) * scale
    return (jnp.cos(cos_angle), jnp.sin(sin_angle))


def body(design, observations, shift_table, shift_index, coef_perm, order_map):
    obs_count = lax.axis_size("obs")
    coef_count = lax.axis_size("coef")
    coef_rank = lax.axis_index("coef")
    obs_rank = lax.axis_index("obs")
    kdev = design.shape[1]
    chunk = kdev // obs_count
    paired_up = all(c & (c - 1) == 0 for c in (obs_count, coef_count))
    direct = (
        chunk % 128 == 0
        and kdev % 256 == 0
        and paired_up
        and LAT_DEV * coef_count <= 8
        and NL // coef_count % 8 == 0
    )
    table_index = jnp.arange(NSHIFT, dtype=jnp.int32)
    shifts = jnp.sum(
        jnp.where(shift_index[:, None] == table_index[None, :], shift_table[None, :], 0.0), axis=1
    )
    centre = shifts + CENTRE_OFFSET
    ratio_start = centre / HALF_WIDTH

    keep = [centre]
    gain = [centre]
    factor = 1.0 / ratio_start
    for iteration in range(ITERS):
        factor_next = 1.0 / (2.0 * ratio_start - factor)
        keep.append(factor_next * factor)
        gain.append(2.0 * factor_next / HALF_WIDTH)
        factor = factor_next
    keep = jnp.stack(keep)[:, :, None]
    gain = jnp.stack(gain)[:, :, None]
    block_count = coef_count * BPO
    block_rows = NL // block_count
    owned_rows = kdev // NL
    block_ids = jnp.arange(block_count, dtype=jnp.int32)
    position = jnp.sum(
        jnp.where(order_map[:, None] == block_ids[None, :], block_ids[:, None], 0), axis=0
    )
    paired_row = coef_perm // NL
    column = coef_perm % NL
    place_of = jnp.sum(
        jnp.where(
            (paired_row // block_rows)[None, :] == block_ids[:, None], position[:, None], 0
        ),
        axis=0,
    )
    owner_row = place_of * block_rows + paired_row % block_rows
    if direct:
        where = jnp.stack([owner_row, column, (paired_row + column >= NL).astype(jnp.int32)])
        band, field = solve(
            obs_count, coef_count, observations, design, shifts[:, None], keep, gain,
            order_map, where,
        )
        lats = LAT_DEV * coef_count
        band = band.reshape(owned_rows, 2, lats, COLS).transpose(0, 1, 3, 2)
        return (band, field[:, None, :])
    full = solve_plain(coef_count, observations, design, shifts[:, None], keep, gain)
    lanes = owned_rows * COLS
    placed = place(owner_row[None, :], column[None, :], full)
    outgoing = placed.astype(jnp.bfloat16).reshape(coef_count, lanes, NL)
    local = coef_scatter(outgoing, coef_count, 5)
    my_blocks = lax.dynamic_slice_in_dim(order_map, coef_rank * BPO, BPO)
    row_offsets = jnp.arange(block_rows, dtype=jnp.int32)
    owned_canon = (my_blocks[:, None] * block_rows + row_offsets[None, :]).reshape(owned_rows)
    lat_block = LAT_DEV * coef_count
    lat_total = lat_block * obs_count
    lat_ids = obs_rank * lat_block + jnp.arange(lat_block, dtype=jnp.int32)
    colatitude = math.pi * (lat_ids.astype(jnp.float32) + 0.5) / lat_total
    orders = jnp.repeat(owned_canon, COLS).astype(jnp.float32)
    parts = legendre(orders, colatitude, local).reshape(2, lat_block, owned_rows, COLS)
    band = parts.transpose(2, 0, 3, 1)
    own_cos, own_sin = wave_tables(owned_canon, NLON)
    first_sum = jnp.einsum("lqc,qk->lck", parts[0], own_cos, precision=lax.Precision.HIGHEST)
    second_sum = jnp.einsum("lqc,qk->lck", parts[1], own_sin, precision=lax.Precision.HIGHEST)
    shares = ((first_sum + second_sum) / math.sqrt(NL)).reshape(
        coef_count, LAT_DEV * COLS, NLON
    )
    field = coef_scatter(shares, coef_count, 6).reshape(LAT_DEV, COLS, NLON).transpose(1, 0, 2)
    return (band, field)


def solution(mesh):
    placed = (P("obs", "coef"), P(None, "obs"), P(), P(), P("coef"), P())
    return jax.shard_map(
        body,
        mesh=mesh,
        in_specs=placed,
        out_specs=(P("coef", None, None, "obs"), P(None, ("obs", "coef"), None)),
        check_vma=False,
    )
```

```python
import functools
import math

import jax
import jax.numpy as jnp
from jax import lax
from jax.experimental import pallas as pl
from jax.experimental.pallas import tpu as pltpu
from jax.sharding import PartitionSpec as P

NL = 192
COLS = 8
ITERS = 2
NSHIFT = 16
BPO = 2
NLON = 1024
LAT_DEV = 1

CENTRE_OFFSET = 1.25
HALF_WIDTH = 0.95
VMEM_SPEC = pl.BlockSpec(memory_space=pltpu.VMEM)
MESH = pl.DeviceIdType.MESH


def greet(axis, n, me):
    barrier = pltpu.get_barrier_semaphore()
    for step in range(1, n):
        pl.semaphore_signal(
            barrier, inc=1, device_id={axis: lax.rem(me + step, n)}, device_id_type=MESH
        )
    pl.semaphore_wait(barrier, n - 1)


def push(axis, n, me, step, src, dst, send_sem, recv_sem):
    return pltpu.make_async_remote_copy(
        src_ref=src,
        dst_ref=dst,
        send_sem=send_sem.at[step],
        recv_sem=recv_sem.at[step],
        device_id={axis: lax.rem(me + step, n)},
        device_id_type=MESH,
    )


def flip(index, mask):
    other = index
    bit = 1
    while bit <= mask:
        if mask & bit:
            other = other + bit - 2 * bit * (index // bit % 2)
        bit *= 2
    return other


def swap(axis, rank, mask, src, dst, send_sem, recv_sem):
    return pltpu.make_async_remote_copy(
        src_ref=src,
        dst_ref=dst,
        send_sem=send_sem.at[mask],
        recv_sem=recv_sem.at[mask],
        device_id={axis: flip(rank, mask)},
        device_id_type=MESH,
    )


def solver_kernel(
    n, nc, obs_ref, design_ref, shift_table, shift_index, map_ref, perm_ref,
    band_out, field_out,
    held, part, landed, gathered, image_sent, image_landed, left_ref, acc,
    places, hot, raw, table, a_tab, b_tab, grow, picked, wave_ref, spectrum, band, sent, arrived,
    load_sem, send_a, recv_a, send_b, recv_b, send_c, recv_c, send_d, recv_d,
):
    me = lax.axis_index("obs")
    mine = lax.axis_index("coef")
    chunk = held.shape[2]
    lanes = hot.shape[0]
    lats = LAT_DEV * nc
    owned = NL // nc
    far_first = list(range(n - 1, 0, -1))

    def load(mask):
        return pltpu.make_async_copy(
            design_ref.at[:, pl.ds(pl.multiple_of(flip(me, mask) * chunk, 128), chunk)],
            held.at[mask],
            load_sem.at[mask],
        )

    for mask in far_first + [0]:
        load(mask).start()
    barrier = pltpu.get_barrier_semaphore()
    for axis, count, rank in (("obs", n, me), ("coef", nc, mine)):
        for mask in range(1, count):
            pl.semaphore_signal(
                barrier, inc=1, device_id={axis: flip(rank, mask)}, device_id_type=MESH
            )

    def scatter_copy(rnd, mask):
        return swap(
            "obs", me, mask, part.at[rnd, mask], landed.at[rnd, mask], send_a.at[rnd], recv_a.at[rnd]
        )

    def gather_copy(rnd, mask):
        return swap(
            "obs", me, mask, gathered.at[rnd, 0], gathered.at[rnd, mask],
            send_b.at[rnd], recv_b.at[rnd],
        )

    def image_copy(rnd, mask):
        return swap(
            "coef", mine, mask, image_sent.at[rnd], image_landed.at[rnd, mask],
            send_c.at[rnd], recv_c.at[rnd],
        )

    def final_copy(mask):
        return swap("coef", mine, mask, sent, arrived.at[mask], send_d, recv_d)

    def canon(shape, axis):
        lane = lax.broadcasted_iota(jnp.int32, shape, axis)
        blocks = nc * BPO
        size = NL // blocks
        total = jnp.zeros(shape, jnp.int32)
        for block in range(blocks):
            inside = jnp.logical_and(lane >= block * size, lane < (block + 1) * size)
            total = jnp.where(inside, lane + (map_ref[block] - block) * size, total)
        return total

    def legendre_table():
        order = canon((8, lanes), 1).astype(jnp.float32)
        other = float(NL) - order
        count = lax.broadcasted_iota(jnp.int32, (NL, lanes), 0).astype(jnp.float32)
        low = order[0:1, :] + jnp.zeros((NL, lanes), jnp.float32)
        high = float(NL) - low
        cosine_part = count < high
        level = jnp.where(cosine_part, count + low, count)
        degree_order = jnp.where(cosine_part, low, high)
        valid = jnp.logical_and(count != high, count > 0.0)
        a, b = table_of(level, degree_order, valid)
        a_tab[...] = a
        b_tab[...] = b
        safe = jnp.maximum(count, 1.0)
        grow[...] = jnp.where(
            count == 1.0, math.sqrt(3.0), jnp.sqrt((2.0 * safe + 1.0) / (2.0 * safe))
        )
        lat = lax.broadcasted_iota(jnp.int32, (8, lanes), 0) + me * lats
        colatitude = math.pi * (lat.astype(jnp.float32) + 0.5) / (lats * n)
        cosine = jnp.cos(colatitude)
        sine = jnp.sin(colatitude)

        def climb(degree, carry):
            diag, dc, ds = carry
            diag = diag * (sine * grow[pl.ds(degree, 1), :])
            here = degree.astype(jnp.float32)
            return diag, jnp.where(order == here, diag, dc), jnp.where(other == here, diag, ds)

        start = jnp.ones((8, lanes), jnp.float32)
        zero = jnp.zeros((8, lanes), jnp.float32)
        _, dc, ds = lax.fori_loop(
            1, NL, climb, (start, jnp.where(order == 0.0, start, zero), zero), unroll=8
        )
        def keep_row(column, value):
            for half in range(lanes // 128):
                raw[half, pl.ds(pl.multiple_of(column * 8, 8), 8), :] = value[
                    :, half * 128 : (half + 1) * 128
                ]

        keep_row(0, dc)

        def advance(column, carry):
            now, before = carry
            at = pl.ds(column, 1)
            begin = jnp.where(other == column.astype(jnp.float32), ds, 0.0)
            value = (a_tab[at, :] * cosine) * now - (b_tab[at, :] * before - begin)
            keep_row(column, value)
            return value, now

        lax.fori_loop(1, NL, advance, (dc, zero), unroll=8)
        for t in range(lats):
            for half in range(lanes // 128):
                table[t, :, half * 128 : (half + 1) * 128] = raw[
                    half, pl.ds(t, NL, stride=8), :
                ].astype(jnp.bfloat16)

    tile = 256
    tiles = hot.shape[1] // tile

    def find_places():
        index = perm_ref[...].astype(jnp.float32)
        paired = jnp.floor((index + 0.5) * (1.0 / NL))
        column = index - paired * NL
        blocks = nc * BPO
        size = NL // blocks
        block = jnp.floor((paired + 0.5) * (1.0 / size))
        inside = paired - block * size
        row = jnp.zeros_like(index)
        for spot in range(blocks):
            here = block == map_ref[spot].astype(jnp.float32)
            row = jnp.where(here, inside + spot * size, row)
        places[0] = row
        group = jnp.floor((column + 0.5) * 0.125)
        places[1] = group
        places[2] = column - group * 8.0
        places[3] = jnp.where(paired + column < NL, 1.0, 0.0)

    def build_hot():
        def one(index, carry):
            at = pl.ds(pl.multiple_of(index * 128, 128), 128)
            row = lax.broadcasted_iota(jnp.int32, (lanes, 128), 0).astype(jnp.float32)
            same = row == places[0, pl.ds(index, 1), :]
            hot[:, at] = jnp.where(same, 1.0, 0.0).astype(jnp.bfloat16)
            return carry

        lax.fori_loop(0, tiles * (tile // 128), one, 0)

    def pick(first, last):
        def one(index, carry):
            wide = pl.ds(pl.multiple_of(index * tile, 128), tile)
            sub = lax.broadcasted_iota(jnp.int32, (8, 128), 0).astype(jnp.float32)
            for t in range(lats):
                product = jnp.dot(table[t], hot[:, wide], preferred_element_type=jnp.float32)
                for half in range(tile // 128):
                    spot = pl.ds(index * (tile // 128) + half, 1)
                    group = places[1, spot, :] + jnp.zeros_like(sub)
                    kept = jnp.zeros_like(sub)
                    for q in range(NL // 8):
                        piece = product[q * 8 : q * 8 + 8, half * 128 : half * 128 + 128]
                        kept = jnp.where(group == float(q), piece, kept)
                    kept = jnp.where(places[2, spot, :] == sub, kept, 0.0)
                    value = jnp.sum(kept, axis=0, keepdims=True)
                    low = value * places[3, spot, :]
                    at = pl.ds(pl.multiple_of(index * tile + half * 128, 128), 128)
                    picked[t : t + 1, at] = low
                    picked[lats + t : lats + t + 1, at] = value - low
            return carry

        lax.fori_loop(first, last, one, 0)

    def waves():
        order = canon((lanes, 128), 0)
        step = lax.broadcasted_iota(jnp.int32, (lanes, 128), 1)
        scale = 2.0 * math.pi / NLON
        for which in range(2):
            speed = order if which == 0 else NL - order
            fine = lax.rem(speed * step, NLON).astype(jnp.float32) * scale
            coarse = lax.rem(speed * step * 128, NLON).astype(jnp.float32) * scale
            fine_cos, fine_sin = jnp.cos(fine), jnp.sin(fine)
            coarse_cos, coarse_sin = jnp.cos(coarse), jnp.sin(coarse)
            for block in range(NLON // 128):
                cos_b = coarse_cos[:, block : block + 1]
                sin_b = coarse_sin[:, block : block + 1]
                if which == 0:
                    value = cos_b * fine_cos - sin_b * fine_sin
                else:
                    value = sin_b * fine_cos + cos_b * fine_sin
                high = value.astype(jnp.bfloat16)
                at = slice(block * 128, block * 128 + 128)
                wave_ref[which, 0, :, at] = high
                wave_ref[which, 1, :, at] = (value - high.astype(jnp.float32)).astype(jnp.bfloat16)

    def transposed_pass(rnd, filler):
        def product(mask):
            both = jnp.dot(left_ref[...], held[mask], preferred_element_type=jnp.float32)
            return both[:COLS] + both[COLS:]

        for mask in far_first:
            if rnd == 0:
                load(mask).wait()
            part[rnd, mask] = product(mask).astype(jnp.bfloat16)
            scatter_copy(rnd, mask).start()
        if rnd == 0:
            load(0).wait()
        total = product(0)
        filler()
        for mask in far_first:
            scatter_copy(rnd, mask).wait_recv()
            total = total + landed[rnd, mask].astype(jnp.float32)
        gathered[rnd, 0] = total.astype(jnp.bfloat16)
        for mask in far_first:
            gather_copy(rnd, mask).start()

    def image_of(rnd, first, second):
        for mask in range(n):
            if mask:
                gather_copy(rnd, mask).wait_recv()
            term = lax.dot_general(
                gathered[rnd, mask],
                held[mask],
                (((1,), (1,)), ((), ())),
                preferred_element_type=jnp.float32,
            )
            acc[...] = term if mask == 0 else acc[...] + term
            if mask == 0:
                first()
        image = acc[...]
        image_sent[rnd] = image.astype(jnp.bfloat16)
        for mask in range(nc - 1, 0, -1):
            image_copy(rnd, mask).start()
        second()
        for mask in range(1, nc):
            image_copy(rnd, mask).wait_recv()
            image = image + image_landed[rnd, mask].astype(jnp.float32)
        return image

    def split(value):
        high = value.astype(jnp.bfloat16).astype(jnp.float32)
        left_ref[...] = jnp.concatenate([high, value - high], axis=0).astype(jnp.bfloat16)

    idle = lambda: None
    pick_step = -(-tiles // 3)
    scatter_fill = [build_hot, waves, idle]
    first_fill = [functools.partial(pick, 0, pick_step), idle]
    second_fill = [
        functools.partial(pick, pick_step, 2 * pick_step),
        functools.partial(pick, 2 * pick_step, tiles),
    ]
    find_places()
    legendre_table()
    pl.semaphore_wait(barrier, n + nc - 2)
    line = lax.broadcasted_iota(jnp.int32, (COLS, 1), 0)
    shift = jnp.zeros((COLS, 1), jnp.float32)
    for right_side in range(COLS):
        shift = jnp.where(line == right_side, shift_table[shift_index[right_side]], shift)
    centre = shift + CENTRE_OFFSET
    ratio_start = centre / HALF_WIDTH
    factor = 1.0 / ratio_start
    residual = obs_ref[...].astype(jnp.float32)
    split(residual)
    transposed_pass(0, scatter_fill[0])
    direction = residual / centre
    answer = direction
    for rnd in range(1, ITERS + 1):
        image = image_of(rnd - 1, first_fill[rnd - 1], second_fill[rnd - 1])
        if rnd == 1:
            image = image / centre
        residual = residual - (image + shift * direction)
        factor_next = 1.0 / (2.0 * ratio_start - factor)
        direction = (factor_next * factor) * direction + (
            2.0 * factor_next / HALF_WIDTH
        ) * residual
        factor = factor_next
        answer = answer + direction
        split(answer if rnd == ITERS else direction)
        transposed_pass(rnd, scatter_fill[rnd])
    for mask in range(n):
        if mask:
            gather_copy(ITERS, mask).wait_recv()
        at = pl.ds(pl.multiple_of(flip(me, mask) * chunk, 128), chunk)
        values = gathered[ITERS, mask].astype(jnp.float32)
        left = jnp.concatenate(
            [values * picked[t : t + 1, at] for t in range(2 * lats)], axis=0
        )
        high = left.astype(jnp.bfloat16).astype(jnp.float32)
        left = jnp.concatenate([high, left - high], axis=0).astype(jnp.bfloat16)
        both = lax.dot_general(
            left, hot[:, at], (((1,), (1,)), ((), ())), preferred_element_type=jnp.float32
        )
        term = both[: 2 * lats * COLS] + both[2 * lats * COLS :]
        sent[...] = term if mask == 0 else sent[...] + term
    for mask in range(nc - 1, 0, -1):
        final_copy(mask).start()
    total = sent[...]
    for mask in range(1, nc):
        final_copy(mask).wait_recv()
        total = total + arrived[mask]
    spectrum[...] = total / math.sqrt(NL)
    side = lats * COLS
    field = jnp.zeros((COLS, NLON), jnp.float32)
    for which in range(2):
        rows = spectrum[pl.ds(pl.multiple_of(which * side + mine * COLS, COLS), COLS), :]
        high = rows.astype(jnp.bfloat16).astype(jnp.float32)
        left = jnp.concatenate([high, rows - high], axis=0).astype(jnp.bfloat16)
        for level in range(2):
            both = jnp.dot(left, wave_ref[which, level], preferred_element_type=jnp.float32)
            field = field + both[:COLS] + both[COLS:]
    field_out[:, 0, :] = field / math.sqrt(NL)
    whole = spectrum[...]
    own = whole[:, :owned]
    for owner in range(1, nc):
        own = jnp.where(mine == owner, whole[:, owner * owned : (owner + 1) * owned], own)
    band[...] = jnp.concatenate([own, jnp.zeros((2 * side, 128 - owned), jnp.float32)], axis=1)
    for which in range(2):
        for column in range(COLS):
            line = band[pl.ds(which * side + column, lats, stride=COLS), :]
            band_out[which, column] = line[:, :owned]
    for rnd in range(ITERS + 1):
        for mask in far_first:
            scatter_copy(rnd, mask).wait_send()
            gather_copy(rnd, mask).wait_send()
        if rnd < ITERS:
            for mask in range(1, nc):
                image_copy(rnd, mask).wait_send()
    for mask in range(1, nc):
        final_copy(mask).wait_send()


def solve(n, nc, observations, design, shift_table, shift_index, order_map, perm):
    rows, kdev = design.shape
    chunk = kdev // n
    rounds = ITERS + 1
    lanes = -(-NL // 128) * 128
    lats = LAT_DEV * nc
    side = 2 * lats * COLS
    blocks = pltpu.VMEM((rounds, n, COLS, chunk), jnp.bfloat16)
    tables = pltpu.VMEM((NL, lanes), jnp.float32)
    return pl.pallas_call(
        functools.partial(solver_kernel, n, nc),
        out_shape=(
            jax.ShapeDtypeStruct((2, COLS, lats, NL // nc), jnp.float32),
            jax.ShapeDtypeStruct((COLS, 1, NLON), jnp.float32),
        ),
        in_specs=[VMEM_SPEC, pl.BlockSpec(memory_space=pl.ANY)]
        + [pl.BlockSpec(memory_space=pltpu.SMEM)] * 3
        + [VMEM_SPEC],
        out_specs=(VMEM_SPEC, VMEM_SPEC),
        scratch_shapes=[pltpu.VMEM((n, rows, chunk), jnp.bfloat16)]
        + [blocks] * 3
        + [
            pltpu.VMEM((ITERS, COLS, rows), jnp.bfloat16),
            pltpu.VMEM((ITERS, nc, COLS, rows), jnp.bfloat16),
            pltpu.VMEM((2 * COLS, rows), jnp.bfloat16),
            pltpu.VMEM((COLS, rows), jnp.float32),
            pltpu.VMEM((4, kdev // 128, 128), jnp.float32),
            pltpu.VMEM((lanes, kdev), jnp.bfloat16),
            pltpu.VMEM((lanes // 128, NL * 8, 128), jnp.float32),
            pltpu.VMEM((lats, NL, lanes), jnp.bfloat16),
            tables,
            tables,
            tables,
            pltpu.VMEM((2 * lats, kdev), jnp.float32),
            pltpu.VMEM((2, 2, lanes, NLON), jnp.bfloat16),
            pltpu.VMEM((side, lanes), jnp.float32),
            pltpu.VMEM((side, 128), jnp.float32),
            pltpu.VMEM((side, lanes), jnp.float32),
            pltpu.VMEM((nc, side, lanes), jnp.float32),
            pltpu.SemaphoreType.DMA((n,)),
        ]
        + [pltpu.SemaphoreType.DMA((rounds, n))] * 4
        + [pltpu.SemaphoreType.DMA((ITERS, nc))] * 2
        + [pltpu.SemaphoreType.DMA((nc,))] * 2,
        compiler_params=pltpu.CompilerParams(
            collective_id=0, has_side_effects=True, vmem_limit_bytes=56 << 20
        ),
        name="solve",
    )(observations, design, shift_table, shift_index, order_map, perm.reshape(-1, 128))


def sum_kernel(n, x_ref, o_ref, landed, send_sem, recv_sem):
    me = lax.axis_index("coef")
    greet("coef", n, me)
    copies = []
    for step in range(1, n):
        copy = push("coef", n, me, step, x_ref, landed.at[step], send_sem, recv_sem)
        copy.start()
        copies.append(copy)
    total = x_ref[...]
    for step in range(1, n):
        copies[step - 1].wait()
        total = total + landed[step]
    o_ref[...] = total.astype(o_ref.dtype)


def coef_sum(partial, n, cid):
    return pl.pallas_call(
        functools.partial(sum_kernel, n),
        out_shape=jax.ShapeDtypeStruct(partial.shape, jnp.bfloat16),
        in_specs=[VMEM_SPEC],
        out_specs=VMEM_SPEC,
        scratch_shapes=[pltpu.VMEM((n,) + partial.shape, jnp.float32)]
        + [pltpu.SemaphoreType.DMA((n,))] * 2,
        compiler_params=pltpu.CompilerParams(collective_id=cid, has_side_effects=True),
        name="coef_sum",
    )(partial)


def solve_plain(nc, observations, design, shift, keep, gain):
    def transposed_pass(left):
        return lax.psum(jnp.dot(left, design, preferred_element_type=jnp.float32), "obs")

    residual = transposed_pass(observations)
    direction = residual / keep[0]
    solution = direction
    for rnd in range(1, ITERS + 1):
        partial_image = lax.dot_general(
            direction.astype(jnp.bfloat16),
            design,
            (((1,), (1,)), ((), ())),
            preferred_element_type=jnp.float32,
        )
        total = transposed_pass(coef_sum(partial_image, nc, 2 + rnd))
        residual = residual - (total + shift * direction)
        direction = keep[rnd] * direction + gain[rnd] * residual
        solution = solution + direction
    return solution.astype(jnp.bfloat16)


def scatter_kernel(n, x_ref, o_ref, landed, send_sem, recv_sem):
    me = lax.axis_index("coef")
    greet("coef", n, me)
    copies = []
    for step in range(1, n):
        target = lax.rem(me + step, n)
        copy = push("coef", n, me, step, x_ref.at[target], landed.at[step], send_sem, recv_sem)
        copy.start()
        copies.append(copy)
    total = x_ref[me].astype(jnp.float32)
    for step in range(1, n):
        copies[step - 1].wait()
        total = total + landed[step].astype(jnp.float32)
    o_ref[...] = total


def coef_scatter(parts, n, cid):
    return pl.pallas_call(
        functools.partial(scatter_kernel, n),
        out_shape=jax.ShapeDtypeStruct(parts.shape[1:], jnp.float32),
        in_specs=[VMEM_SPEC],
        out_specs=VMEM_SPEC,
        scratch_shapes=[pltpu.VMEM(parts.shape, parts.dtype)]
        + [pltpu.SemaphoreType.DMA((n,))] * 2,
        compiler_params=pltpu.CompilerParams(collective_id=cid, has_side_effects=True),
        name="coef_scatter",
    )(parts)


def place_kernel(width, row_ref, col_ref, sol_ref, out_ref, spread):
    out_ref[...] = jnp.zeros_like(out_ref)
    wide = jnp.zeros((COLS, width), jnp.int32)

    def step(index, carry):
        at = pl.ds(pl.multiple_of(index * width, 128), width)
        values = sol_ref[:, at].astype(jnp.float32)
        rows = row_ref[:, at] + wide
        for pair in range(NL // 2):
            first = jnp.where(rows == 2 * pair, values, 0.0)
            second = jnp.where(rows == 2 * pair + 1, values, 0.0)
            both = jnp.concatenate([first, second], axis=0)
            spread[pair * 2 * COLS : (pair + 1) * 2 * COLS, :] = both.astype(jnp.bfloat16)
        degree = lax.broadcasted_iota(jnp.int32, (NL, width), 0)
        hot = jnp.where(degree == col_ref[:, at], 1.0, 0.0).astype(jnp.bfloat16)
        out_ref[...] += lax.dot_general(
            spread[...], hot, (((1,), (1,)), ((), ())), preferred_element_type=jnp.float32
        )
        return carry

    lax.fori_loop(0, sol_ref.shape[1] // width, step, 0)


def place(rows, cols, sol):
    kdev = sol.shape[1]
    width = next(w for w in (512, 384, 256, 128) if kdev % w == 0)
    return pl.pallas_call(
        functools.partial(place_kernel, width),
        out_shape=jax.ShapeDtypeStruct((NL * COLS, NL), jnp.float32),
        in_specs=[VMEM_SPEC] * 3,
        out_specs=VMEM_SPEC,
        scratch_shapes=[pltpu.VMEM((NL * COLS, width), jnp.bfloat16)],
        compiler_params=pltpu.CompilerParams(vmem_limit_bytes=32 << 20),
        name="place",
    )(rows, cols, sol)


def table_of(level, order, valid):
    product = (level - order) * (level + order)
    denom = jnp.where(valid, product, 1.0)
    first = jnp.sqrt(jnp.maximum((2.0 * level - 1.0) * (2.0 * level + 1.0), 0.0) / denom)
    second = jnp.sqrt(
        jnp.maximum((2.0 * level + 1.0) * (level + order - 1.0) * (level - order - 1.0), 0.0)
        / (denom * jnp.maximum(2.0 * level - 3.0, 1.0))
    )
    return jnp.where(valid, first, 0.0), jnp.where(valid, second, 0.0)


def legendre_kernel(
    angle_ref, local_ref, out_ref, a_c, b_c, a_s, b_s, grow, w_ref
):
    lats, lanes = angle_ref.shape[1:]
    w_ref[...] = local_ref[...].T
    order = angle_ref[0, 0:1, :]
    other = float(NL) - order
    count = lax.broadcasted_iota(jnp.int32, (NL, lanes), 0).astype(jnp.float32)
    wide = jnp.zeros((NL, lanes), jnp.float32)
    low = order + wide
    high = other + wide
    level = count + low
    a, b = table_of(level, low, jnp.logical_and(count > 0.0, level < float(NL)))
    a_c[...] = a
    b_c[...] = b
    a, b = table_of(count, high, count > high)
    a_s[...] = a
    b_s[...] = b
    safe = jnp.maximum(count, 1.0)
    grow[...] = jnp.where(
        count == 1.0, math.sqrt(3.0), jnp.sqrt((2.0 * safe + 1.0) / (2.0 * safe))
    )
    cosine = angle_ref[1]
    sine = angle_ref[2]
    zero = cosine * 0.0
    low = angle_ref[0]
    high = float(NL) - low

    def climb(degree, carry):
        diag, dc, ds = carry
        diag = diag * sine * grow[pl.ds(degree, 1), :]
        here = degree.astype(jnp.float32)
        return diag, jnp.where(low == here, diag, dc), jnp.where(high == here, diag, ds)

    start = zero + 1.0
    _, dc, ds = lax.fori_loop(
        1, NL, climb, (start, jnp.where(low == 0.0, start, zero), zero), unroll=4
    )
    acc_c = dc * w_ref[pl.ds(0, 1), :]

    def advance(column, carry):
        pc, ec, ps, es, acc_c, acc_s = carry
        at = pl.ds(column, 1)
        w = w_ref[at, :]
        vc = a_c[at, :] * cosine * pc - b_c[at, :] * ec
        begin = jnp.where(high == column.astype(jnp.float32), ds, 0.0)
        vs = a_s[at, :] * cosine * ps - b_s[at, :] * es + begin
        return vc, pc, vs, ps, acc_c + vc * w, acc_s + vs * w

    _, _, _, _, acc_c, acc_s = lax.fori_loop(
        1, NL, advance, (dc, zero, zero, zero, acc_c, zero), unroll=4
    )
    out_ref[0] = acc_c / math.sqrt(NL)
    out_ref[1] = acc_s / math.sqrt(NL)


def legendre(orders, colatitude, w):
    lanes = w.shape[0]
    lats = colatitude.shape[0]
    which = lax.broadcasted_iota(jnp.int32, (3, lats, lanes), 0)
    angles = jnp.where(
        which == 0,
        orders[None, None, :],
        jnp.where(which == 1, jnp.cos(colatitude)[:, None], jnp.sin(colatitude)[:, None]),
    )
    table = pltpu.VMEM((NL, lanes), jnp.float32)
    return pl.pallas_call(
        legendre_kernel,
        out_shape=jax.ShapeDtypeStruct((2, lats, lanes), jnp.float32),
        in_specs=[VMEM_SPEC] * 2,
        out_specs=VMEM_SPEC,
        scratch_shapes=[table] * 6,
        name="legendre",
    )(
        angles,
        w,
    )


def wave_tables(rows, longitudes):
    steps_k = jnp.arange(longitudes, dtype=jnp.int32)
    scale = 2.0 * math.pi / longitudes
    cos_angle = (rows[:, None] * steps_k[None, :] % longitudes).astype(jnp.float32) * scale
    sin_angle = ((NL - rows)[:, None] * steps_k[None, :] % longitudes).astype(jnp.float32) * scale
    return (jnp.cos(cos_angle), jnp.sin(sin_angle))


def body(design, observations, shift_table, shift_index, coef_perm, order_map):
    obs_count = lax.axis_size("obs")
    coef_count = lax.axis_size("coef")
    coef_rank = lax.axis_index("coef")
    obs_rank = lax.axis_index("obs")
    kdev = design.shape[1]
    chunk = kdev // obs_count
    paired_up = all(c & (c - 1) == 0 for c in (obs_count, coef_count))
    direct = (
        chunk % 128 == 0
        and kdev % 256 == 0
        and paired_up
        and LAT_DEV * coef_count <= 8
        and NL // coef_count <= 128
    )
    if direct:
        band, field = solve(
            obs_count, coef_count, observations, design, shift_table, shift_index, order_map,
            coef_perm,
        )
        return (band.transpose(3, 0, 1, 2), field)
    table_index = jnp.arange(NSHIFT, dtype=jnp.int32)
    shifts = jnp.sum(
        jnp.where(shift_index[:, None] == table_index[None, :], shift_table[None, :], 0.0), axis=1
    )
    centre = shifts + CENTRE_OFFSET
    ratio_start = centre / HALF_WIDTH

    keep = [centre]
    gain = [centre]
    factor = 1.0 / ratio_start
    for iteration in range(ITERS):
        factor_next = 1.0 / (2.0 * ratio_start - factor)
        keep.append(factor_next * factor)
        gain.append(2.0 * factor_next / HALF_WIDTH)
        factor = factor_next
    keep = jnp.stack(keep)[:, :, None]
    gain = jnp.stack(gain)[:, :, None]
    block_count = coef_count * BPO
    block_rows = NL // block_count
    owned_rows = kdev // NL
    block_ids = jnp.arange(block_count, dtype=jnp.int32)
    position = jnp.sum(
        jnp.where(order_map[:, None] == block_ids[None, :], block_ids[:, None], 0), axis=0
    )
    paired_row = coef_perm // NL
    column = coef_perm % NL
    place_of = jnp.sum(
        jnp.where(
            (paired_row // block_rows)[None, :] == block_ids[:, None], position[:, None], 0
        ),
        axis=0,
    )
    owner_row = place_of * block_rows + paired_row % block_rows
    full = solve_plain(coef_count, observations, design, shifts[:, None], keep, gain)
    lanes = owned_rows * COLS
    placed = place(owner_row[None, :], column[None, :], full)
    outgoing = placed.astype(jnp.bfloat16).reshape(coef_count, lanes, NL)
    local = coef_scatter(outgoing, coef_count, 5)
    my_blocks = lax.dynamic_slice_in_dim(order_map, coef_rank * BPO, BPO)
    row_offsets = jnp.arange(block_rows, dtype=jnp.int32)
    owned_canon = (my_blocks[:, None] * block_rows + row_offsets[None, :]).reshape(owned_rows)
    lat_block = LAT_DEV * coef_count
    lat_total = lat_block * obs_count
    lat_ids = obs_rank * lat_block + jnp.arange(lat_block, dtype=jnp.int32)
    colatitude = math.pi * (lat_ids.astype(jnp.float32) + 0.5) / lat_total
    orders = jnp.repeat(owned_canon, COLS).astype(jnp.float32)
    parts = legendre(orders, colatitude, local).reshape(2, lat_block, owned_rows, COLS)
    band = parts.transpose(2, 0, 3, 1)
    own_cos, own_sin = wave_tables(owned_canon, NLON)
    first_sum = jnp.einsum("lqc,qk->lck", parts[0], own_cos, precision=lax.Precision.HIGHEST)
    second_sum = jnp.einsum("lqc,qk->lck", parts[1], own_sin, precision=lax.Precision.HIGHEST)
    shares = ((first_sum + second_sum) / math.sqrt(NL)).reshape(
        coef_count, LAT_DEV * COLS, NLON
    )
    field = coef_scatter(shares, coef_count, 6).reshape(LAT_DEV, COLS, NLON).transpose(1, 0, 2)
    return (band, field)


def solution(mesh):
    placed = (P("obs", "coef"), P(None, "obs"), P(), P(), P("coef"), P())
    return jax.shard_map(
        body,
        mesh=mesh,
        in_specs=placed,
        out_specs=(P("coef", None, None, "obs"), P(None, ("obs", "coef"), None)),
        check_vma=False,
    )
```

```python
import functools
import math

import jax
import jax.numpy as jnp
from jax import lax
from jax.experimental import pallas as pl
from jax.experimental.pallas import tpu as pltpu
from jax.sharding import PartitionSpec as P

NL = 192
COLS = 8
ITERS = 2
NSHIFT = 16
BPO = 2
NLON = 1024
LAT_DEV = 1

CENTRE_OFFSET = 1.25
HALF_WIDTH = 0.95
VMEM_SPEC = pl.BlockSpec(memory_space=pltpu.VMEM)
MESH = pl.DeviceIdType.MESH


def greet(axis, n, me):
    barrier = pltpu.get_barrier_semaphore()
    for step in range(1, n):
        pl.semaphore_signal(
            barrier, inc=1, device_id={axis: lax.rem(me + step, n)}, device_id_type=MESH
        )
    pl.semaphore_wait(barrier, n - 1)


def push(axis, n, me, step, src, dst, send_sem, recv_sem):
    return pltpu.make_async_remote_copy(
        src_ref=src,
        dst_ref=dst,
        send_sem=send_sem.at[step],
        recv_sem=recv_sem.at[step],
        device_id={axis: lax.rem(me + step, n)},
        device_id_type=MESH,
    )


def flip(index, mask):
    other = index
    bit = 1
    while bit <= mask:
        if mask & bit:
            other = other + bit - 2 * bit * (index // bit % 2)
        bit *= 2
    return other


def swap(axis, rank, mask, src, dst, send_sem, recv_sem):
    return pltpu.make_async_remote_copy(
        src_ref=src,
        dst_ref=dst,
        send_sem=send_sem.at[mask],
        recv_sem=recv_sem.at[mask],
        device_id={axis: flip(rank, mask)},
        device_id_type=MESH,
    )


def solver_kernel(
    n, nc, obs_hbm, design_ref, shift_hbm, index_hbm, map_hbm, perm_hbm,
    band_out, field_out,
    held, part, landed, gathered, image_sent, image_landed, left_ref, acc,
    obs_ref, shift_table, shift_index, map_ref, perm_ref, turned, places, hot, raw, table, a_tab, b_tab, grow, picked, wave_ref, sent, rows_sent, rows_here, lats_sent, lats_here,
    small_sem, load_sem, send_a, recv_a, send_b, recv_b, send_c, recv_c, send_d, recv_d,
    send_e, recv_e,
):
    me = lax.axis_index("obs")
    mine = lax.axis_index("coef")
    chunk = held.shape[2]
    lanes = hot.shape[0]
    lats = LAT_DEV * nc
    owned = NL // nc
    far_first = list(range(n - 1, 0, -1))

    def load(mask):
        return pltpu.make_async_copy(
            design_ref.at[:, pl.ds(pl.multiple_of(flip(me, mask) * chunk, 128), chunk)],
            held.at[mask],
            load_sem.at[mask],
        )

    small = [
        pltpu.make_async_copy(source, target, small_sem.at[spot])
        for spot, (source, target) in enumerate(
            (
                (map_hbm, map_ref),
                (perm_hbm, perm_ref),
                (obs_hbm, obs_ref),
                (shift_hbm, shift_table),
                (index_hbm, shift_index),
            )
        )
    ]
    for copy in small:
        copy.start()
    for mask in far_first + [0]:
        load(mask).start()
    barrier = pltpu.get_barrier_semaphore()
    for axis, count, rank in (("obs", n, me), ("coef", nc, mine)):
        for mask in range(1, count):
            pl.semaphore_signal(
                barrier, inc=1, device_id={axis: flip(rank, mask)}, device_id_type=MESH
            )

    def scatter_copy(rnd, mask):
        return swap(
            "obs", me, mask, part.at[rnd, mask], landed.at[rnd, mask], send_a.at[rnd], recv_a.at[rnd]
        )

    def gather_copy(rnd, mask):
        return swap(
            "obs", me, mask, gathered.at[rnd, 0], gathered.at[rnd, mask],
            send_b.at[rnd], recv_b.at[rnd],
        )

    def image_copy(rnd, mask):
        return swap(
            "coef", mine, mask, image_sent.at[rnd], image_landed.at[rnd, mask],
            send_c.at[rnd], recv_c.at[rnd],
        )

    def final_copies(mask):
        target = flip(mine, mask)
        return [
            swap("coef", mine, mask, rows_sent.at[target], rows_here.at[mask], send_d, recv_d),
            swap("coef", mine, mask, lats_sent.at[target], lats_here.at[mask], send_e, recv_e),
        ]

    def canon(shape, axis):
        lane = lax.broadcasted_iota(jnp.int32, shape, axis)
        blocks = nc * BPO
        size = NL // blocks
        total = jnp.zeros(shape, jnp.int32)
        for block in range(blocks):
            inside = jnp.logical_and(lane >= block * size, lane < (block + 1) * size)
            total = jnp.where(inside, lane + (map_ref[block] - block) * size, total)
        return total

    def legendre_table():
        order = canon((8, lanes), 1).astype(jnp.float32)
        other = float(NL) - order
        count = lax.broadcasted_iota(jnp.int32, (NL, lanes), 0).astype(jnp.float32)
        low = order[0:1, :] + jnp.zeros((NL, lanes), jnp.float32)
        high = float(NL) - low
        cosine_part = count < high
        level = jnp.where(cosine_part, count + low, count)
        degree_order = jnp.where(cosine_part, low, high)
        valid = jnp.logical_and(count != high, count > 0.0)
        a, b = table_of(level, degree_order, valid)
        a_tab[...] = a
        b_tab[...] = b
        safe = jnp.maximum(count, 1.0)
        grow[...] = jnp.where(
            count == 1.0, math.sqrt(3.0), jnp.sqrt((2.0 * safe + 1.0) / (2.0 * safe))
        )
        lat = lax.broadcasted_iota(jnp.int32, (8, lanes), 0) + me * lats
        colatitude = math.pi * (lat.astype(jnp.float32) + 0.5) / (lats * n)
        cosine = jnp.cos(colatitude)
        sine = jnp.sin(colatitude)

        def climb(degree, carry):
            diag, dc, ds = carry
            diag = diag * (sine * grow[pl.ds(degree, 1), :])
            here = degree.astype(jnp.float32)
            return diag, jnp.where(order == here, diag, dc), jnp.where(other == here, diag, ds)

        start = jnp.ones((8, lanes), jnp.float32)
        zero = jnp.zeros((8, lanes), jnp.float32)
        _, dc, ds = lax.fori_loop(
            1, NL, climb, (start, jnp.where(order == 0.0, start, zero), zero), unroll=8
        )
        def keep_row(column, value):
            for half in range(lanes // 128):
                raw[half, pl.ds(pl.multiple_of(column * 8, 8), 8), :] = value[
                    :, half * 128 : (half + 1) * 128
                ]

        keep_row(0, dc)

        def advance(column, carry):
            now, before = carry
            at = pl.ds(column, 1)
            begin = jnp.where(other == column.astype(jnp.float32), ds, 0.0)
            value = (a_tab[at, :] * cosine) * now - (b_tab[at, :] * before - begin)
            keep_row(column, value)
            return value, now

        lax.fori_loop(1, NL, advance, (dc, zero), unroll=8)
        for t in range(lats):
            for half in range(lanes // 128):
                table[t * NL : (t + 1) * NL, half * 128 : (half + 1) * 128] = raw[
                    half, pl.ds(t, NL, stride=8), :
                ].astype(jnp.bfloat16)

    tile = 256
    tiles = hot.shape[1] // tile

    def find_places():
        index = perm_ref[...].astype(jnp.float32)
        paired = jnp.floor((index + 0.5) * (1.0 / NL))
        column = index - paired * NL
        blocks = nc * BPO
        size = NL // blocks
        block = jnp.floor((paired + 0.5) * (1.0 / size))
        inside = paired - block * size
        row = jnp.zeros_like(index)
        for spot in range(blocks):
            here = block == map_ref[spot].astype(jnp.float32)
            row = jnp.where(here, inside + spot * size, row)
        places[0] = row
        group = jnp.floor((column + 0.5) * 0.125)
        places[1] = group
        places[2] = column - group * 8.0
        places[3] = jnp.where(paired + column < NL, 1.0, 0.0)

    def build_hot():
        def one(index, carry):
            at = pl.ds(pl.multiple_of(index * 128, 128), 128)
            row = lax.broadcasted_iota(jnp.int32, (lanes, 128), 0).astype(jnp.bfloat16)
            same = row == places[0, pl.ds(index, 1), :].astype(jnp.bfloat16)
            hot[:, at] = jnp.where(same, jnp.bfloat16(1.0), jnp.bfloat16(0.0))
            return carry

        lax.fori_loop(0, tiles * (tile // 128), one, 0, unroll=4)

    def pick(first, last):
        def one(index, carry):
            wide = pl.ds(pl.multiple_of(index * tile, 128), tile)
            sub = lax.broadcasted_iota(jnp.int32, (8, 128), 0).astype(jnp.float32)
            product = jnp.dot(table[...], hot[:, wide], preferred_element_type=jnp.float32)
            for half in range(tile // 128):
                spot = pl.ds(index * (tile // 128) + half, 1)
                group = places[1, spot, :] + jnp.zeros_like(sub)
                inner = places[2, spot, :] == sub
                early = places[3, spot, :]
                kept = [jnp.zeros_like(sub)] * lats
                for q in range(NL // 8):
                    here = group == float(q)
                    for t in range(lats):
                        first_row = t * NL + q * 8
                        piece = product[first_row : first_row + 8, half * 128 : half * 128 + 128]
                        kept[t] = jnp.where(here, piece, kept[t])
                at = pl.ds(pl.multiple_of(index * tile + half * 128, 128), 128)
                for t in range(lats):
                    value = jnp.sum(jnp.where(inner, kept[t], 0.0), axis=0, keepdims=True)
                    low = value * early
                    picked[t : t + 1, at] = low
                    picked[lats + t : lats + t + 1, at] = value - low
            return carry

        lax.fori_loop(first, last, one, 0, unroll=last - first)

    def waves():
        order = canon((lanes, 128), 0)
        step = lax.broadcasted_iota(jnp.int32, (lanes, 128), 1)
        scale = 2.0 * math.pi / NLON
        for which in range(2):
            speed = order if which == 0 else NL - order
            fine = lax.rem(speed * step, NLON).astype(jnp.float32) * scale
            coarse = lax.rem(speed * step * 128, NLON).astype(jnp.float32) * scale
            fine_cos, fine_sin = jnp.cos(fine), jnp.sin(fine)
            coarse_cos, coarse_sin = jnp.cos(coarse), jnp.sin(coarse)
            for block in range(NLON // 128):
                cos_b = coarse_cos[:, block : block + 1]
                sin_b = coarse_sin[:, block : block + 1]
                if which == 0:
                    value = cos_b * fine_cos - sin_b * fine_sin
                else:
                    value = sin_b * fine_cos + cos_b * fine_sin
                high = value.astype(jnp.bfloat16)
                at = slice(block * 128, block * 128 + 128)
                wave_ref[which, 0, :, at] = high
                wave_ref[which, 1, :, at] = (value - high.astype(jnp.float32)).astype(jnp.bfloat16)

    def turn():
        for mask in far_first[: n // 2]:
            turned[mask - n // 2] = held[mask].T

    def transposed_pass(rnd, filler):
        def product(mask):
            both = jnp.dot(left_ref[...], held[mask], preferred_element_type=jnp.float32)
            return both[:COLS] + both[COLS:]

        for mask in far_first:
            if rnd == 0:
                load(mask).wait()
            part[rnd, mask] = product(mask).astype(jnp.bfloat16)
            scatter_copy(rnd, mask).start()
        if rnd == 0:
            load(0).wait()
        total = product(0)
        filler()
        for mask in far_first:
            scatter_copy(rnd, mask).wait_recv()
            total = total + landed[rnd, mask].astype(jnp.float32)
        gathered[rnd, 0] = total.astype(jnp.bfloat16)
        for mask in far_first:
            gather_copy(rnd, mask).start()

    def image_of(rnd, first, second):
        for mask in range(n):
            if mask:
                gather_copy(rnd, mask).wait_recv()
            block = gathered[rnd, mask]
            if mask >= n // 2:
                term = jnp.dot(block, turned[mask - n // 2], preferred_element_type=jnp.float32)
            else:
                term = lax.dot_general(
                    block, held[mask], (((1,), (1,)), ((), ())), preferred_element_type=jnp.float32
                )
            acc[...] = term if mask == 0 else acc[...] + term
            if mask == 0:
                first()
        image = acc[...]
        image_sent[rnd] = image.astype(jnp.bfloat16)
        for mask in range(nc - 1, 0, -1):
            image_copy(rnd, mask).start()
        second()
        for mask in range(1, nc):
            image_copy(rnd, mask).wait_recv()
            image = image + image_landed[rnd, mask].astype(jnp.float32)
        return image

    def split(value):
        high = value.astype(jnp.bfloat16).astype(jnp.float32)
        left_ref[...] = jnp.concatenate([high, value - high], axis=0).astype(jnp.bfloat16)

    share = [functools.partial(pick, i * tiles // 6, (i + 1) * tiles // 6) for i in range(6)]
    scatter_fill = [turn, lambda: (share[0](), share[1](), share[2]()), share[5]]
    first_fill = [legendre_table, share[3]]
    second_fill = [build_hot, share[4]]
    for copy in small:
        copy.wait()
    find_places()
    pl.semaphore_wait(barrier, n + nc - 2)
    line = lax.broadcasted_iota(jnp.int32, (COLS, 1), 0)
    shift = jnp.zeros((COLS, 1), jnp.float32)
    for right_side in range(COLS):
        shift = jnp.where(line == right_side, shift_table[shift_index[right_side]], shift)
    centre = shift + CENTRE_OFFSET
    ratio_start = centre / HALF_WIDTH
    factor = 1.0 / ratio_start
    residual = obs_ref[...].astype(jnp.float32)
    split(residual)
    transposed_pass(0, scatter_fill[0])
    direction = residual / centre
    answer = direction
    for rnd in range(1, ITERS + 1):
        image = image_of(rnd - 1, first_fill[rnd - 1], second_fill[rnd - 1])
        if rnd == 1:
            image = image / centre
        residual = residual - (image + shift * direction)
        factor_next = 1.0 / (2.0 * ratio_start - factor)
        direction = (factor_next * factor) * direction + (
            2.0 * factor_next / HALF_WIDTH
        ) * residual
        factor = factor_next
        answer = answer + direction
        split(answer if rnd == ITERS else direction)
        transposed_pass(rnd, scatter_fill[rnd])
    for mask in range(n):
        if mask:
            gather_copy(ITERS, mask).wait_recv()
        at = pl.ds(pl.multiple_of(flip(me, mask) * chunk, 128), chunk)
        values = gathered[ITERS, mask].astype(jnp.float32)
        left = jnp.concatenate(
            [values * picked[t : t + 1, at] for t in range(2 * lats)], axis=0
        )
        high = left.astype(jnp.bfloat16).astype(jnp.float32)
        left = jnp.concatenate([high, left - high], axis=0).astype(jnp.bfloat16)
        both = lax.dot_general(
            left, hot[:, at], (((1,), (1,)), ((), ())), preferred_element_type=jnp.float32
        )
        term = both[: 2 * lats * COLS] + both[2 * lats * COLS :]
        sent[...] = term if mask == 0 else sent[...] + term
    side = lats * COLS
    total = sent[...]
    blank = jnp.zeros((side, rows_sent.shape[2] - 2 * owned), jnp.float32)
    for owner in range(nc):
        block = total[:, owner * owned : (owner + 1) * owned]
        rows_sent[owner] = jnp.concatenate([block[:side], block[side:], blank], axis=1)
        for which in range(2):
            first = which * side + owner * COLS
            lats_sent[owner, which] = total[first : first + COLS]
    for mask in range(nc - 1, 0, -1):
        for copy in final_copies(mask):
            copy.start()
    waves()
    own = rows_sent[mine]
    waved = lats_sent[mine]
    for mask in range(1, nc):
        for copy in final_copies(mask):
            copy.wait_recv()
        own = own + rows_here[mask]
        waved = waved + lats_here[mask]
    own = own / math.sqrt(NL)
    waved = waved / math.sqrt(NL)
    field = jnp.zeros((COLS, NLON), jnp.float32)
    for which in range(2):
        rows = waved[which]
        high = rows.astype(jnp.bfloat16).astype(jnp.float32)
        left = jnp.concatenate([high, rows - high], axis=0).astype(jnp.bfloat16)
        for level in range(2):
            both = jnp.dot(left, wave_ref[which, level], preferred_element_type=jnp.float32)
            field = field + both[:COLS] + both[COLS:]
    field_out[...] = field / math.sqrt(NL)
    band_out[...] = own
    for rnd in range(ITERS + 1):
        for mask in far_first:
            scatter_copy(rnd, mask).wait_send()
            gather_copy(rnd, mask).wait_send()
        if rnd < ITERS:
            for mask in range(1, nc):
                image_copy(rnd, mask).wait_send()
    for mask in range(1, nc):
        for copy in final_copies(mask):
            copy.wait_send()


def arrange_kernel(band_ref, field_ref, band_out, field_out):
    owned = band_out.shape[3]
    lats = band_out.shape[2]
    field_out[:, 0, :] = field_ref[...]
    for column in range(COLS):
        line = band_ref[pl.ds(column, lats, stride=COLS), :]
        for which in range(2):
            band_out[which, column] = line[:, which * owned : (which + 1) * owned]


def arrange(band, field, owned):
    return pl.pallas_call(
        arrange_kernel,
        out_shape=(
            jax.ShapeDtypeStruct((2, COLS, band.shape[0] // COLS, owned), jnp.float32),
            jax.ShapeDtypeStruct((COLS, 1, NLON), jnp.float32),
        ),
        in_specs=[VMEM_SPEC] * 2,
        out_specs=(VMEM_SPEC,) * 2,
        name="arrange",
    )(band, field)


def solve(n, nc, observations, design, shift_table, shift_index, order_map, perm):
    rows, kdev = design.shape
    chunk = kdev // n
    rounds = ITERS + 1
    lanes = -(-NL // 128) * 128
    lats = LAT_DEV * nc
    side = 2 * lats * COLS
    blocks = pltpu.VMEM((rounds, n, COLS, chunk), jnp.bfloat16)
    tables = pltpu.VMEM((NL, lanes), jnp.float32)
    return pl.pallas_call(
        functools.partial(solver_kernel, n, nc),
        out_shape=(
            jax.ShapeDtypeStruct((side // 2, 128), jnp.float32),
            jax.ShapeDtypeStruct((COLS, NLON), jnp.float32),
        ),
        in_specs=[pl.BlockSpec(memory_space=pltpu.HBM)] * 6,
        out_specs=(VMEM_SPEC, VMEM_SPEC),
        scratch_shapes=[pltpu.VMEM((n, rows, chunk), jnp.bfloat16)]
        + [blocks] * 3
        + [
            pltpu.VMEM((ITERS, COLS, rows), jnp.bfloat16),
            pltpu.VMEM((ITERS, nc, COLS, rows), jnp.bfloat16),
            pltpu.VMEM((2 * COLS, rows), jnp.bfloat16),
            pltpu.VMEM((COLS, rows), jnp.float32),
            pltpu.VMEM(observations.shape, observations.dtype),
            pltpu.SMEM(shift_table.shape, jnp.float32),
            pltpu.SMEM(shift_index.shape, jnp.int32),
            pltpu.SMEM(order_map.shape, jnp.int32),
            pltpu.VMEM((kdev // 128, 128), jnp.int32),
            pltpu.VMEM((n // 2, chunk, rows), jnp.bfloat16),
            pltpu.VMEM((4, kdev // 128, 128), jnp.float32),
            pltpu.VMEM((lanes, kdev), jnp.bfloat16),
            pltpu.VMEM((lanes // 128, NL * 8, 128), jnp.float32),
            pltpu.VMEM((lats * NL, lanes), jnp.bfloat16),
            tables,
            tables,
            tables,
            pltpu.VMEM((2 * lats, kdev), jnp.float32),
            pltpu.VMEM((2, 2, lanes, NLON), jnp.bfloat16),
            pltpu.VMEM((side, lanes), jnp.float32),
        ]
        + [pltpu.VMEM((nc, side // 2, 128), jnp.float32)] * 2
        + [pltpu.VMEM((nc, 2, COLS, lanes), jnp.float32)] * 2
        + [
            pltpu.SemaphoreType.DMA((5,)),
            pltpu.SemaphoreType.DMA((n,)),
        ]
        + [pltpu.SemaphoreType.DMA((rounds, n))] * 4
        + [pltpu.SemaphoreType.DMA((ITERS, nc))] * 2
        + [pltpu.SemaphoreType.DMA((nc,))] * 4,
        compiler_params=pltpu.CompilerParams(
            collective_id=0, has_side_effects=True, vmem_limit_bytes=56 << 20
        ),
        name="solve",
    )(observations, design, shift_table, shift_index, order_map, perm.reshape(-1, 128))


def sum_kernel(n, x_ref, o_ref, landed, send_sem, recv_sem):
    me = lax.axis_index("coef")
    greet("coef", n, me)
    copies = []
    for step in range(1, n):
        copy = push("coef", n, me, step, x_ref, landed.at[step], send_sem, recv_sem)
        copy.start()
        copies.append(copy)
    total = x_ref[...]
    for step in range(1, n):
        copies[step - 1].wait()
        total = total + landed[step]
    o_ref[...] = total.astype(o_ref.dtype)


def coef_sum(partial, n, cid):
    return pl.pallas_call(
        functools.partial(sum_kernel, n),
        out_shape=jax.ShapeDtypeStruct(partial.shape, jnp.bfloat16),
        in_specs=[VMEM_SPEC],
        out_specs=VMEM_SPEC,
        scratch_shapes=[pltpu.VMEM((n,) + partial.shape, jnp.float32)]
        + [pltpu.SemaphoreType.DMA((n,))] * 2,
        compiler_params=pltpu.CompilerParams(collective_id=cid, has_side_effects=True),
        name="coef_sum",
    )(partial)


def solve_plain(nc, observations, design, shift, keep, gain):
    def transposed_pass(left):
        return lax.psum(jnp.dot(left, design, preferred_element_type=jnp.float32), "obs")

    residual = transposed_pass(observations)
    direction = residual / keep[0]
    solution = direction
    for rnd in range(1, ITERS + 1):
        partial_image = lax.dot_general(
            direction.astype(jnp.bfloat16),
            design,
            (((1,), (1,)), ((), ())),
            preferred_element_type=jnp.float32,
        )
        total = transposed_pass(coef_sum(partial_image, nc, 2 + rnd))
        residual = residual - (total + shift * direction)
        direction = keep[rnd] * direction + gain[rnd] * residual
        solution = solution + direction
    return solution.astype(jnp.bfloat16)


def scatter_kernel(n, x_ref, o_ref, landed, send_sem, recv_sem):
    me = lax.axis_index("coef")
    greet("coef", n, me)
    copies = []
    for step in range(1, n):
        target = lax.rem(me + step, n)
        copy = push("coef", n, me, step, x_ref.at[target], landed.at[step], send_sem, recv_sem)
        copy.start()
        copies.append(copy)
    total = x_ref[me].astype(jnp.float32)
    for step in range(1, n):
        copies[step - 1].wait()
        total = total + landed[step].astype(jnp.float32)
    o_ref[...] = total


def coef_scatter(parts, n, cid):
    return pl.pallas_call(
        functools.partial(scatter_kernel, n),
        out_shape=jax.ShapeDtypeStruct(parts.shape[1:], jnp.float32),
        in_specs=[VMEM_SPEC],
        out_specs=VMEM_SPEC,
        scratch_shapes=[pltpu.VMEM(parts.shape, parts.dtype)]
        + [pltpu.SemaphoreType.DMA((n,))] * 2,
        compiler_params=pltpu.CompilerParams(collective_id=cid, has_side_effects=True),
        name="coef_scatter",
    )(parts)


def place_kernel(width, row_ref, col_ref, sol_ref, out_ref, spread):
    out_ref[...] = jnp.zeros_like(out_ref)
    wide = jnp.zeros((COLS, width), jnp.int32)

    def step(index, carry):
        at = pl.ds(pl.multiple_of(index * width, 128), width)
        values = sol_ref[:, at].astype(jnp.float32)
        rows = row_ref[:, at] + wide
        for pair in range(NL // 2):
            first = jnp.where(rows == 2 * pair, values, 0.0)
            second = jnp.where(rows == 2 * pair + 1, values, 0.0)
            both = jnp.concatenate([first, second], axis=0)
            spread[pair * 2 * COLS : (pair + 1) * 2 * COLS, :] = both.astype(jnp.bfloat16)
        degree = lax.broadcasted_iota(jnp.int32, (NL, width), 0)
        hot = jnp.where(degree == col_ref[:, at], 1.0, 0.0).astype(jnp.bfloat16)
        out_ref[...] += lax.dot_general(
            spread[...], hot, (((1,), (1,)), ((), ())), preferred_element_type=jnp.float32
        )
        return carry

    lax.fori_loop(0, sol_ref.shape[1] // width, step, 0)


def place(rows, cols, sol):
    kdev = sol.shape[1]
    width = next(w for w in (512, 384, 256, 128) if kdev % w == 0)
    return pl.pallas_call(
        functools.partial(place_kernel, width),
        out_shape=jax.ShapeDtypeStruct((NL * COLS, NL), jnp.float32),
        in_specs=[VMEM_SPEC] * 3,
        out_specs=VMEM_SPEC,
        scratch_shapes=[pltpu.VMEM((NL * COLS, width), jnp.bfloat16)],
        compiler_params=pltpu.CompilerParams(vmem_limit_bytes=32 << 20),
        name="place",
    )(rows, cols, sol)


def table_of(level, order, valid):
    product = (level - order) * (level + order)
    denom = jnp.where(valid, product, 1.0)
    first = jnp.sqrt(jnp.maximum((2.0 * level - 1.0) * (2.0 * level + 1.0), 0.0) / denom)
    second = jnp.sqrt(
        jnp.maximum((2.0 * level + 1.0) * (level + order - 1.0) * (level - order - 1.0), 0.0)
        / (denom * jnp.maximum(2.0 * level - 3.0, 1.0))
    )
    return jnp.where(valid, first, 0.0), jnp.where(valid, second, 0.0)


def legendre_kernel(
    angle_ref, local_ref, out_ref, a_c, b_c, a_s, b_s, grow, w_ref
):
    lats, lanes = angle_ref.shape[1:]
    w_ref[...] = local_ref[...].T
    order = angle_ref[0, 0:1, :]
    other = float(NL) - order
    count = lax.broadcasted_iota(jnp.int32, (NL, lanes), 0).astype(jnp.float32)
    wide = jnp.zeros((NL, lanes), jnp.float32)
    low = order + wide
    high = other + wide
    level = count + low
    a, b = table_of(level, low, jnp.logical_and(count > 0.0, level < float(NL)))
    a_c[...] = a
    b_c[...] = b
    a, b = table_of(count, high, count > high)
    a_s[...] = a
    b_s[...] = b
    safe = jnp.maximum(count, 1.0)
    grow[...] = jnp.where(
        count == 1.0, math.sqrt(3.0), jnp.sqrt((2.0 * safe + 1.0) / (2.0 * safe))
    )
    cosine = angle_ref[1]
    sine = angle_ref[2]
    zero = cosine * 0.0
    low = angle_ref[0]
    high = float(NL) - low

    def climb(degree, carry):
        diag, dc, ds = carry
        diag = diag * sine * grow[pl.ds(degree, 1), :]
        here = degree.astype(jnp.float32)
        return diag, jnp.where(low == here, diag, dc), jnp.where(high == here, diag, ds)

    start = zero + 1.0
    _, dc, ds = lax.fori_loop(
        1, NL, climb, (start, jnp.where(low == 0.0, start, zero), zero), unroll=4
    )
    acc_c = dc * w_ref[pl.ds(0, 1), :]

    def advance(column, carry):
        pc, ec, ps, es, acc_c, acc_s = carry
        at = pl.ds(column, 1)
        w = w_ref[at, :]
        vc = a_c[at, :] * cosine * pc - b_c[at, :] * ec
        begin = jnp.where(high == column.astype(jnp.float32), ds, 0.0)
        vs = a_s[at, :] * cosine * ps - b_s[at, :] * es + begin
        return vc, pc, vs, ps, acc_c + vc * w, acc_s + vs * w

    _, _, _, _, acc_c, acc_s = lax.fori_loop(
        1, NL, advance, (dc, zero, zero, zero, acc_c, zero), unroll=4
    )
    out_ref[0] = acc_c / math.sqrt(NL)
    out_ref[1] = acc_s / math.sqrt(NL)


def legendre(orders, colatitude, w):
    lanes = w.shape[0]
    lats = colatitude.shape[0]
    which = lax.broadcasted_iota(jnp.int32, (3, lats, lanes), 0)
    angles = jnp.where(
        which == 0,
        orders[None, None, :],
        jnp.where(which == 1, jnp.cos(colatitude)[:, None], jnp.sin(colatitude)[:, None]),
    )
    table = pltpu.VMEM((NL, lanes), jnp.float32)
    return pl.pallas_call(
        legendre_kernel,
        out_shape=jax.ShapeDtypeStruct((2, lats, lanes), jnp.float32),
        in_specs=[VMEM_SPEC] * 2,
        out_specs=VMEM_SPEC,
        scratch_shapes=[table] * 6,
        name="legendre",
    )(
        angles,
        w,
    )


def wave_tables(rows, longitudes):
    steps_k = jnp.arange(longitudes, dtype=jnp.int32)
    scale = 2.0 * math.pi / longitudes
    cos_angle = (rows[:, None] * steps_k[None, :] % longitudes).astype(jnp.float32) * scale
    sin_angle = ((NL - rows)[:, None] * steps_k[None, :] % longitudes).astype(jnp.float32) * scale
    return (jnp.cos(cos_angle), jnp.sin(sin_angle))


def body(design, observations, shift_table, shift_index, coef_perm, order_map):
    obs_count = lax.axis_size("obs")
    coef_count = lax.axis_size("coef")
    coef_rank = lax.axis_index("coef")
    obs_rank = lax.axis_index("obs")
    kdev = design.shape[1]
    chunk = kdev // obs_count
    paired_up = all(c & (c - 1) == 0 for c in (obs_count, coef_count))
    direct = (
        chunk % 128 == 0
        and kdev % 256 == 0
        and paired_up
        and LAT_DEV * coef_count <= 8
        and 2 * NL // coef_count <= 128
        and NL <= 256
    )
    if direct:
        band, field = solve(
            obs_count, coef_count, observations, design, shift_table, shift_index, order_map,
            coef_perm,
        )
        band, field = arrange(band, field, NL // coef_count)
        return (band.transpose(3, 0, 1, 2), field)
    table_index = jnp.arange(NSHIFT, dtype=jnp.int32)
    shifts = jnp.sum(
        jnp.where(shift_index[:, None] == table_index[None, :], shift_table[None, :], 0.0), axis=1
    )
    centre = shifts + CENTRE_OFFSET
    ratio_start = centre / HALF_WIDTH

    keep = [centre]
    gain = [centre]
    factor = 1.0 / ratio_start
    for iteration in range(ITERS):
        factor_next = 1.0 / (2.0 * ratio_start - factor)
        keep.append(factor_next * factor)
        gain.append(2.0 * factor_next / HALF_WIDTH)
        factor = factor_next
    keep = jnp.stack(keep)[:, :, None]
    gain = jnp.stack(gain)[:, :, None]
    block_count = coef_count * BPO
    block_rows = NL // block_count
    owned_rows = kdev // NL
    block_ids = jnp.arange(block_count, dtype=jnp.int32)
    position = jnp.sum(
        jnp.where(order_map[:, None] == block_ids[None, :], block_ids[:, None], 0), axis=0
    )
    paired_row = coef_perm // NL
    column = coef_perm % NL
    place_of = jnp.sum(
        jnp.where(
            (paired_row // block_rows)[None, :] == block_ids[:, None], position[:, None], 0
        ),
        axis=0,
    )
    owner_row = place_of * block_rows + paired_row % block_rows
    full = solve_plain(coef_count, observations, design, shifts[:, None], keep, gain)
    lanes = owned_rows * COLS
    placed = place(owner_row[None, :], column[None, :], full)
    outgoing = placed.astype(jnp.bfloat16).reshape(coef_count, lanes, NL)
    local = coef_scatter(outgoing, coef_count, 5)
    my_blocks = lax.dynamic_slice_in_dim(order_map, coef_rank * BPO, BPO)
    row_offsets = jnp.arange(block_rows, dtype=jnp.int32)
    owned_canon = (my_blocks[:, None] * block_rows + row_offsets[None, :]).reshape(owned_rows)
    lat_block = LAT_DEV * coef_count
    lat_total = lat_block * obs_count
    lat_ids = obs_rank * lat_block + jnp.arange(lat_block, dtype=jnp.int32)
    colatitude = math.pi * (lat_ids.astype(jnp.float32) + 0.5) / lat_total
    orders = jnp.repeat(owned_canon, COLS).astype(jnp.float32)
    parts = legendre(orders, colatitude, local).reshape(2, lat_block, owned_rows, COLS)
    band = parts.transpose(2, 0, 3, 1)
    own_cos, own_sin = wave_tables(owned_canon, NLON)
    first_sum = jnp.einsum("lqc,qk->lck", parts[0], own_cos, precision=lax.Precision.HIGHEST)
    second_sum = jnp.einsum("lqc,qk->lck", parts[1], own_sin, precision=lax.Precision.HIGHEST)
    shares = ((first_sum + second_sum) / math.sqrt(NL)).reshape(
        coef_count, LAT_DEV * COLS, NLON
    )
    field = coef_scatter(shares, coef_count, 6).reshape(LAT_DEV, COLS, NLON).transpose(1, 0, 2)
    return (band, field)


def solution(mesh):
    placed = (P("obs", "coef"), P(None, "obs"), P(), P(), P("coef"), P())
    return jax.shard_map(
        body,
        mesh=mesh,
        in_specs=placed,
        out_specs=(P("coef", None, None, "obs"), P(None, ("obs", "coef"), None)),
        check_vma=False,
    )
```

```python
import functools
import math

import jax
import jax.numpy as jnp
from jax import lax
from jax.experimental import pallas as pl
from jax.experimental.pallas import tpu as pltpu
from jax.sharding import PartitionSpec as P

NL = 192
COLS = 8
ITERS = 2
NSHIFT = 16
BPO = 2
NLON = 1024
LAT_DEV = 1

CENTRE_OFFSET = 1.25
HALF_WIDTH = 0.95
VMEM_SPEC = pl.BlockSpec(memory_space=pltpu.VMEM)
MESH = pl.DeviceIdType.MESH


def greet(axis, n, me):
    barrier = pltpu.get_barrier_semaphore()
    for step in range(1, n):
        pl.semaphore_signal(
            barrier, inc=1, device_id={axis: lax.rem(me + step, n)}, device_id_type=MESH
        )
    pl.semaphore_wait(barrier, n - 1)


def push(axis, n, me, step, src, dst, send_sem, recv_sem):
    return pltpu.make_async_remote_copy(
        src_ref=src,
        dst_ref=dst,
        send_sem=send_sem.at[step],
        recv_sem=recv_sem.at[step],
        device_id={axis: lax.rem(me + step, n)},
        device_id_type=MESH,
    )


def flip(index, mask):
    other = index
    bit = 1
    while bit <= mask:
        if mask & bit:
            other = other + bit - 2 * bit * (index // bit % 2)
        bit *= 2
    return other


def swap(axis, rank, mask, src, dst, send_sem, recv_sem):
    return pltpu.make_async_remote_copy(
        src_ref=src,
        dst_ref=dst,
        send_sem=send_sem.at[mask],
        recv_sem=recv_sem.at[mask],
        device_id={axis: flip(rank, mask)},
        device_id_type=MESH,
    )


def solver_kernel(
    n, nc, obs_hbm, design_ref, shift_hbm, index_hbm, map_hbm, perm_hbm,
    band_out, field_out,
    held, part, landed, gathered, image_sent, image_landed, left_ref, acc,
    obs_ref, shift_table, shift_index, map_ref, perm_ref, turned, places, hot, raw, table, a_tab, b_tab, grow, picked, wave_ref, sent, rows_sent, rows_here, lats_sent, lats_here,
    small_sem, load_sem, send_a, recv_a, send_b, recv_b, send_c, recv_c, send_d, recv_d,
    send_e, recv_e,
):
    me = lax.axis_index("obs")
    mine = lax.axis_index("coef")
    chunk = held.shape[2]
    lanes = hot.shape[0]
    lats = LAT_DEV * nc
    owned = NL // nc
    far_first = list(range(n - 1, 0, -1))

    def load(mask):
        return pltpu.make_async_copy(
            design_ref.at[:, pl.ds(pl.multiple_of(flip(me, mask) * chunk, 128), chunk)],
            held.at[mask],
            load_sem.at[mask],
        )

    small = [
        pltpu.make_async_copy(source, target, small_sem.at[spot])
        for spot, (source, target) in enumerate(
            (
                (map_hbm, map_ref),
                (perm_hbm, perm_ref),
                (obs_hbm, obs_ref),
                (shift_hbm, shift_table),
                (index_hbm, shift_index),
            )
        )
    ]
    for copy in small:
        copy.start()
    for mask in far_first + [0]:
        load(mask).start()
    barrier = pltpu.get_barrier_semaphore()
    for axis, count, rank in (("obs", n, me), ("coef", nc, mine)):
        for mask in range(1, count):
            pl.semaphore_signal(
                barrier, inc=1, device_id={axis: flip(rank, mask)}, device_id_type=MESH
            )

    def scatter_copy(rnd, mask):
        return swap(
            "obs", me, mask, part.at[rnd, mask], landed.at[rnd, mask], send_a.at[rnd], recv_a.at[rnd]
        )

    def gather_copy(rnd, mask):
        return swap(
            "obs", me, mask, gathered.at[rnd, 0], gathered.at[rnd, mask],
            send_b.at[rnd], recv_b.at[rnd],
        )

    def image_copy(rnd, mask):
        return swap(
            "coef", mine, mask, image_sent.at[rnd], image_landed.at[rnd, mask],
            send_c.at[rnd], recv_c.at[rnd],
        )

    def final_copies(mask):
        target = flip(mine, mask)
        return [
            swap("coef", mine, mask, rows_sent.at[target], rows_here.at[mask], send_d, recv_d),
            swap("coef", mine, mask, lats_sent.at[target], lats_here.at[mask], send_e, recv_e),
        ]

    def canon(shape, axis):
        lane = lax.broadcasted_iota(jnp.int32, shape, axis)
        blocks = nc * BPO
        size = NL // blocks
        total = jnp.zeros(shape, jnp.int32)
        for block in range(blocks):
            inside = jnp.logical_and(lane >= block * size, lane < (block + 1) * size)
            total = jnp.where(inside, lane + (map_ref[block] - block) * size, total)
        return total

    def legendre_table():
        order = canon((8, lanes), 1).astype(jnp.float32)
        other = float(NL) - order
        count = lax.broadcasted_iota(jnp.int32, (NL, lanes), 0).astype(jnp.float32)
        low = order[0:1, :] + jnp.zeros((NL, lanes), jnp.float32)
        high = float(NL) - low
        cosine_part = count < high
        level = jnp.where(cosine_part, count + low, count)
        degree_order = jnp.where(cosine_part, low, high)
        valid = jnp.logical_and(count != high, count > 0.0)
        a, b = table_of(level, degree_order, valid)
        a_tab[...] = a
        b_tab[...] = b
        safe = jnp.maximum(count, 1.0)
        grow[...] = jnp.where(
            count == 1.0, math.sqrt(3.0), jnp.sqrt((2.0 * safe + 1.0) / (2.0 * safe))
        )
        lat = lax.broadcasted_iota(jnp.int32, (8, lanes), 0) + me * lats
        colatitude = math.pi * (lat.astype(jnp.float32) + 0.5) / (lats * n)
        cosine = jnp.cos(colatitude)
        sine = jnp.sin(colatitude)

        def climb(degree, carry):
            diag, dc, ds = carry
            diag = diag * (sine * grow[pl.ds(degree, 1), :])
            here = degree.astype(jnp.float32)
            return diag, jnp.where(order == here, diag, dc), jnp.where(other == here, diag, ds)

        start = jnp.ones((8, lanes), jnp.float32)
        zero = jnp.zeros((8, lanes), jnp.float32)
        _, dc, ds = lax.fori_loop(
            1, NL, climb, (start, jnp.where(order == 0.0, start, zero), zero), unroll=8
        )
        def keep_row(column, value):
            for half in range(lanes // 128):
                raw[half, pl.ds(pl.multiple_of(column * 8, 8), 8), :] = value[
                    :, half * 128 : (half + 1) * 128
                ]

        keep_row(0, dc)

        def advance(column, carry):
            now, before = carry
            at = pl.ds(column, 1)
            begin = jnp.where(other == column.astype(jnp.float32), ds, 0.0)
            value = (a_tab[at, :] * cosine) * now - (b_tab[at, :] * before - begin)
            keep_row(column, value)
            return value, now

        lax.fori_loop(1, NL, advance, (dc, zero), unroll=8)
        for t in range(lats):
            for half in range(lanes // 128):
                table[t * NL : (t + 1) * NL, half * 128 : (half + 1) * 128] = raw[
                    half, pl.ds(t, NL, stride=8), :
                ].astype(jnp.bfloat16)

    tile = 256
    tiles = hot.shape[1] // tile

    def find_places():
        index = perm_ref[...].astype(jnp.float32)
        paired = jnp.floor((index + 0.5) * (1.0 / NL))
        column = index - paired * NL
        blocks = nc * BPO
        size = NL // blocks
        block = jnp.floor((paired + 0.5) * (1.0 / size))
        inside = paired - block * size
        row = jnp.zeros_like(index)
        for spot in range(blocks):
            here = block == map_ref[spot].astype(jnp.float32)
            row = jnp.where(here, inside + spot * size, row)
        places[0] = row
        group = jnp.floor((column + 0.5) * 0.125)
        places[1] = group
        places[2] = column - group * 8.0
        places[3] = jnp.where(paired + column < NL, 1.0, 0.0)

    def build_hot():
        def one(index, carry):
            at = pl.ds(pl.multiple_of(index * 128, 128), 128)
            row = lax.broadcasted_iota(jnp.int32, (lanes, 128), 0).astype(jnp.bfloat16)
            same = row == places[0, pl.ds(index, 1), :].astype(jnp.bfloat16)
            hot[:, at] = jnp.where(same, jnp.bfloat16(1.0), jnp.bfloat16(0.0))
            return carry

        lax.fori_loop(0, tiles * (tile // 128), one, 0, unroll=4)

    def pick(first, last):
        def one(index, carry):
            wide = pl.ds(pl.multiple_of(index * tile, 128), tile)
            sub = lax.broadcasted_iota(jnp.int32, (8, 128), 0).astype(jnp.float32)
            product = jnp.dot(table[...], hot[:, wide], preferred_element_type=jnp.float32)
            for half in range(tile // 128):
                spot = pl.ds(index * (tile // 128) + half, 1)
                group = places[1, spot, :] + jnp.zeros_like(sub)
                inner = places[2, spot, :] == sub
                early = places[3, spot, :]
                kept = [jnp.zeros_like(sub)] * lats
                for q in range(NL // 8):
                    here = group == float(q)
                    for t in range(lats):
                        first_row = t * NL + q * 8
                        piece = product[first_row : first_row + 8, half * 128 : half * 128 + 128]
                        kept[t] = jnp.where(here, piece, kept[t])
                at = pl.ds(pl.multiple_of(index * tile + half * 128, 128), 128)
                for t in range(lats):
                    value = jnp.sum(jnp.where(inner, kept[t], 0.0), axis=0, keepdims=True)
                    low = value * early
                    picked[t : t + 1, at] = low
                    picked[lats + t : lats + t + 1, at] = value - low
            return carry

        lax.fori_loop(first, last, one, 0, unroll=last - first)

    def waves():
        order = canon((lanes, 128), 0)
        step = lax.broadcasted_iota(jnp.int32, (lanes, 128), 1)
        scale = 2.0 * math.pi / NLON
        for which in range(2):
            speed = order if which == 0 else NL - order
            fine = lax.rem(speed * step, NLON).astype(jnp.float32) * scale
            coarse = lax.rem(speed * step * 128, NLON).astype(jnp.float32) * scale
            fine_cos, fine_sin = jnp.cos(fine), jnp.sin(fine)
            coarse_cos, coarse_sin = jnp.cos(coarse), jnp.sin(coarse)
            for block in range(NLON // 128):
                cos_b = coarse_cos[:, block : block + 1]
                sin_b = coarse_sin[:, block : block + 1]
                if which == 0:
                    value = cos_b * fine_cos - sin_b * fine_sin
                else:
                    value = sin_b * fine_cos + cos_b * fine_sin
                high = value.astype(jnp.bfloat16)
                at = slice(block * 128, block * 128 + 128)
                wave_ref[which, 0, :, at] = high
                wave_ref[which, 1, :, at] = (value - high.astype(jnp.float32)).astype(jnp.bfloat16)

    straight = n - turned.shape[0]

    def turn(masks):
        for mask in masks:
            turned[mask - straight] = held[mask].T

    def transposed_pass(rnd, filler):
        def product(mask):
            both = jnp.dot(left_ref[...], held[mask], preferred_element_type=jnp.float32)
            return both[:COLS] + both[COLS:]

        for mask in far_first:
            if rnd == 0:
                load(mask).wait()
            part[rnd, mask] = product(mask).astype(jnp.bfloat16)
            scatter_copy(rnd, mask).start()
        if rnd == 0:
            load(0).wait()
        total = product(0)
        filler()
        for mask in far_first:
            scatter_copy(rnd, mask).wait_recv()
            total = total + landed[rnd, mask].astype(jnp.float32)
        gathered[rnd, 0] = total.astype(jnp.bfloat16)
        for mask in far_first:
            gather_copy(rnd, mask).start()

    def image_of(rnd, first, second):
        for mask in range(n):
            if mask:
                gather_copy(rnd, mask).wait_recv()
            block = gathered[rnd, mask]
            if mask >= straight:
                term = jnp.dot(block, turned[mask - straight], preferred_element_type=jnp.float32)
            else:
                term = lax.dot_general(
                    block, held[mask], (((1,), (1,)), ((), ())), preferred_element_type=jnp.float32
                )
            acc[...] = term if mask == 0 else acc[...] + term
            if mask == 0:
                first()
        image = acc[...]
        image_sent[rnd] = image.astype(jnp.bfloat16)
        for mask in range(nc - 1, 0, -1):
            image_copy(rnd, mask).start()
        second()
        for mask in range(1, nc):
            image_copy(rnd, mask).wait_recv()
            image = image + image_landed[rnd, mask].astype(jnp.float32)
        return image

    def split(value):
        high = value.astype(jnp.bfloat16).astype(jnp.float32)
        left_ref[...] = jnp.concatenate([high, value - high], axis=0).astype(jnp.bfloat16)

    share = [functools.partial(pick, i * tiles // 6, (i + 1) * tiles // 6) for i in range(6)]
    turn_first, turn_second = far_first[: n // 2], far_first[n // 2 : n - straight]
    scatter_fill = [
        functools.partial(turn, turn_first), lambda: (share[1](), share[2]()), share[5]
    ]
    first_fill = [lambda: (turn(turn_second), legendre_table()), share[3]]
    second_fill = [lambda: (build_hot(), share[0]()), share[4]]
    for copy in small:
        copy.wait()
    find_places()
    pl.semaphore_wait(barrier, n + nc - 2)
    line = lax.broadcasted_iota(jnp.int32, (COLS, 1), 0)
    shift = jnp.zeros((COLS, 1), jnp.float32)
    for right_side in range(COLS):
        shift = jnp.where(line == right_side, shift_table[shift_index[right_side]], shift)
    centre = shift + CENTRE_OFFSET
    ratio_start = centre / HALF_WIDTH
    factor = 1.0 / ratio_start
    residual = obs_ref[...].astype(jnp.float32)
    split(residual)
    transposed_pass(0, scatter_fill[0])
    direction = residual / centre
    answer = direction
    for rnd in range(1, ITERS + 1):
        image = image_of(rnd - 1, first_fill[rnd - 1], second_fill[rnd - 1])
        if rnd == 1:
            image = image / centre
        residual = residual - (image + shift * direction)
        factor_next = 1.0 / (2.0 * ratio_start - factor)
        direction = (factor_next * factor) * direction + (
            2.0 * factor_next / HALF_WIDTH
        ) * residual
        factor = factor_next
        answer = answer + direction
        split(answer if rnd == ITERS else direction)
        transposed_pass(rnd, scatter_fill[rnd])
    for mask in range(n):
        if mask:
            gather_copy(ITERS, mask).wait_recv()
        at = pl.ds(pl.multiple_of(flip(me, mask) * chunk, 128), chunk)
        values = gathered[ITERS, mask].astype(jnp.float32)
        left = jnp.concatenate(
            [values * picked[t : t + 1, at] for t in range(2 * lats)], axis=0
        )
        high = left.astype(jnp.bfloat16).astype(jnp.float32)
        left = jnp.concatenate([high, left - high], axis=0).astype(jnp.bfloat16)
        both = lax.dot_general(
            left, hot[:, at], (((1,), (1,)), ((), ())), preferred_element_type=jnp.float32
        )
        term = both[: 2 * lats * COLS] + both[2 * lats * COLS :]
        sent[...] = term if mask == 0 else sent[...] + term
    side = lats * COLS
    total = sent[...]
    blank = jnp.zeros((side, rows_sent.shape[2] - 2 * owned), jnp.float32)
    for owner in range(nc):
        block = total[:, owner * owned : (owner + 1) * owned]
        rows_sent[owner] = jnp.concatenate([block[:side], block[side:], blank], axis=1)
        for which in range(2):
            first = which * side + owner * COLS
            lats_sent[owner, which] = total[first : first + COLS]
    for mask in range(nc - 1, 0, -1):
        for copy in final_copies(mask):
            copy.start()
    waves()
    own = rows_sent[mine]
    waved = lats_sent[mine]
    for mask in range(1, nc):
        for copy in final_copies(mask):
            copy.wait_recv()
        own = own + rows_here[mask]
        waved = waved + lats_here[mask]
    own = own / math.sqrt(NL)
    waved = waved / math.sqrt(NL)
    field = jnp.zeros((COLS, NLON), jnp.float32)
    for which in range(2):
        rows = waved[which]
        high = rows.astype(jnp.bfloat16).astype(jnp.float32)
        left = jnp.concatenate([high, rows - high], axis=0).astype(jnp.bfloat16)
        for level in range(2):
            both = jnp.dot(left, wave_ref[which, level], preferred_element_type=jnp.float32)
            field = field + both[:COLS] + both[COLS:]
    field_out[...] = field / math.sqrt(NL)
    band_out[...] = own
    for rnd in range(ITERS + 1):
        for mask in far_first:
            scatter_copy(rnd, mask).wait_send()
            gather_copy(rnd, mask).wait_send()
        if rnd < ITERS:
            for mask in range(1, nc):
                image_copy(rnd, mask).wait_send()
    for mask in range(1, nc):
        for copy in final_copies(mask):
            copy.wait_send()


def arrange_kernel(band_ref, field_ref, band_out, field_out):
    owned = band_out.shape[3]
    lats = band_out.shape[2]
    field_out[:, 0, :] = field_ref[...]
    for column in range(COLS):
        line = band_ref[pl.ds(column, lats, stride=COLS), :]
        for which in range(2):
            band_out[which, column] = line[:, which * owned : (which + 1) * owned]


def arrange(band, field, owned):
    return pl.pallas_call(
        arrange_kernel,
        out_shape=(
            jax.ShapeDtypeStruct((2, COLS, band.shape[0] // COLS, owned), jnp.float32),
            jax.ShapeDtypeStruct((COLS, 1, NLON), jnp.float32),
        ),
        in_specs=[VMEM_SPEC] * 2,
        out_specs=(VMEM_SPEC,) * 2,
        name="arrange",
    )(band, field)


def solve(n, nc, observations, design, shift_table, shift_index, order_map, perm):
    rows, kdev = design.shape
    chunk = kdev // n
    rounds = ITERS + 1
    lanes = -(-NL // 128) * 128
    lats = LAT_DEV * nc
    side = 2 * lats * COLS
    blocks = pltpu.VMEM((rounds, n, COLS, chunk), jnp.bfloat16)
    tables = pltpu.VMEM((NL, lanes), jnp.float32)
    return pl.pallas_call(
        functools.partial(solver_kernel, n, nc),
        out_shape=(
            jax.ShapeDtypeStruct((side // 2, 128), jnp.float32),
            jax.ShapeDtypeStruct((COLS, NLON), jnp.float32),
        ),
        in_specs=[pl.BlockSpec(memory_space=pltpu.HBM)] * 6,
        out_specs=(VMEM_SPEC, VMEM_SPEC),
        scratch_shapes=[pltpu.VMEM((n, rows, chunk), jnp.bfloat16)]
        + [blocks] * 3
        + [
            pltpu.VMEM((ITERS, COLS, rows), jnp.bfloat16),
            pltpu.VMEM((ITERS, nc, COLS, rows), jnp.bfloat16),
            pltpu.VMEM((2 * COLS, rows), jnp.bfloat16),
            pltpu.VMEM((COLS, rows), jnp.float32),
            pltpu.VMEM(observations.shape, observations.dtype),
            pltpu.SMEM(shift_table.shape, jnp.float32),
            pltpu.SMEM(shift_index.shape, jnp.int32),
            pltpu.SMEM(order_map.shape, jnp.int32),
            pltpu.VMEM((kdev // 128, 128), jnp.int32),
            pltpu.VMEM((3 * n // 4, chunk, rows), jnp.bfloat16),
            pltpu.VMEM((4, kdev // 128, 128), jnp.float32),
            pltpu.VMEM((lanes, kdev), jnp.bfloat16),
            pltpu.VMEM((lanes // 128, NL * 8, 128), jnp.float32),
            pltpu.VMEM((lats * NL, lanes), jnp.bfloat16),
            tables,
            tables,
            tables,
            pltpu.VMEM((2 * lats, kdev), jnp.float32),
            pltpu.VMEM((2, 2, lanes, NLON), jnp.bfloat16),
            pltpu.VMEM((side, lanes), jnp.float32),
        ]
        + [pltpu.VMEM((nc, side // 2, 128), jnp.float32)] * 2
        + [pltpu.VMEM((nc, 2, COLS, lanes), jnp.float32)] * 2
        + [
            pltpu.SemaphoreType.DMA((5,)),
            pltpu.SemaphoreType.DMA((n,)),
        ]
        + [pltpu.SemaphoreType.DMA((rounds, n))] * 4
        + [pltpu.SemaphoreType.DMA((ITERS, nc))] * 2
        + [pltpu.SemaphoreType.DMA((nc,))] * 4,
        compiler_params=pltpu.CompilerParams(
            collective_id=0, has_side_effects=True, vmem_limit_bytes=56 << 20
        ),
        name="solve",
    )(observations, design, shift_table, shift_index, order_map, perm.reshape(-1, 128))


def sum_kernel(n, x_ref, o_ref, landed, send_sem, recv_sem):
    me = lax.axis_index("coef")
    greet("coef", n, me)
    copies = []
    for step in range(1, n):
        copy = push("coef", n, me, step, x_ref, landed.at[step], send_sem, recv_sem)
        copy.start()
        copies.append(copy)
    total = x_ref[...]
    for step in range(1, n):
        copies[step - 1].wait()
        total = total + landed[step]
    o_ref[...] = total.astype(o_ref.dtype)


def coef_sum(partial, n, cid):
    return pl.pallas_call(
        functools.partial(sum_kernel, n),
        out_shape=jax.ShapeDtypeStruct(partial.shape, jnp.bfloat16),
        in_specs=[VMEM_SPEC],
        out_specs=VMEM_SPEC,
        scratch_shapes=[pltpu.VMEM((n,) + partial.shape, jnp.float32)]
        + [pltpu.SemaphoreType.DMA((n,))] * 2,
        compiler_params=pltpu.CompilerParams(collective_id=cid, has_side_effects=True),
        name="coef_sum",
    )(partial)


def solve_plain(nc, observations, design, shift, keep, gain):
    def transposed_pass(left):
        return lax.psum(jnp.dot(left, design, preferred_element_type=jnp.float32), "obs")

    residual = transposed_pass(observations)
    direction = residual / keep[0]
    solution = direction
    for rnd in range(1, ITERS + 1):
        partial_image = lax.dot_general(
            direction.astype(jnp.bfloat16),
            design,
            (((1,), (1,)), ((), ())),
            preferred_element_type=jnp.float32,
        )
        total = transposed_pass(coef_sum(partial_image, nc, 2 + rnd))
        residual = residual - (total + shift * direction)
        direction = keep[rnd] * direction + gain[rnd] * residual
        solution = solution + direction
    return solution.astype(jnp.bfloat16)


def scatter_kernel(n, x_ref, o_ref, landed, send_sem, recv_sem):
    me = lax.axis_index("coef")
    greet("coef", n, me)
    copies = []
    for step in range(1, n):
        target = lax.rem(me + step, n)
        copy = push("coef", n, me, step, x_ref.at[target], landed.at[step], send_sem, recv_sem)
        copy.start()
        copies.append(copy)
    total = x_ref[me].astype(jnp.float32)
    for step in range(1, n):
        copies[step - 1].wait()
        total = total + landed[step].astype(jnp.float32)
    o_ref[...] = total


def coef_scatter(parts, n, cid):
    return pl.pallas_call(
        functools.partial(scatter_kernel, n),
        out_shape=jax.ShapeDtypeStruct(parts.shape[1:], jnp.float32),
        in_specs=[VMEM_SPEC],
        out_specs=VMEM_SPEC,
        scratch_shapes=[pltpu.VMEM(parts.shape, parts.dtype)]
        + [pltpu.SemaphoreType.DMA((n,))] * 2,
        compiler_params=pltpu.CompilerParams(collective_id=cid, has_side_effects=True),
        name="coef_scatter",
    )(parts)


def place_kernel(width, row_ref, col_ref, sol_ref, out_ref, spread):
    out_ref[...] = jnp.zeros_like(out_ref)
    wide = jnp.zeros((COLS, width), jnp.int32)

    def step(index, carry):
        at = pl.ds(pl.multiple_of(index * width, 128), width)
        values = sol_ref[:, at].astype(jnp.float32)
        rows = row_ref[:, at] + wide
        for pair in range(NL // 2):
            first = jnp.where(rows == 2 * pair, values, 0.0)
            second = jnp.where(rows == 2 * pair + 1, values, 0.0)
            both = jnp.concatenate([first, second], axis=0)
            spread[pair * 2 * COLS : (pair + 1) * 2 * COLS, :] = both.astype(jnp.bfloat16)
        degree = lax.broadcasted_iota(jnp.int32, (NL, width), 0)
        hot = jnp.where(degree == col_ref[:, at], 1.0, 0.0).astype(jnp.bfloat16)
        out_ref[...] += lax.dot_general(
            spread[...], hot, (((1,), (1,)), ((), ())), preferred_element_type=jnp.float32
        )
        return carry

    lax.fori_loop(0, sol_ref.shape[1] // width, step, 0)


def place(rows, cols, sol):
    kdev = sol.shape[1]
    width = next(w for w in (512, 384, 256, 128) if kdev % w == 0)
    return pl.pallas_call(
        functools.partial(place_kernel, width),
        out_shape=jax.ShapeDtypeStruct((NL * COLS, NL), jnp.float32),
        in_specs=[VMEM_SPEC] * 3,
        out_specs=VMEM_SPEC,
        scratch_shapes=[pltpu.VMEM((NL * COLS, width), jnp.bfloat16)],
        compiler_params=pltpu.CompilerParams(vmem_limit_bytes=32 << 20),
        name="place",
    )(rows, cols, sol)


def table_of(level, order, valid):
    product = (level - order) * (level + order)
    denom = jnp.where(valid, product, 1.0)
    first = jnp.sqrt(jnp.maximum((2.0 * level - 1.0) * (2.0 * level + 1.0), 0.0) / denom)
    second = jnp.sqrt(
        jnp.maximum((2.0 * level + 1.0) * (level + order - 1.0) * (level - order - 1.0), 0.0)
        / (denom * jnp.maximum(2.0 * level - 3.0, 1.0))
    )
    return jnp.where(valid, first, 0.0), jnp.where(valid, second, 0.0)


def legendre_kernel(
    angle_ref, local_ref, out_ref, a_c, b_c, a_s, b_s, grow, w_ref
):
    lats, lanes = angle_ref.shape[1:]
    w_ref[...] = local_ref[...].T
    order = angle_ref[0, 0:1, :]
    other = float(NL) - order
    count = lax.broadcasted_iota(jnp.int32, (NL, lanes), 0).astype(jnp.float32)
    wide = jnp.zeros((NL, lanes), jnp.float32)
    low = order + wide
    high = other + wide
    level = count + low
    a, b = table_of(level, low, jnp.logical_and(count > 0.0, level < float(NL)))
    a_c[...] = a
    b_c[...] = b
    a, b = table_of(count, high, count > high)
    a_s[...] = a
    b_s[...] = b
    safe = jnp.maximum(count, 1.0)
    grow[...] = jnp.where(
        count == 1.0, math.sqrt(3.0), jnp.sqrt((2.0 * safe + 1.0) / (2.0 * safe))
    )
    cosine = angle_ref[1]
    sine = angle_ref[2]
    zero = cosine * 0.0
    low = angle_ref[0]
    high = float(NL) - low

    def climb(degree, carry):
        diag, dc, ds = carry
        diag = diag * sine * grow[pl.ds(degree, 1), :]
        here = degree.astype(jnp.float32)
        return diag, jnp.where(low == here, diag, dc), jnp.where(high == here, diag, ds)

    start = zero + 1.0
    _, dc, ds = lax.fori_loop(
        1, NL, climb, (start, jnp.where(low == 0.0, start, zero), zero), unroll=4
    )
    acc_c = dc * w_ref[pl.ds(0, 1), :]

    def advance(column, carry):
        pc, ec, ps, es, acc_c, acc_s = carry
        at = pl.ds(column, 1)
        w = w_ref[at, :]
        vc = a_c[at, :] * cosine * pc - b_c[at, :] * ec
        begin = jnp.where(high == column.astype(jnp.float32), ds, 0.0)
        vs = a_s[at, :] * cosine * ps - b_s[at, :] * es + begin
        return vc, pc, vs, ps, acc_c + vc * w, acc_s + vs * w

    _, _, _, _, acc_c, acc_s = lax.fori_loop(
        1, NL, advance, (dc, zero, zero, zero, acc_c, zero), unroll=4
    )
    out_ref[0] = acc_c / math.sqrt(NL)
    out_ref[1] = acc_s / math.sqrt(NL)


def legendre(orders, colatitude, w):
    lanes = w.shape[0]
    lats = colatitude.shape[0]
    which = lax.broadcasted_iota(jnp.int32, (3, lats, lanes), 0)
    angles = jnp.where(
        which == 0,
        orders[None, None, :],
        jnp.where(which == 1, jnp.cos(colatitude)[:, None], jnp.sin(colatitude)[:, None]),
    )
    table = pltpu.VMEM((NL, lanes), jnp.float32)
    return pl.pallas_call(
        legendre_kernel,
        out_shape=jax.ShapeDtypeStruct((2, lats, lanes), jnp.float32),
        in_specs=[VMEM_SPEC] * 2,
        out_specs=VMEM_SPEC,
        scratch_shapes=[table] * 6,
        name="legendre",
    )(
        angles,
        w,
    )


def wave_tables(rows, longitudes):
    steps_k = jnp.arange(longitudes, dtype=jnp.int32)
    scale = 2.0 * math.pi / longitudes
    cos_angle = (rows[:, None] * steps_k[None, :] % longitudes).astype(jnp.float32) * scale
    sin_angle = ((NL - rows)[:, None] * steps_k[None, :] % longitudes).astype(jnp.float32) * scale
    return (jnp.cos(cos_angle), jnp.sin(sin_angle))


def body(design, observations, shift_table, shift_index, coef_perm, order_map):
    obs_count = lax.axis_size("obs")
    coef_count = lax.axis_size("coef")
    coef_rank = lax.axis_index("coef")
    obs_rank = lax.axis_index("obs")
    kdev = design.shape[1]
    chunk = kdev // obs_count
    paired_up = all(c & (c - 1) == 0 for c in (obs_count, coef_count))
    direct = (
        chunk % 128 == 0
        and kdev % 256 == 0
        and paired_up
        and LAT_DEV * coef_count <= 8
        and 2 * NL // coef_count <= 128
        and NL <= 256
    )
    if direct:
        band, field = solve(
            obs_count, coef_count, observations, design, shift_table, shift_index, order_map,
            coef_perm,
        )
        band, field = arrange(band, field, NL // coef_count)
        return (band.transpose(3, 0, 1, 2), field)
    table_index = jnp.arange(NSHIFT, dtype=jnp.int32)
    shifts = jnp.sum(
        jnp.where(shift_index[:, None] == table_index[None, :], shift_table[None, :], 0.0), axis=1
    )
    centre = shifts + CENTRE_OFFSET
    ratio_start = centre / HALF_WIDTH

    keep = [centre]
    gain = [centre]
    factor = 1.0 / ratio_start
    for iteration in range(ITERS):
        factor_next = 1.0 / (2.0 * ratio_start - factor)
        keep.append(factor_next * factor)
        gain.append(2.0 * factor_next / HALF_WIDTH)
        factor = factor_next
    keep = jnp.stack(keep)[:, :, None]
    gain = jnp.stack(gain)[:, :, None]
    block_count = coef_count * BPO
    block_rows = NL // block_count
    owned_rows = kdev // NL
    block_ids = jnp.arange(block_count, dtype=jnp.int32)
    position = jnp.sum(
        jnp.where(order_map[:, None] == block_ids[None, :], block_ids[:, None], 0), axis=0
    )
    paired_row = coef_perm // NL
    column = coef_perm % NL
    place_of = jnp.sum(
        jnp.where(
            (paired_row // block_rows)[None, :] == block_ids[:, None], position[:, None], 0
        ),
        axis=0,
    )
    owner_row = place_of * block_rows + paired_row % block_rows
    full = solve_plain(coef_count, observations, design, shifts[:, None], keep, gain)
    lanes = owned_rows * COLS
    placed = place(owner_row[None, :], column[None, :], full)
    outgoing = placed.astype(jnp.bfloat16).reshape(coef_count, lanes, NL)
    local = coef_scatter(outgoing, coef_count, 5)
    my_blocks = lax.dynamic_slice_in_dim(order_map, coef_rank * BPO, BPO)
    row_offsets = jnp.arange(block_rows, dtype=jnp.int32)
    owned_canon = (my_blocks[:, None] * block_rows + row_offsets[None, :]).reshape(owned_rows)
    lat_block = LAT_DEV * coef_count
    lat_total = lat_block * obs_count
    lat_ids = obs_rank * lat_block + jnp.arange(lat_block, dtype=jnp.int32)
    colatitude = math.pi * (lat_ids.astype(jnp.float32) + 0.5) / lat_total
    orders = jnp.repeat(owned_canon, COLS).astype(jnp.float32)
    parts = legendre(orders, colatitude, local).reshape(2, lat_block, owned_rows, COLS)
    band = parts.transpose(2, 0, 3, 1)
    own_cos, own_sin = wave_tables(owned_canon, NLON)
    first_sum = jnp.einsum("lqc,qk->lck", parts[0], own_cos, precision=lax.Precision.HIGHEST)
    second_sum = jnp.einsum("lqc,qk->lck", parts[1], own_sin, precision=lax.Precision.HIGHEST)
    shares = ((first_sum + second_sum) / math.sqrt(NL)).reshape(
        coef_count, LAT_DEV * COLS, NLON
    )
    field = coef_scatter(shares, coef_count, 6).reshape(LAT_DEV, COLS, NLON).transpose(1, 0, 2)
    return (band, field)


def solution(mesh):
    placed = (P("obs", "coef"), P(None, "obs"), P(), P(), P("coef"), P())
    return jax.shard_map(
        body,
        mesh=mesh,
        in_specs=placed,
        out_specs=(P("coef", None, None, "obs"), P(None, ("obs", "coef"), None)),
        check_vma=False,
    )
```

```python
import functools
import math

import jax
import jax.numpy as jnp
from jax import lax
from jax.experimental import pallas as pl
from jax.experimental.pallas import tpu as pltpu
from jax.sharding import PartitionSpec as P

NL = 192
COLS = 8
ITERS = 2
NSHIFT = 16
BPO = 2
NLON = 1024
LAT_DEV = 1

CENTRE_OFFSET = 1.25
HALF_WIDTH = 0.95
VMEM_SPEC = pl.BlockSpec(memory_space=pltpu.VMEM)
MESH = pl.DeviceIdType.MESH


def greet(axis, n, me):
    barrier = pltpu.get_barrier_semaphore()
    for step in range(1, n):
        pl.semaphore_signal(
            barrier, inc=1, device_id={axis: lax.rem(me + step, n)}, device_id_type=MESH
        )
    pl.semaphore_wait(barrier, n - 1)


def push(axis, n, me, step, src, dst, send_sem, recv_sem):
    return pltpu.make_async_remote_copy(
        src_ref=src,
        dst_ref=dst,
        send_sem=send_sem.at[step],
        recv_sem=recv_sem.at[step],
        device_id={axis: lax.rem(me + step, n)},
        device_id_type=MESH,
    )


def flip(index, mask):
    other = index
    bit = 1
    while bit <= mask:
        if mask & bit:
            other = other + bit - 2 * bit * (index // bit % 2)
        bit *= 2
    return other


def swap(axis, rank, mask, src, dst, send_sem, recv_sem):
    return pltpu.make_async_remote_copy(
        src_ref=src,
        dst_ref=dst,
        send_sem=send_sem.at[mask],
        recv_sem=recv_sem.at[mask],
        device_id={axis: flip(rank, mask)},
        device_id_type=MESH,
    )


def solver_kernel(
    n, nc, obs_hbm, design_ref, shift_hbm, index_hbm, map_hbm, perm_hbm,
    band_out, field_out,
    held, part, landed, gathered, image_sent, image_landed, left_ref, acc,
    obs_ref, shift_table, shift_index, map_ref, perm_ref, turned, places, hot, hot_turned, raw, table, a_tab, b_tab, grow, picked, wave_ref, sent, rows_sent, rows_here, lats_sent, lats_here,
    small_sem, load_sem, send_a, recv_a, send_b, recv_b, send_c, recv_c, send_d, recv_d,
    send_e, recv_e,
):
    me = lax.axis_index("obs")
    mine = lax.axis_index("coef")
    chunk = held.shape[2]
    lanes = hot.shape[0]
    lats = LAT_DEV * nc
    owned = NL // nc
    far_first = list(range(n - 1, 0, -1))

    def load(mask):
        return pltpu.make_async_copy(
            design_ref.at[:, pl.ds(pl.multiple_of(flip(me, mask) * chunk, 128), chunk)],
            held.at[mask],
            load_sem.at[mask],
        )

    small = [
        pltpu.make_async_copy(source, target, small_sem.at[spot])
        for spot, (source, target) in enumerate(
            (
                (map_hbm, map_ref),
                (perm_hbm, perm_ref),
                (obs_hbm, obs_ref),
                (shift_hbm, shift_table),
                (index_hbm, shift_index),
            )
        )
    ]
    for copy in small:
        copy.start()
    for mask in far_first + [0]:
        load(mask).start()
    barrier = pltpu.get_barrier_semaphore()
    for axis, count, rank in (("obs", n, me), ("coef", nc, mine)):
        for mask in range(1, count):
            pl.semaphore_signal(
                barrier, inc=1, device_id={axis: flip(rank, mask)}, device_id_type=MESH
            )

    def scatter_copy(rnd, mask):
        return swap(
            "obs", me, mask, part.at[rnd, mask], landed.at[rnd, mask], send_a.at[rnd], recv_a.at[rnd]
        )

    def gather_copy(rnd, mask):
        return swap(
            "obs", me, mask, gathered.at[rnd, 0], gathered.at[rnd, mask],
            send_b.at[rnd], recv_b.at[rnd],
        )

    def image_copy(rnd, mask):
        return swap(
            "coef", mine, mask, image_sent.at[rnd], image_landed.at[rnd, mask],
            send_c.at[rnd], recv_c.at[rnd],
        )

    def final_copies(mask):
        target = flip(mine, mask)
        return [
            swap("coef", mine, mask, rows_sent.at[target], rows_here.at[mask], send_d, recv_d),
            swap("coef", mine, mask, lats_sent.at[target], lats_here.at[mask], send_e, recv_e),
        ]

    def canon(shape, axis):
        lane = lax.broadcasted_iota(jnp.int32, shape, axis)
        blocks = nc * BPO
        size = NL // blocks
        total = jnp.zeros(shape, jnp.int32)
        for block in range(blocks):
            inside = jnp.logical_and(lane >= block * size, lane < (block + 1) * size)
            total = jnp.where(inside, lane + (map_ref[block] - block) * size, total)
        return total

    def legendre_table():
        order = canon((8, lanes), 1).astype(jnp.float32)
        other = float(NL) - order
        count = lax.broadcasted_iota(jnp.int32, (NL, lanes), 0).astype(jnp.float32)
        low = order[0:1, :] + jnp.zeros((NL, lanes), jnp.float32)
        high = float(NL) - low
        cosine_part = count < high
        level = jnp.where(cosine_part, count + low, count)
        degree_order = jnp.where(cosine_part, low, high)
        valid = jnp.logical_and(count != high, count > 0.0)
        a, b = table_of(level, degree_order, valid)
        a_tab[...] = a
        b_tab[...] = b
        safe = jnp.maximum(count, 1.0)
        grow[...] = jnp.where(
            count == 1.0, math.sqrt(3.0), jnp.sqrt((2.0 * safe + 1.0) / (2.0 * safe))
        )
        lat = lax.broadcasted_iota(jnp.int32, (8, lanes), 0) + me * lats
        colatitude = math.pi * (lat.astype(jnp.float32) + 0.5) / (lats * n)
        cosine = jnp.cos(colatitude)
        sine = jnp.sin(colatitude)

        def climb(degree, carry):
            diag, dc, ds = carry
            diag = diag * (sine * grow[pl.ds(degree, 1), :])
            here = degree.astype(jnp.float32)
            return diag, jnp.where(order == here, diag, dc), jnp.where(other == here, diag, ds)

        start = jnp.ones((8, lanes), jnp.float32)
        zero = jnp.zeros((8, lanes), jnp.float32)
        _, dc, ds = lax.fori_loop(
            1, NL, climb, (start, jnp.where(order == 0.0, start, zero), zero), unroll=8
        )
        def keep_row(column, value):
            for half in range(lanes // 128):
                raw[half, pl.ds(pl.multiple_of(column * 8, 8), 8), :] = value[
                    :, half * 128 : (half + 1) * 128
                ]

        keep_row(0, dc)

        def advance(column, carry):
            now, before = carry
            at = pl.ds(column, 1)
            begin = jnp.where(other == column.astype(jnp.float32), ds, 0.0)
            value = (a_tab[at, :] * cosine) * now - (b_tab[at, :] * before - begin)
            keep_row(column, value)
            return value, now

        lax.fori_loop(1, NL, advance, (dc, zero), unroll=8)
        for t in range(lats):
            for half in range(lanes // 128):
                table[t * NL : (t + 1) * NL, half * 128 : (half + 1) * 128] = raw[
                    half, pl.ds(t, NL, stride=8), :
                ].astype(jnp.bfloat16)

    tile = 256
    tiles = hot.shape[1] // tile

    def find_places():
        index = perm_ref[...].astype(jnp.float32)
        paired = jnp.floor((index + 0.5) * (1.0 / NL))
        column = index - paired * NL
        blocks = nc * BPO
        size = NL // blocks
        block = jnp.floor((paired + 0.5) * (1.0 / size))
        inside = paired - block * size
        row = jnp.zeros_like(index)
        for spot in range(blocks):
            here = block == map_ref[spot].astype(jnp.float32)
            row = jnp.where(here, inside + spot * size, row)
        places[0] = row
        group = jnp.floor((column + 0.5) * 0.125)
        places[1] = group
        places[2] = column - group * 8.0
        places[3] = jnp.where(paired + column < NL, 1.0, 0.0)

    def build_hot():
        def one(index, carry):
            at = pl.ds(pl.multiple_of(index * 128, 128), 128)
            row = lax.broadcasted_iota(jnp.int32, (lanes, 128), 0).astype(jnp.bfloat16)
            same = row == places[0, pl.ds(index, 1), :].astype(jnp.bfloat16)
            hot[:, at] = jnp.where(same, jnp.bfloat16(1.0), jnp.bfloat16(0.0))
            return carry

        lax.fori_loop(0, tiles * (tile // 128), one, 0, unroll=4)

    def turn_hot():
        for mask in range(n):
            at = pl.ds(pl.multiple_of(flip(me, mask) * chunk, 128), chunk)
            hot_turned[mask] = hot[:, at].T

    def pick(first, last):
        def one(index, carry):
            wide = pl.ds(pl.multiple_of(index * tile, 128), tile)
            sub = lax.broadcasted_iota(jnp.int32, (8, 128), 0).astype(jnp.float32)
            product = jnp.dot(table[...], hot[:, wide], preferred_element_type=jnp.float32)
            for half in range(tile // 128):
                spot = pl.ds(index * (tile // 128) + half, 1)
                group = places[1, spot, :] + jnp.zeros_like(sub)
                inner = places[2, spot, :] == sub
                early = places[3, spot, :]
                kept = [jnp.zeros_like(sub)] * lats
                for q in range(NL // 8):
                    here = group == float(q)
                    for t in range(lats):
                        first_row = t * NL + q * 8
                        piece = product[first_row : first_row + 8, half * 128 : half * 128 + 128]
                        kept[t] = jnp.where(here, piece, kept[t])
                at = pl.ds(pl.multiple_of(index * tile + half * 128, 128), 128)
                for t in range(lats):
                    value = jnp.sum(jnp.where(inner, kept[t], 0.0), axis=0, keepdims=True)
                    low = value * early
                    picked[t : t + 1, at] = low
                    picked[lats + t : lats + t + 1, at] = value - low
            return carry

        lax.fori_loop(first, last, one, 0, unroll=last - first)

    def waves():
        order = canon((lanes, 128), 0)
        step = lax.broadcasted_iota(jnp.int32, (lanes, 128), 1)
        scale = 2.0 * math.pi / NLON
        for which in range(2):
            speed = order if which == 0 else NL - order
            fine = lax.rem(speed * step, NLON).astype(jnp.float32) * scale
            coarse = lax.rem(speed * step * 128, NLON).astype(jnp.float32) * scale
            fine_cos, fine_sin = jnp.cos(fine), jnp.sin(fine)
            coarse_cos, coarse_sin = jnp.cos(coarse), jnp.sin(coarse)
            for block in range(NLON // 128):
                cos_b = coarse_cos[:, block : block + 1]
                sin_b = coarse_sin[:, block : block + 1]
                if which == 0:
                    value = cos_b * fine_cos - sin_b * fine_sin
                else:
                    value = sin_b * fine_cos + cos_b * fine_sin
                high = value.astype(jnp.bfloat16)
                at = slice(block * 128, block * 128 + 128)
                wave_ref[which, 0, :, at] = high
                wave_ref[which, 1, :, at] = (value - high.astype(jnp.float32)).astype(jnp.bfloat16)

    straight = n - turned.shape[0]

    def turn(masks):
        for mask in masks:
            turned[mask - straight] = held[mask].T

    def transposed_pass(rnd, filler):
        def product(mask):
            both = jnp.dot(left_ref[...], held[mask], preferred_element_type=jnp.float32)
            return both[:COLS] + both[COLS:]

        for mask in far_first:
            if rnd == 0:
                load(mask).wait()
            part[rnd, mask] = product(mask).astype(jnp.bfloat16)
            scatter_copy(rnd, mask).start()
        if rnd == 0:
            load(0).wait()
        total = product(0)
        filler()
        for mask in far_first:
            scatter_copy(rnd, mask).wait_recv()
            total = total + landed[rnd, mask].astype(jnp.float32)
        gathered[rnd, 0] = total.astype(jnp.bfloat16)
        for mask in far_first:
            gather_copy(rnd, mask).start()

    def image_of(rnd, first, second):
        for mask in range(n):
            if mask:
                gather_copy(rnd, mask).wait_recv()
            block = gathered[rnd, mask]
            if mask >= straight:
                term = jnp.dot(block, turned[mask - straight], preferred_element_type=jnp.float32)
            else:
                term = lax.dot_general(
                    block, held[mask], (((1,), (1,)), ((), ())), preferred_element_type=jnp.float32
                )
            acc[...] = term if mask == 0 else acc[...] + term
            if mask == 0:
                first()
        image = acc[...]
        image_sent[rnd] = image.astype(jnp.bfloat16)
        for mask in range(nc - 1, 0, -1):
            image_copy(rnd, mask).start()
        second()
        for mask in range(1, nc):
            image_copy(rnd, mask).wait_recv()
            image = image + image_landed[rnd, mask].astype(jnp.float32)
        return image

    def split(value):
        high = value.astype(jnp.bfloat16).astype(jnp.float32)
        left_ref[...] = jnp.concatenate([high, value - high], axis=0).astype(jnp.bfloat16)

    share = [functools.partial(pick, i * tiles // 6, (i + 1) * tiles // 6) for i in range(6)]
    turn_first, turn_second = far_first[: n // 2], far_first[n // 2 : n - straight]
    scatter_fill = [
        functools.partial(turn, turn_first), lambda: (share[1](), share[2]()), turn_hot
    ]
    first_fill = [
        lambda: (turn(turn_second), legendre_table()), lambda: (share[3](), share[4]())
    ]
    second_fill = [lambda: (build_hot(), share[0]()), share[5]]
    for copy in small:
        copy.wait()
    find_places()
    pl.semaphore_wait(barrier, n + nc - 2)
    line = lax.broadcasted_iota(jnp.int32, (COLS, 1), 0)
    shift = jnp.zeros((COLS, 1), jnp.float32)
    for right_side in range(COLS):
        shift = jnp.where(line == right_side, shift_table[shift_index[right_side]], shift)
    centre = shift + CENTRE_OFFSET
    ratio_start = centre / HALF_WIDTH
    factor = 1.0 / ratio_start
    residual = obs_ref[...].astype(jnp.float32)
    split(residual)
    transposed_pass(0, scatter_fill[0])
    direction = residual / centre
    answer = direction
    for rnd in range(1, ITERS + 1):
        image = image_of(rnd - 1, first_fill[rnd - 1], second_fill[rnd - 1])
        if rnd == 1:
            image = image / centre
        residual = residual - (image + shift * direction)
        factor_next = 1.0 / (2.0 * ratio_start - factor)
        direction = (factor_next * factor) * direction + (
            2.0 * factor_next / HALF_WIDTH
        ) * residual
        factor = factor_next
        answer = answer + direction
        split(answer if rnd == ITERS else direction)
        transposed_pass(rnd, scatter_fill[rnd])
    for mask in range(n):
        if mask:
            gather_copy(ITERS, mask).wait_recv()
        at = pl.ds(pl.multiple_of(flip(me, mask) * chunk, 128), chunk)
        values = gathered[ITERS, mask].astype(jnp.float32)
        left = jnp.concatenate(
            [values * picked[t : t + 1, at] for t in range(2 * lats)], axis=0
        )
        high = left.astype(jnp.bfloat16).astype(jnp.float32)
        left = jnp.concatenate([high, left - high], axis=0).astype(jnp.bfloat16)
        both = jnp.dot(left, hot_turned[mask], preferred_element_type=jnp.float32)
        term = both[: 2 * lats * COLS] + both[2 * lats * COLS :]
        sent[...] = term if mask == 0 else sent[...] + term
    side = lats * COLS
    total = sent[...]
    blank = jnp.zeros((side, rows_sent.shape[2] - 2 * owned), jnp.float32)
    for owner in range(nc):
        block = total[:, owner * owned : (owner + 1) * owned]
        rows_sent[owner] = jnp.concatenate([block[:side], block[side:], blank], axis=1)
        for which in range(2):
            first = which * side + owner * COLS
            lats_sent[owner, which] = total[first : first + COLS]
    for mask in range(nc - 1, 0, -1):
        for copy in final_copies(mask):
            copy.start()
    waves()
    own = rows_sent[mine]
    waved = lats_sent[mine]
    for mask in range(1, nc):
        for copy in final_copies(mask):
            copy.wait_recv()
        own = own + rows_here[mask]
        waved = waved + lats_here[mask]
    own = own / math.sqrt(NL)
    waved = waved / math.sqrt(NL)
    field = jnp.zeros((COLS, NLON), jnp.float32)
    for which in range(2):
        rows = waved[which]
        high = rows.astype(jnp.bfloat16).astype(jnp.float32)
        left = jnp.concatenate([high, rows - high], axis=0).astype(jnp.bfloat16)
        for level in range(2):
            both = jnp.dot(left, wave_ref[which, level], preferred_element_type=jnp.float32)
            field = field + both[:COLS] + both[COLS:]
    field_out[...] = field / math.sqrt(NL)
    band_out[...] = own
    for rnd in range(ITERS + 1):
        for mask in far_first:
            scatter_copy(rnd, mask).wait_send()
            gather_copy(rnd, mask).wait_send()
        if rnd < ITERS:
            for mask in range(1, nc):
                image_copy(rnd, mask).wait_send()
    for mask in range(1, nc):
        for copy in final_copies(mask):
            copy.wait_send()


def arrange_kernel(band_ref, field_ref, band_out, field_out):
    owned = band_out.shape[3]
    lats = band_out.shape[2]
    field_out[:, 0, :] = field_ref[...]
    for column in range(COLS):
        line = band_ref[pl.ds(column, lats, stride=COLS), :]
        for which in range(2):
            band_out[which, column] = line[:, which * owned : (which + 1) * owned]


def arrange(band, field, owned):
    return pl.pallas_call(
        arrange_kernel,
        out_shape=(
            jax.ShapeDtypeStruct((2, COLS, band.shape[0] // COLS, owned), jnp.float32),
            jax.ShapeDtypeStruct((COLS, 1, NLON), jnp.float32),
        ),
        in_specs=[VMEM_SPEC] * 2,
        out_specs=(VMEM_SPEC,) * 2,
        name="arrange",
    )(band, field)


def solve(n, nc, observations, design, shift_table, shift_index, order_map, perm):
    rows, kdev = design.shape
    chunk = kdev // n
    rounds = ITERS + 1
    lanes = -(-NL // 128) * 128
    lats = LAT_DEV * nc
    side = 2 * lats * COLS
    blocks = pltpu.VMEM((rounds, n, COLS, chunk), jnp.bfloat16)
    tables = pltpu.VMEM((NL, lanes), jnp.float32)
    return pl.pallas_call(
        functools.partial(solver_kernel, n, nc),
        out_shape=(
            jax.ShapeDtypeStruct((side // 2, 128), jnp.float32),
            jax.ShapeDtypeStruct((COLS, NLON), jnp.float32),
        ),
        in_specs=[pl.BlockSpec(memory_space=pltpu.HBM)] * 6,
        out_specs=(VMEM_SPEC, VMEM_SPEC),
        scratch_shapes=[pltpu.VMEM((n, rows, chunk), jnp.bfloat16)]
        + [blocks] * 3
        + [
            pltpu.VMEM((ITERS, COLS, rows), jnp.bfloat16),
            pltpu.VMEM((ITERS, nc, COLS, rows), jnp.bfloat16),
            pltpu.VMEM((2 * COLS, rows), jnp.bfloat16),
            pltpu.VMEM((COLS, rows), jnp.float32),
            pltpu.VMEM(observations.shape, observations.dtype),
            pltpu.SMEM(shift_table.shape, jnp.float32),
            pltpu.SMEM(shift_index.shape, jnp.int32),
            pltpu.SMEM(order_map.shape, jnp.int32),
            pltpu.VMEM((kdev // 128, 128), jnp.int32),
            pltpu.VMEM((3 * n // 4, chunk, rows), jnp.bfloat16),
            pltpu.VMEM((4, kdev // 128, 128), jnp.float32),
            pltpu.VMEM((lanes, kdev), jnp.bfloat16),
            pltpu.VMEM((n, chunk, lanes), jnp.bfloat16),
            pltpu.VMEM((lanes // 128, NL * 8, 128), jnp.float32),
            pltpu.VMEM((lats * NL, lanes), jnp.bfloat16),
            tables,
            tables,
            tables,
            pltpu.VMEM((2 * lats, kdev), jnp.float32),
            pltpu.VMEM((2, 2, lanes, NLON), jnp.bfloat16),
            pltpu.VMEM((side, lanes), jnp.float32),
        ]
        + [pltpu.VMEM((nc, side // 2, 128), jnp.float32)] * 2
        + [pltpu.VMEM((nc, 2, COLS, lanes), jnp.float32)] * 2
        + [
            pltpu.SemaphoreType.DMA((5,)),
            pltpu.SemaphoreType.DMA((n,)),
        ]
        + [pltpu.SemaphoreType.DMA((rounds, n))] * 4
        + [pltpu.SemaphoreType.DMA((ITERS, nc))] * 2
        + [pltpu.SemaphoreType.DMA((nc,))] * 4,
        compiler_params=pltpu.CompilerParams(
            collective_id=0, has_side_effects=True, vmem_limit_bytes=56 << 20
        ),
        name="solve",
    )(observations, design, shift_table, shift_index, order_map, perm.reshape(-1, 128))


def sum_kernel(n, x_ref, o_ref, landed, send_sem, recv_sem):
    me = lax.axis_index("coef")
    greet("coef", n, me)
    copies = []
    for step in range(1, n):
        copy = push("coef", n, me, step, x_ref, landed.at[step], send_sem, recv_sem)
        copy.start()
        copies.append(copy)
    total = x_ref[...]
    for step in range(1, n):
        copies[step - 1].wait()
        total = total + landed[step]
    o_ref[...] = total.astype(o_ref.dtype)


def coef_sum(partial, n, cid):
    return pl.pallas_call(
        functools.partial(sum_kernel, n),
        out_shape=jax.ShapeDtypeStruct(partial.shape, jnp.bfloat16),
        in_specs=[VMEM_SPEC],
        out_specs=VMEM_SPEC,
        scratch_shapes=[pltpu.VMEM((n,) + partial.shape, jnp.float32)]
        + [pltpu.SemaphoreType.DMA((n,))] * 2,
        compiler_params=pltpu.CompilerParams(collective_id=cid, has_side_effects=True),
        name="coef_sum",
    )(partial)


def solve_plain(nc, observations, design, shift, keep, gain):
    def transposed_pass(left):
        return lax.psum(jnp.dot(left, design, preferred_element_type=jnp.float32), "obs")

    residual = transposed_pass(observations)
    direction = residual / keep[0]
    solution = direction
    for rnd in range(1, ITERS + 1):
        partial_image = lax.dot_general(
            direction.astype(jnp.bfloat16),
            design,
            (((1,), (1,)), ((), ())),
            preferred_element_type=jnp.float32,
        )
        total = transposed_pass(coef_sum(partial_image, nc, 2 + rnd))
        residual = residual - (total + shift * direction)
        direction = keep[rnd] * direction + gain[rnd] * residual
        solution = solution + direction
    return solution.astype(jnp.bfloat16)


def scatter_kernel(n, x_ref, o_ref, landed, send_sem, recv_sem):
    me = lax.axis_index("coef")
    greet("coef", n, me)
    copies = []
    for step in range(1, n):
        target = lax.rem(me + step, n)
        copy = push("coef", n, me, step, x_ref.at[target], landed.at[step], send_sem, recv_sem)
        copy.start()
        copies.append(copy)
    total = x_ref[me].astype(jnp.float32)
    for step in range(1, n):
        copies[step - 1].wait()
        total = total + landed[step].astype(jnp.float32)
    o_ref[...] = total


def coef_scatter(parts, n, cid):
    return pl.pallas_call(
        functools.partial(scatter_kernel, n),
        out_shape=jax.ShapeDtypeStruct(parts.shape[1:], jnp.float32),
        in_specs=[VMEM_SPEC],
        out_specs=VMEM_SPEC,
        scratch_shapes=[pltpu.VMEM(parts.shape, parts.dtype)]
        + [pltpu.SemaphoreType.DMA((n,))] * 2,
        compiler_params=pltpu.CompilerParams(collective_id=cid, has_side_effects=True),
        name="coef_scatter",
    )(parts)


def place_kernel(width, row_ref, col_ref, sol_ref, out_ref, spread):
    out_ref[...] = jnp.zeros_like(out_ref)
    wide = jnp.zeros((COLS, width), jnp.int32)

    def step(index, carry):
        at = pl.ds(pl.multiple_of(index * width, 128), width)
        values = sol_ref[:, at].astype(jnp.float32)
        rows = row_ref[:, at] + wide
        for pair in range(NL // 2):
            first = jnp.where(rows == 2 * pair, values, 0.0)
            second = jnp.where(rows == 2 * pair + 1, values, 0.0)
            both = jnp.concatenate([first, second], axis=0)
            spread[pair * 2 * COLS : (pair + 1) * 2 * COLS, :] = both.astype(jnp.bfloat16)
        degree = lax.broadcasted_iota(jnp.int32, (NL, width), 0)
        hot = jnp.where(degree == col_ref[:, at], 1.0, 0.0).astype(jnp.bfloat16)
        out_ref[...] += lax.dot_general(
            spread[...], hot, (((1,), (1,)), ((), ())), preferred_element_type=jnp.float32
        )
        return carry

    lax.fori_loop(0, sol_ref.shape[1] // width, step, 0)


def place(rows, cols, sol):
    kdev = sol.shape[1]
    width = next(w for w in (512, 384, 256, 128) if kdev % w == 0)
    return pl.pallas_call(
        functools.partial(place_kernel, width),
        out_shape=jax.ShapeDtypeStruct((NL * COLS, NL), jnp.float32),
        in_specs=[VMEM_SPEC] * 3,
        out_specs=VMEM_SPEC,
        scratch_shapes=[pltpu.VMEM((NL * COLS, width), jnp.bfloat16)],
        compiler_params=pltpu.CompilerParams(vmem_limit_bytes=32 << 20),
        name="place",
    )(rows, cols, sol)


def table_of(level, order, valid):
    product = (level - order) * (level + order)
    denom = jnp.where(valid, product, 1.0)
    first = jnp.sqrt(jnp.maximum((2.0 * level - 1.0) * (2.0 * level + 1.0), 0.0) / denom)
    second = jnp.sqrt(
        jnp.maximum((2.0 * level + 1.0) * (level + order - 1.0) * (level - order - 1.0), 0.0)
        / (denom * jnp.maximum(2.0 * level - 3.0, 1.0))
    )
    return jnp.where(valid, first, 0.0), jnp.where(valid, second, 0.0)


def legendre_kernel(
    angle_ref, local_ref, out_ref, a_c, b_c, a_s, b_s, grow, w_ref
):
    lats, lanes = angle_ref.shape[1:]
    w_ref[...] = local_ref[...].T
    order = angle_ref[0, 0:1, :]
    other = float(NL) - order
    count = lax.broadcasted_iota(jnp.int32, (NL, lanes), 0).astype(jnp.float32)
    wide = jnp.zeros((NL, lanes), jnp.float32)
    low = order + wide
    high = other + wide
    level = count + low
    a, b = table_of(level, low, jnp.logical_and(count > 0.0, level < float(NL)))
    a_c[...] = a
    b_c[...] = b
    a, b = table_of(count, high, count > high)
    a_s[...] = a
    b_s[...] = b
    safe = jnp.maximum(count, 1.0)
    grow[...] = jnp.where(
        count == 1.0, math.sqrt(3.0), jnp.sqrt((2.0 * safe + 1.0) / (2.0 * safe))
    )
    cosine = angle_ref[1]
    sine = angle_ref[2]
    zero = cosine * 0.0
    low = angle_ref[0]
    high = float(NL) - low

    def climb(degree, carry):
        diag, dc, ds = carry
        diag = diag * sine * grow[pl.ds(degree, 1), :]
        here = degree.astype(jnp.float32)
        return diag, jnp.where(low == here, diag, dc), jnp.where(high == here, diag, ds)

    start = zero + 1.0
    _, dc, ds = lax.fori_loop(
        1, NL, climb, (start, jnp.where(low == 0.0, start, zero), zero), unroll=4
    )
    acc_c = dc * w_ref[pl.ds(0, 1), :]

    def advance(column, carry):
        pc, ec, ps, es, acc_c, acc_s = carry
        at = pl.ds(column, 1)
        w = w_ref[at, :]
        vc = a_c[at, :] * cosine * pc - b_c[at, :] * ec
        begin = jnp.where(high == column.astype(jnp.float32), ds, 0.0)
        vs = a_s[at, :] * cosine * ps - b_s[at, :] * es + begin
        return vc, pc, vs, ps, acc_c + vc * w, acc_s + vs * w

    _, _, _, _, acc_c, acc_s = lax.fori_loop(
        1, NL, advance, (dc, zero, zero, zero, acc_c, zero), unroll=4
    )
    out_ref[0] = acc_c / math.sqrt(NL)
    out_ref[1] = acc_s / math.sqrt(NL)


def legendre(orders, colatitude, w):
    lanes = w.shape[0]
    lats = colatitude.shape[0]
    which = lax.broadcasted_iota(jnp.int32, (3, lats, lanes), 0)
    angles = jnp.where(
        which == 0,
        orders[None, None, :],
        jnp.where(which == 1, jnp.cos(colatitude)[:, None], jnp.sin(colatitude)[:, None]),
    )
    table = pltpu.VMEM((NL, lanes), jnp.float32)
    return pl.pallas_call(
        legendre_kernel,
        out_shape=jax.ShapeDtypeStruct((2, lats, lanes), jnp.float32),
        in_specs=[VMEM_SPEC] * 2,
        out_specs=VMEM_SPEC,
        scratch_shapes=[table] * 6,
        name="legendre",
    )(
        angles,
        w,
    )


def wave_tables(rows, longitudes):
    steps_k = jnp.arange(longitudes, dtype=jnp.int32)
    scale = 2.0 * math.pi / longitudes
    cos_angle = (rows[:, None] * steps_k[None, :] % longitudes).astype(jnp.float32) * scale
    sin_angle = ((NL - rows)[:, None] * steps_k[None, :] % longitudes).astype(jnp.float32) * scale
    return (jnp.cos(cos_angle), jnp.sin(sin_angle))


def body(design, observations, shift_table, shift_index, coef_perm, order_map):
    obs_count = lax.axis_size("obs")
    coef_count = lax.axis_size("coef")
    coef_rank = lax.axis_index("coef")
    obs_rank = lax.axis_index("obs")
    kdev = design.shape[1]
    chunk = kdev // obs_count
    paired_up = all(c & (c - 1) == 0 for c in (obs_count, coef_count))
    direct = (
        chunk % 128 == 0
        and kdev % 256 == 0
        and paired_up
        and LAT_DEV * coef_count <= 8
        and 2 * NL // coef_count <= 128
        and NL <= 256
    )
    if direct:
        band, field = solve(
            obs_count, coef_count, observations, design, shift_table, shift_index, order_map,
            coef_perm,
        )
        band, field = arrange(band, field, NL // coef_count)
        return (band.transpose(3, 0, 1, 2), field)
    table_index = jnp.arange(NSHIFT, dtype=jnp.int32)
    shifts = jnp.sum(
        jnp.where(shift_index[:, None] == table_index[None, :], shift_table[None, :], 0.0), axis=1
    )
    centre = shifts + CENTRE_OFFSET
    ratio_start = centre / HALF_WIDTH

    keep = [centre]
    gain = [centre]
    factor = 1.0 / ratio_start
    for iteration in range(ITERS):
        factor_next = 1.0 / (2.0 * ratio_start - factor)
        keep.append(factor_next * factor)
        gain.append(2.0 * factor_next / HALF_WIDTH)
        factor = factor_next
    keep = jnp.stack(keep)[:, :, None]
    gain = jnp.stack(gain)[:, :, None]
    block_count = coef_count * BPO
    block_rows = NL // block_count
    owned_rows = kdev // NL
    block_ids = jnp.arange(block_count, dtype=jnp.int32)
    position = jnp.sum(
        jnp.where(order_map[:, None] == block_ids[None, :], block_ids[:, None], 0), axis=0
    )
    paired_row = coef_perm // NL
    column = coef_perm % NL
    place_of = jnp.sum(
        jnp.where(
            (paired_row // block_rows)[None, :] == block_ids[:, None], position[:, None], 0
        ),
        axis=0,
    )
    owner_row = place_of * block_rows + paired_row % block_rows
    full = solve_plain(coef_count, observations, design, shifts[:, None], keep, gain)
    lanes = owned_rows * COLS
    placed = place(owner_row[None, :], column[None, :], full)
    outgoing = placed.astype(jnp.bfloat16).reshape(coef_count, lanes, NL)
    local = coef_scatter(outgoing, coef_count, 5)
    my_blocks = lax.dynamic_slice_in_dim(order_map, coef_rank * BPO, BPO)
    row_offsets = jnp.arange(block_rows, dtype=jnp.int32)
    owned_canon = (my_blocks[:, None] * block_rows + row_offsets[None, :]).reshape(owned_rows)
    lat_block = LAT_DEV * coef_count
    lat_total = lat_block * obs_count
    lat_ids = obs_rank * lat_block + jnp.arange(lat_block, dtype=jnp.int32)
    colatitude = math.pi * (lat_ids.astype(jnp.float32) + 0.5) / lat_total
    orders = jnp.repeat(owned_canon, COLS).astype(jnp.float32)
    parts = legendre(orders, colatitude, local).reshape(2, lat_block, owned_rows, COLS)
    band = parts.transpose(2, 0, 3, 1)
    own_cos, own_sin = wave_tables(owned_canon, NLON)
    first_sum = jnp.einsum("lqc,qk->lck", parts[0], own_cos, precision=lax.Precision.HIGHEST)
    second_sum = jnp.einsum("lqc,qk->lck", parts[1], own_sin, precision=lax.Precision.HIGHEST)
    shares = ((first_sum + second_sum) / math.sqrt(NL)).reshape(
        coef_count, LAT_DEV * COLS, NLON
    )
    field = coef_scatter(shares, coef_count, 6).reshape(LAT_DEV, COLS, NLON).transpose(1, 0, 2)
    return (band, field)


def solution(mesh):
    placed = (P("obs", "coef"), P(None, "obs"), P(), P(), P("coef"), P())
    return jax.shard_map(
        body,
        mesh=mesh,
        in_specs=placed,
        out_specs=(P("coef", None, None, "obs"), P(None, ("obs", "coef"), None)),
        check_vma=False,
    )
```

```python
import functools
import math

import jax
import jax.numpy as jnp
from jax import lax
from jax.experimental import pallas as pl
from jax.experimental.pallas import tpu as pltpu
from jax.sharding import PartitionSpec as P

NL = 192
COLS = 8
ITERS = 2
NSHIFT = 16
BPO = 2
NLON = 1024
LAT_DEV = 1

CENTRE_OFFSET = 1.25
HALF_WIDTH = 0.95
VMEM_SPEC = pl.BlockSpec(memory_space=pltpu.VMEM)
MESH = pl.DeviceIdType.MESH


def greet(axis, n, me):
    barrier = pltpu.get_barrier_semaphore()
    for step in range(1, n):
        pl.semaphore_signal(
            barrier, inc=1, device_id={axis: lax.rem(me + step, n)}, device_id_type=MESH
        )
    pl.semaphore_wait(barrier, n - 1)


def push(axis, n, me, step, src, dst, send_sem, recv_sem):
    return pltpu.make_async_remote_copy(
        src_ref=src,
        dst_ref=dst,
        send_sem=send_sem.at[step],
        recv_sem=recv_sem.at[step],
        device_id={axis: lax.rem(me + step, n)},
        device_id_type=MESH,
    )


def flip(index, mask):
    other = index
    bit = 1
    while bit <= mask:
        if mask & bit:
            other = other + bit - 2 * bit * (index // bit % 2)
        bit *= 2
    return other


def swap(axis, rank, mask, src, dst, send_sem, recv_sem):
    return pltpu.make_async_remote_copy(
        src_ref=src,
        dst_ref=dst,
        send_sem=send_sem.at[mask],
        recv_sem=recv_sem.at[mask],
        device_id={axis: flip(rank, mask)},
        device_id_type=MESH,
    )


def solver_kernel(
    n, nc, obs_hbm, design_ref, shift_hbm, index_hbm, map_hbm, perm_hbm,
    band_out, field_out,
    held, part, landed, gathered, image_sent, image_landed, left_ref, acc,
    obs_ref, shift_table, shift_index, map_ref, perm_ref, turned, places, hot, hot_turned, raw, table, a_tab, b_tab, grow, picked, wave_ref, sent, rows_sent, rows_here, lats_sent, lats_here,
    small_sem, load_sem, send_a, recv_a, send_b, recv_b, send_c, recv_c, send_d, recv_d,
    send_e, recv_e,
):
    me = lax.axis_index("obs")
    mine = lax.axis_index("coef")
    chunk = held.shape[2]
    lanes = hot.shape[0]
    lats = LAT_DEV * nc
    owned = NL // nc
    far_first = list(range(n - 1, 0, -1))

    def load(mask):
        return pltpu.make_async_copy(
            design_ref.at[:, pl.ds(pl.multiple_of(flip(me, mask) * chunk, 128), chunk)],
            held.at[mask],
            load_sem.at[mask],
        )

    barrier = pltpu.get_barrier_semaphore()
    for axis, count, rank in (("obs", n, me), ("coef", nc, mine)):
        for mask in range(1, count):
            pl.semaphore_signal(
                barrier, inc=1, device_id={axis: flip(rank, mask)}, device_id_type=MESH
            )

    small = [
        pltpu.make_async_copy(source, target, small_sem.at[spot])
        for spot, (source, target) in enumerate(
            (
                (map_hbm, map_ref),
                (perm_hbm, perm_ref),
                (obs_hbm, obs_ref),
                (shift_hbm, shift_table),
                (index_hbm, shift_index),
            )
        )
    ]
    for copy in small:
        copy.start()
    for mask in far_first + [0]:
        load(mask).start()

    def scatter_copy(rnd, mask):
        return swap(
            "obs", me, mask, part.at[rnd, mask], landed.at[rnd, mask], send_a.at[rnd], recv_a.at[rnd]
        )

    def gather_copy(rnd, mask):
        return swap(
            "obs", me, mask, gathered.at[rnd, 0], gathered.at[rnd, mask],
            send_b.at[rnd], recv_b.at[rnd],
        )

    def image_copy(rnd, mask):
        return swap(
            "coef", mine, mask, image_sent.at[rnd], image_landed.at[rnd, mask],
            send_c.at[rnd], recv_c.at[rnd],
        )

    def final_copies(mask):
        target = flip(mine, mask)
        return [
            swap("coef", mine, mask, rows_sent.at[target], rows_here.at[mask], send_d, recv_d),
            swap("coef", mine, mask, lats_sent.at[target], lats_here.at[mask], send_e, recv_e),
        ]

    def canon(shape, axis):
        lane = lax.broadcasted_iota(jnp.int32, shape, axis)
        blocks = nc * BPO
        size = NL // blocks
        total = jnp.zeros(shape, jnp.int32)
        for block in range(blocks):
            inside = jnp.logical_and(lane >= block * size, lane < (block + 1) * size)
            total = jnp.where(inside, lane + (map_ref[block] - block) * size, total)
        return total

    def legendre_table():
        order = canon((8, lanes), 1).astype(jnp.float32)
        other = float(NL) - order
        count = lax.broadcasted_iota(jnp.int32, (NL, lanes), 0).astype(jnp.float32)
        low = order[0:1, :] + jnp.zeros((NL, lanes), jnp.float32)
        high = float(NL) - low
        cosine_part = count < high
        level = jnp.where(cosine_part, count + low, count)
        degree_order = jnp.where(cosine_part, low, high)
        valid = jnp.logical_and(count != high, count > 0.0)
        a, b = table_of(level, degree_order, valid)
        a_tab[...] = a
        b_tab[...] = b
        safe = jnp.maximum(count, 1.0)
        grow[...] = jnp.where(
            count == 1.0, math.sqrt(3.0), jnp.sqrt((2.0 * safe + 1.0) / (2.0 * safe))
        )
        lat = lax.broadcasted_iota(jnp.int32, (8, lanes), 0) + me * lats
        colatitude = math.pi * (lat.astype(jnp.float32) + 0.5) / (lats * n)
        cosine = jnp.cos(colatitude)
        sine = jnp.sin(colatitude)

        def climb(degree, carry):
            diag, dc, ds = carry
            diag = diag * (sine * grow[pl.ds(degree, 1), :])
            here = degree.astype(jnp.float32)
            return diag, jnp.where(order == here, diag, dc), jnp.where(other == here, diag, ds)

        start = jnp.ones((8, lanes), jnp.float32)
        zero = jnp.zeros((8, lanes), jnp.float32)
        _, dc, ds = lax.fori_loop(
            1, NL, climb, (start, jnp.where(order == 0.0, start, zero), zero), unroll=8
        )
        def keep_row(column, value):
            for half in range(lanes // 128):
                raw[half, pl.ds(pl.multiple_of(column * 8, 8), 8), :] = value[
                    :, half * 128 : (half + 1) * 128
                ]

        keep_row(0, dc)

        def advance(column, carry):
            now, before = carry
            at = pl.ds(column, 1)
            begin = jnp.where(other == column.astype(jnp.float32), ds, 0.0)
            value = (a_tab[at, :] * cosine) * now - (b_tab[at, :] * before - begin)
            keep_row(column, value)
            return value, now

        lax.fori_loop(1, NL, advance, (dc, zero), unroll=8)
        for t in range(lats):
            for half in range(lanes // 128):
                table[t * NL : (t + 1) * NL, half * 128 : (half + 1) * 128] = raw[
                    half, pl.ds(t, NL, stride=8), :
                ].astype(jnp.bfloat16)

    tile = 256
    tiles = hot.shape[1] // tile

    def find_places():
        index = perm_ref[...].astype(jnp.float32)
        paired = jnp.floor((index + 0.5) * (1.0 / NL))
        column = index - paired * NL
        blocks = nc * BPO
        size = NL // blocks
        block = jnp.floor((paired + 0.5) * (1.0 / size))
        inside = paired - block * size
        row = jnp.zeros_like(index)
        for spot in range(blocks):
            here = block == map_ref[spot].astype(jnp.float32)
            row = jnp.where(here, inside + spot * size, row)
        places[0] = row
        group = jnp.floor((column + 0.5) * 0.125)
        places[1] = group
        places[2] = column - group * 8.0
        places[3] = jnp.where(paired + column < NL, 1.0, 0.0)

    def build_hot():
        def one(index, carry):
            at = pl.ds(pl.multiple_of(index * 128, 128), 128)
            row = lax.broadcasted_iota(jnp.int32, (lanes, 128), 0).astype(jnp.bfloat16)
            same = row == places[0, pl.ds(index, 1), :].astype(jnp.bfloat16)
            hot[:, at] = jnp.where(same, jnp.bfloat16(1.0), jnp.bfloat16(0.0))
            return carry

        lax.fori_loop(0, tiles * (tile // 128), one, 0, unroll=4)

    def turn_hot():
        for mask in range(n):
            at = pl.ds(pl.multiple_of(flip(me, mask) * chunk, 128), chunk)
            hot_turned[mask] = hot[:, at].T

    def pick(first, last):
        def one(index, carry):
            wide = pl.ds(pl.multiple_of(index * tile, 128), tile)
            sub = lax.broadcasted_iota(jnp.int32, (8, 128), 0).astype(jnp.float32)
            product = jnp.dot(table[...], hot[:, wide], preferred_element_type=jnp.float32)
            for half in range(tile // 128):
                spot = pl.ds(index * (tile // 128) + half, 1)
                group = places[1, spot, :] + jnp.zeros_like(sub)
                inner = places[2, spot, :] == sub
                early = places[3, spot, :]
                kept = [jnp.zeros_like(sub)] * lats
                for q in range(NL // 8):
                    here = group == float(q)
                    for t in range(lats):
                        first_row = t * NL + q * 8
                        piece = product[first_row : first_row + 8, half * 128 : half * 128 + 128]
                        kept[t] = jnp.where(here, piece, kept[t])
                at = pl.ds(pl.multiple_of(index * tile + half * 128, 128), 128)
                for t in range(lats):
                    value = jnp.sum(jnp.where(inner, kept[t], 0.0), axis=0, keepdims=True)
                    low = value * early
                    picked[t : t + 1, at] = low
                    picked[lats + t : lats + t + 1, at] = value - low
            return carry

        lax.fori_loop(first, last, one, 0, unroll=last - first)

    def waves():
        order = canon((lanes, 128), 0)
        step = lax.broadcasted_iota(jnp.int32, (lanes, 128), 1)
        scale = 2.0 * math.pi / NLON
        for which in range(2):
            speed = order if which == 0 else NL - order
            fine = lax.rem(speed * step, NLON).astype(jnp.float32) * scale
            coarse = lax.rem(speed * step * 128, NLON).astype(jnp.float32) * scale
            fine_cos, fine_sin = jnp.cos(fine), jnp.sin(fine)
            coarse_cos, coarse_sin = jnp.cos(coarse), jnp.sin(coarse)
            for block in range(NLON // 128):
                cos_b = coarse_cos[:, block : block + 1]
                sin_b = coarse_sin[:, block : block + 1]
                if which == 0:
                    value = cos_b * fine_cos - sin_b * fine_sin
                else:
                    value = sin_b * fine_cos + cos_b * fine_sin
                high = value.astype(jnp.bfloat16)
                at = slice(block * 128, block * 128 + 128)
                wave_ref[which, 0, :, at] = high
                wave_ref[which, 1, :, at] = (value - high.astype(jnp.float32)).astype(jnp.bfloat16)

    straight = n - turned.shape[0]

    def turn(masks):
        for mask in masks:
            turned[mask - straight] = held[mask].T

    def transposed_pass(rnd, filler):
        def product(mask):
            both = jnp.dot(left_ref[...], held[mask], preferred_element_type=jnp.float32)
            return both[:COLS] + both[COLS:]

        for mask in far_first:
            if rnd == 0:
                load(mask).wait()
            part[rnd, mask] = product(mask).astype(jnp.bfloat16)
            scatter_copy(rnd, mask).start()
        if rnd == 0:
            load(0).wait()
        total = product(0)
        filler()
        for mask in far_first:
            scatter_copy(rnd, mask).wait_recv()
            total = total + landed[rnd, mask].astype(jnp.float32)
        gathered[rnd, 0] = total.astype(jnp.bfloat16)
        for mask in far_first:
            gather_copy(rnd, mask).start()

    def image_of(rnd, first, second):
        for mask in range(n):
            if mask:
                gather_copy(rnd, mask).wait_recv()
            block = gathered[rnd, mask]
            if mask >= straight:
                term = jnp.dot(block, turned[mask - straight], preferred_element_type=jnp.float32)
            else:
                term = lax.dot_general(
                    block, held[mask], (((1,), (1,)), ((), ())), preferred_element_type=jnp.float32
                )
            acc[...] = term if mask == 0 else acc[...] + term
            if mask == 0:
                first()
        image = acc[...]
        image_sent[rnd] = image.astype(jnp.bfloat16)
        for mask in range(nc - 1, 0, -1):
            image_copy(rnd, mask).start()
        second()
        for mask in range(1, nc):
            image_copy(rnd, mask).wait_recv()
            image = image + image_landed[rnd, mask].astype(jnp.float32)
        return image

    def split(value):
        high = value.astype(jnp.bfloat16).astype(jnp.float32)
        left_ref[...] = jnp.concatenate([high, value - high], axis=0).astype(jnp.bfloat16)

    share = [functools.partial(pick, i * tiles // 6, (i + 1) * tiles // 6) for i in range(6)]
    turn_first, turn_second = far_first[: n // 2], far_first[n // 2 : n - straight]
    scatter_fill = [
        functools.partial(turn, turn_first), lambda: (share[1](), share[2]()), turn_hot
    ]
    first_fill = [
        lambda: (turn(turn_second), legendre_table()), lambda: (share[3](), share[4]())
    ]
    second_fill = [lambda: (build_hot(), share[0]()), share[5]]
    for copy in small:
        copy.wait()
    find_places()
    pl.semaphore_wait(barrier, n + nc - 2)
    line = lax.broadcasted_iota(jnp.int32, (COLS, 1), 0)
    shift = jnp.zeros((COLS, 1), jnp.float32)
    for right_side in range(COLS):
        shift = jnp.where(line == right_side, shift_table[shift_index[right_side]], shift)
    centre = shift + CENTRE_OFFSET
    ratio_start = centre / HALF_WIDTH
    factor = 1.0 / ratio_start
    residual = obs_ref[...].astype(jnp.float32)
    split(residual)
    transposed_pass(0, scatter_fill[0])
    direction = residual / centre
    answer = direction
    for rnd in range(1, ITERS + 1):
        image = image_of(rnd - 1, first_fill[rnd - 1], second_fill[rnd - 1])
        if rnd == 1:
            image = image / centre
        residual = residual - (image + shift * direction)
        factor_next = 1.0 / (2.0 * ratio_start - factor)
        direction = (factor_next * factor) * direction + (
            2.0 * factor_next / HALF_WIDTH
        ) * residual
        factor = factor_next
        answer = answer + direction
        split(answer if rnd == ITERS else direction)
        transposed_pass(rnd, scatter_fill[rnd])
    for mask in range(n):
        if mask:
            gather_copy(ITERS, mask).wait_recv()
        at = pl.ds(pl.multiple_of(flip(me, mask) * chunk, 128), chunk)
        values = gathered[ITERS, mask].astype(jnp.float32)
        left = jnp.concatenate(
            [values * picked[t : t + 1, at] for t in range(2 * lats)], axis=0
        )
        high = left.astype(jnp.bfloat16).astype(jnp.float32)
        left = jnp.concatenate([high, left - high], axis=0).astype(jnp.bfloat16)
        both = jnp.dot(left, hot_turned[mask], preferred_element_type=jnp.float32)
        term = both[: 2 * lats * COLS] + both[2 * lats * COLS :]
        sent[...] = term if mask == 0 else sent[...] + term
    side = lats * COLS
    total = sent[...]
    blank = jnp.zeros((side, rows_sent.shape[2] - 2 * owned), jnp.float32)
    for owner in range(nc):
        block = total[:, owner * owned : (owner + 1) * owned]
        rows_sent[owner] = jnp.concatenate([block[:side], block[side:], blank], axis=1)
        for which in range(2):
            first = which * side + owner * COLS
            lats_sent[owner, which] = total[first : first + COLS]
    for mask in range(nc - 1, 0, -1):
        for copy in final_copies(mask):
            copy.start()
    waves()
    own = rows_sent[mine]
    waved = lats_sent[mine]
    for mask in range(1, nc):
        for copy in final_copies(mask):
            copy.wait_recv()
        own = own + rows_here[mask]
        waved = waved + lats_here[mask]
    own = own / math.sqrt(NL)
    waved = waved / math.sqrt(NL)
    field = jnp.zeros((COLS, NLON), jnp.float32)
    for which in range(2):
        rows = waved[which]
        high = rows.astype(jnp.bfloat16).astype(jnp.float32)
        left = jnp.concatenate([high, rows - high], axis=0).astype(jnp.bfloat16)
        for level in range(2):
            both = jnp.dot(left, wave_ref[which, level], preferred_element_type=jnp.float32)
            field = field + both[:COLS] + both[COLS:]
    field_out[...] = field / math.sqrt(NL)
    band_out[...] = own
    for rnd in range(ITERS + 1):
        for mask in far_first:
            scatter_copy(rnd, mask).wait_send()
            gather_copy(rnd, mask).wait_send()
        if rnd < ITERS:
            for mask in range(1, nc):
                image_copy(rnd, mask).wait_send()
    for mask in range(1, nc):
        for copy in final_copies(mask):
            copy.wait_send()


def arrange_kernel(band_ref, field_ref, band_out, field_out):
    owned = band_out.shape[3]
    lats = band_out.shape[2]
    field_out[:, 0, :] = field_ref[...]
    for column in range(COLS):
        line = band_ref[pl.ds(column, lats, stride=COLS), :]
        for which in range(2):
            band_out[which, column] = line[:, which * owned : (which + 1) * owned]


def arrange(band, field, owned):
    return pl.pallas_call(
        arrange_kernel,
        out_shape=(
            jax.ShapeDtypeStruct((2, COLS, band.shape[0] // COLS, owned), jnp.float32),
            jax.ShapeDtypeStruct((COLS, 1, NLON), jnp.float32),
        ),
        in_specs=[VMEM_SPEC] * 2,
        out_specs=(VMEM_SPEC,) * 2,
        name="arrange",
    )(band, field)


def solve(n, nc, observations, design, shift_table, shift_index, order_map, perm):
    rows, kdev = design.shape
    chunk = kdev // n
    rounds = ITERS + 1
    lanes = -(-NL // 128) * 128
    lats = LAT_DEV * nc
    side = 2 * lats * COLS
    blocks = pltpu.VMEM((rounds, n, COLS, chunk), jnp.bfloat16)
    tables = pltpu.VMEM((NL, lanes), jnp.float32)
    return pl.pallas_call(
        functools.partial(solver_kernel, n, nc),
        out_shape=(
            jax.ShapeDtypeStruct((side // 2, 128), jnp.float32),
            jax.ShapeDtypeStruct((COLS, NLON), jnp.float32),
        ),
        in_specs=[pl.BlockSpec(memory_space=pltpu.HBM)] * 6,
        out_specs=(VMEM_SPEC, VMEM_SPEC),
        scratch_shapes=[pltpu.VMEM((n, rows, chunk), jnp.bfloat16)]
        + [blocks] * 3
        + [
            pltpu.VMEM((ITERS, COLS, rows), jnp.bfloat16),
            pltpu.VMEM((ITERS, nc, COLS, rows), jnp.bfloat16),
            pltpu.VMEM((2 * COLS, rows), jnp.bfloat16),
            pltpu.VMEM((COLS, rows), jnp.float32),
            pltpu.VMEM(observations.shape, observations.dtype),
            pltpu.SMEM(shift_table.shape, jnp.float32),
            pltpu.SMEM(shift_index.shape, jnp.int32),
            pltpu.SMEM(order_map.shape, jnp.int32),
            pltpu.VMEM((kdev // 128, 128), jnp.int32),
            pltpu.VMEM((3 * n // 4, chunk, rows), jnp.bfloat16),
            pltpu.VMEM((4, kdev // 128, 128), jnp.float32),
            pltpu.VMEM((lanes, kdev), jnp.bfloat16),
            pltpu.VMEM((n, chunk, lanes), jnp.bfloat16),
            pltpu.VMEM((lanes // 128, NL * 8, 128), jnp.float32),
            pltpu.VMEM((lats * NL, lanes), jnp.bfloat16),
            tables,
            tables,
            tables,
            pltpu.VMEM((2 * lats, kdev), jnp.float32),
            pltpu.VMEM((2, 2, lanes, NLON), jnp.bfloat16),
            pltpu.VMEM((side, lanes), jnp.float32),
        ]
        + [pltpu.VMEM((nc, side // 2, 128), jnp.float32)] * 2
        + [pltpu.VMEM((nc, 2, COLS, lanes), jnp.float32)] * 2
        + [
            pltpu.SemaphoreType.DMA((5,)),
            pltpu.SemaphoreType.DMA((n,)),
        ]
        + [pltpu.SemaphoreType.DMA((rounds, n))] * 4
        + [pltpu.SemaphoreType.DMA((ITERS, nc))] * 2
        + [pltpu.SemaphoreType.DMA((nc,))] * 4,
        compiler_params=pltpu.CompilerParams(
            collective_id=0, has_side_effects=True, vmem_limit_bytes=56 << 20
        ),
        name="solve",
    )(observations, design, shift_table, shift_index, order_map, perm.reshape(-1, 128))


def sum_kernel(n, x_ref, o_ref, landed, send_sem, recv_sem):
    me = lax.axis_index("coef")
    greet("coef", n, me)
    copies = []
    for step in range(1, n):
        copy = push("coef", n, me, step, x_ref, landed.at[step], send_sem, recv_sem)
        copy.start()
        copies.append(copy)
    total = x_ref[...]
    for step in range(1, n):
        copies[step - 1].wait()
        total = total + landed[step]
    o_ref[...] = total.astype(o_ref.dtype)


def coef_sum(partial, n, cid):
    return pl.pallas_call(
        functools.partial(sum_kernel, n),
        out_shape=jax.ShapeDtypeStruct(partial.shape, jnp.bfloat16),
        in_specs=[VMEM_SPEC],
        out_specs=VMEM_SPEC,
        scratch_shapes=[pltpu.VMEM((n,) + partial.shape, jnp.float32)]
        + [pltpu.SemaphoreType.DMA((n,))] * 2,
        compiler_params=pltpu.CompilerParams(collective_id=cid, has_side_effects=True),
        name="coef_sum",
    )(partial)


def solve_plain(nc, observations, design, shift, keep, gain):
    def transposed_pass(left):
        return lax.psum(jnp.dot(left, design, preferred_element_type=jnp.float32), "obs")

    residual = transposed_pass(observations)
    direction = residual / keep[0]
    solution = direction
    for rnd in range(1, ITERS + 1):
        partial_image = lax.dot_general(
            direction.astype(jnp.bfloat16),
            design,
            (((1,), (1,)), ((), ())),
            preferred_element_type=jnp.float32,
        )
        total = transposed_pass(coef_sum(partial_image, nc, 2 + rnd))
        residual = residual - (total + shift * direction)
        direction = keep[rnd] * direction + gain[rnd] * residual
        solution = solution + direction
    return solution.astype(jnp.bfloat16)


def scatter_kernel(n, x_ref, o_ref, landed, send_sem, recv_sem):
    me = lax.axis_index("coef")
    greet("coef", n, me)
    copies = []
    for step in range(1, n):
        target = lax.rem(me + step, n)
        copy = push("coef", n, me, step, x_ref.at[target], landed.at[step], send_sem, recv_sem)
        copy.start()
        copies.append(copy)
    total = x_ref[me].astype(jnp.float32)
    for step in range(1, n):
        copies[step - 1].wait()
        total = total + landed[step].astype(jnp.float32)
    o_ref[...] = total


def coef_scatter(parts, n, cid):
    return pl.pallas_call(
        functools.partial(scatter_kernel, n),
        out_shape=jax.ShapeDtypeStruct(parts.shape[1:], jnp.float32),
        in_specs=[VMEM_SPEC],
        out_specs=VMEM_SPEC,
        scratch_shapes=[pltpu.VMEM(parts.shape, parts.dtype)]
        + [pltpu.SemaphoreType.DMA((n,))] * 2,
        compiler_params=pltpu.CompilerParams(collective_id=cid, has_side_effects=True),
        name="coef_scatter",
    )(parts)


def place_kernel(width, row_ref, col_ref, sol_ref, out_ref, spread):
    out_ref[...] = jnp.zeros_like(out_ref)
    wide = jnp.zeros((COLS, width), jnp.int32)

    def step(index, carry):
        at = pl.ds(pl.multiple_of(index * width, 128), width)
        values = sol_ref[:, at].astype(jnp.float32)
        rows = row_ref[:, at] + wide
        for pair in range(NL // 2):
            first = jnp.where(rows == 2 * pair, values, 0.0)
            second = jnp.where(rows == 2 * pair + 1, values, 0.0)
            both = jnp.concatenate([first, second], axis=0)
            spread[pair * 2 * COLS : (pair + 1) * 2 * COLS, :] = both.astype(jnp.bfloat16)
        degree = lax.broadcasted_iota(jnp.int32, (NL, width), 0)
        hot = jnp.where(degree == col_ref[:, at], 1.0, 0.0).astype(jnp.bfloat16)
        out_ref[...] += lax.dot_general(
            spread[...], hot, (((1,), (1,)), ((), ())), preferred_element_type=jnp.float32
        )
        return carry

    lax.fori_loop(0, sol_ref.shape[1] // width, step, 0)


def place(rows, cols, sol):
    kdev = sol.shape[1]
    width = next(w for w in (512, 384, 256, 128) if kdev % w == 0)
    return pl.pallas_call(
        functools.partial(place_kernel, width),
        out_shape=jax.ShapeDtypeStruct((NL * COLS, NL), jnp.float32),
        in_specs=[VMEM_SPEC] * 3,
        out_specs=VMEM_SPEC,
        scratch_shapes=[pltpu.VMEM((NL * COLS, width), jnp.bfloat16)],
        compiler_params=pltpu.CompilerParams(vmem_limit_bytes=32 << 20),
        name="place",
    )(rows, cols, sol)


def table_of(level, order, valid):
    product = (level - order) * (level + order)
    denom = jnp.where(valid, product, 1.0)
    first = jnp.sqrt(jnp.maximum((2.0 * level - 1.0) * (2.0 * level + 1.0), 0.0) / denom)
    second = jnp.sqrt(
        jnp.maximum((2.0 * level + 1.0) * (level + order - 1.0) * (level - order - 1.0), 0.0)
        / (denom * jnp.maximum(2.0 * level - 3.0, 1.0))
    )
    return jnp.where(valid, first, 0.0), jnp.where(valid, second, 0.0)


def legendre_kernel(
    angle_ref, local_ref, out_ref, a_c, b_c, a_s, b_s, grow, w_ref
):
    lats, lanes = angle_ref.shape[1:]
    w_ref[...] = local_ref[...].T
    order = angle_ref[0, 0:1, :]
    other = float(NL) - order
    count = lax.broadcasted_iota(jnp.int32, (NL, lanes), 0).astype(jnp.float32)
    wide = jnp.zeros((NL, lanes), jnp.float32)
    low = order + wide
    high = other + wide
    level = count + low
    a, b = table_of(level, low, jnp.logical_and(count > 0.0, level < float(NL)))
    a_c[...] = a
    b_c[...] = b
    a, b = table_of(count, high, count > high)
    a_s[...] = a
    b_s[...] = b
    safe = jnp.maximum(count, 1.0)
    grow[...] = jnp.where(
        count == 1.0, math.sqrt(3.0), jnp.sqrt((2.0 * safe + 1.0) / (2.0 * safe))
    )
    cosine = angle_ref[1]
    sine = angle_ref[2]
    zero = cosine * 0.0
    low = angle_ref[0]
    high = float(NL) - low

    def climb(degree, carry):
        diag, dc, ds = carry
        diag = diag * sine * grow[pl.ds(degree, 1), :]
        here = degree.astype(jnp.float32)
        return diag, jnp.where(low == here, diag, dc), jnp.where(high == here, diag, ds)

    start = zero + 1.0
    _, dc, ds = lax.fori_loop(
        1, NL, climb, (start, jnp.where(low == 0.0, start, zero), zero), unroll=4
    )
    acc_c = dc * w_ref[pl.ds(0, 1), :]

    def advance(column, carry):
        pc, ec, ps, es, acc_c, acc_s = carry
        at = pl.ds(column, 1)
        w = w_ref[at, :]
        vc = a_c[at, :] * cosine * pc - b_c[at, :] * ec
        begin = jnp.where(high == column.astype(jnp.float32), ds, 0.0)
        vs = a_s[at, :] * cosine * ps - b_s[at, :] * es + begin
        return vc, pc, vs, ps, acc_c + vc * w, acc_s + vs * w

    _, _, _, _, acc_c, acc_s = lax.fori_loop(
        1, NL, advance, (dc, zero, zero, zero, acc_c, zero), unroll=4
    )
    out_ref[0] = acc_c / math.sqrt(NL)
    out_ref[1] = acc_s / math.sqrt(NL)


def legendre(orders, colatitude, w):
    lanes = w.shape[0]
    lats = colatitude.shape[0]
    which = lax.broadcasted_iota(jnp.int32, (3, lats, lanes), 0)
    angles = jnp.where(
        which == 0,
        orders[None, None, :],
        jnp.where(which == 1, jnp.cos(colatitude)[:, None], jnp.sin(colatitude)[:, None]),
    )
    table = pltpu.VMEM((NL, lanes), jnp.float32)
    return pl.pallas_call(
        legendre_kernel,
        out_shape=jax.ShapeDtypeStruct((2, lats, lanes), jnp.float32),
        in_specs=[VMEM_SPEC] * 2,
        out_specs=VMEM_SPEC,
        scratch_shapes=[table] * 6,
        name="legendre",
    )(
        angles,
        w,
    )


def wave_tables(rows, longitudes):
    steps_k = jnp.arange(longitudes, dtype=jnp.int32)
    scale = 2.0 * math.pi / longitudes
    cos_angle = (rows[:, None] * steps_k[None, :] % longitudes).astype(jnp.float32) * scale
    sin_angle = ((NL - rows)[:, None] * steps_k[None, :] % longitudes).astype(jnp.float32) * scale
    return (jnp.cos(cos_angle), jnp.sin(sin_angle))


def body(design, observations, shift_table, shift_index, coef_perm, order_map):
    obs_count = lax.axis_size("obs")
    coef_count = lax.axis_size("coef")
    coef_rank = lax.axis_index("coef")
    obs_rank = lax.axis_index("obs")
    kdev = design.shape[1]
    chunk = kdev // obs_count
    paired_up = all(c & (c - 1) == 0 for c in (obs_count, coef_count))
    direct = (
        chunk % 128 == 0
        and kdev % 256 == 0
        and paired_up
        and LAT_DEV * coef_count <= 8
        and 2 * NL // coef_count <= 128
        and NL <= 256
    )
    if direct:
        band, field = solve(
            obs_count, coef_count, observations, design, shift_table, shift_index, order_map,
            coef_perm,
        )
        band, field = arrange(band, field, NL // coef_count)
        return (band.transpose(3, 0, 1, 2), field)
    table_index = jnp.arange(NSHIFT, dtype=jnp.int32)
    shifts = jnp.sum(
        jnp.where(shift_index[:, None] == table_index[None, :], shift_table[None, :], 0.0), axis=1
    )
    centre = shifts + CENTRE_OFFSET
    ratio_start = centre / HALF_WIDTH

    keep = [centre]
    gain = [centre]
    factor = 1.0 / ratio_start
    for iteration in range(ITERS):
        factor_next = 1.0 / (2.0 * ratio_start - factor)
        keep.append(factor_next * factor)
        gain.append(2.0 * factor_next / HALF_WIDTH)
        factor = factor_next
    keep = jnp.stack(keep)[:, :, None]
    gain = jnp.stack(gain)[:, :, None]
    block_count = coef_count * BPO
    block_rows = NL // block_count
    owned_rows = kdev // NL
    block_ids = jnp.arange(block_count, dtype=jnp.int32)
    position = jnp.sum(
        jnp.where(order_map[:, None] == block_ids[None, :], block_ids[:, None], 0), axis=0
    )
    paired_row = coef_perm // NL
    column = coef_perm % NL
    place_of = jnp.sum(
        jnp.where(
            (paired_row // block_rows)[None, :] == block_ids[:, None], position[:, None], 0
        ),
        axis=0,
    )
    owner_row = place_of * block_rows + paired_row % block_rows
    full = solve_plain(coef_count, observations, design, shifts[:, None], keep, gain)
    lanes = owned_rows * COLS
    placed = place(owner_row[None, :], column[None, :], full)
    outgoing = placed.astype(jnp.bfloat16).reshape(coef_count, lanes, NL)
    local = coef_scatter(outgoing, coef_count, 5)
    my_blocks = lax.dynamic_slice_in_dim(order_map, coef_rank * BPO, BPO)
    row_offsets = jnp.arange(block_rows, dtype=jnp.int32)
    owned_canon = (my_blocks[:, None] * block_rows + row_offsets[None, :]).reshape(owned_rows)
    lat_block = LAT_DEV * coef_count
    lat_total = lat_block * obs_count
    lat_ids = obs_rank * lat_block + jnp.arange(lat_block, dtype=jnp.int32)
    colatitude = math.pi * (lat_ids.astype(jnp.float32) + 0.5) / lat_total
    orders = jnp.repeat(owned_canon, COLS).astype(jnp.float32)
    parts = legendre(orders, colatitude, local).reshape(2, lat_block, owned_rows, COLS)
    band = parts.transpose(2, 0, 3, 1)
    own_cos, own_sin = wave_tables(owned_canon, NLON)
    first_sum = jnp.einsum("lqc,qk->lck", parts[0], own_cos, precision=lax.Precision.HIGHEST)
    second_sum = jnp.einsum("lqc,qk->lck", parts[1], own_sin, precision=lax.Precision.HIGHEST)
    shares = ((first_sum + second_sum) / math.sqrt(NL)).reshape(
        coef_count, LAT_DEV * COLS, NLON
    )
    field = coef_scatter(shares, coef_count, 6).reshape(LAT_DEV, COLS, NLON).transpose(1, 0, 2)
    return (band, field)


def solution(mesh):
    placed = (P("obs", "coef"), P(None, "obs"), P(), P(), P("coef"), P())
    return jax.shard_map(
        body,
        mesh=mesh,
        in_specs=placed,
        out_specs=(P("coef", None, None, "obs"), P(None, ("obs", "coef"), None)),
        check_vma=False,
    )
```
